32 devices in a mesh: tok: 4 (over z), hid: 8 (over y, x, core).
Axes of the slice: x: 2, y: 2, z: 4, core: 2. Of those that a mesh axis runs over, the one named last changes fastest.
Arguments:
- tokens: bfloat16 [2048, 1024], P('tok', 'hid'), may hold values from -6 to 6
- cotangent: bfloat16 [2048, 1024], P('tok', 'hid'), may hold values from -6 to 6
- frozen_in: bfloat16 [1024, 16384], P('tok', 'hid'), may hold values from -0.1875 to 0.1875
- frozen_out: bfloat16 [16384, 1024], P('hid', 'tok'), may hold values from -0.046875 to 0.046875
- input_adapter_first: bfloat16 [1024, 128], P('hid'), may hold values from -0.1875 to 0.1875
- input_adapter_second: bfloat16 [128, 16384], P(None, 'hid'), may hold values from -0.5 to 0.5
- adapter_out_a: bfloat16 [16384, 128], P('hid'), may hold values from -0.046875 to 0.046875
- adapter_out_b: bfloat16 [128, 1024], replicated, may hold values from -0.5 to 0.5
Outputs:
- input_gradient: float32 [2048, 1024], P('tok', 'hid')
- grad_in_a: float32 [1024, 128], P('hid')
- grad_in_b: float32 [128, 16384], P(None, 'hid')
- grad_out_a: float32 [16384, 128], P('hid')
- grad_out_b: float32 [128, 1024], P(None, 'hid')
The draws below stay inside these ranges and needn't reach their ends.
All inputs are finite; a program needn't handle non-finite values.
Results may differ from the reference program's by a relative error of at most 0.0029.
Values may be sent and summed in bfloat16 or wider, within the bound.
A program may use at most 64 MiB of HBM per device.

```python
import math
import jax
import jax.numpy as jnp
from jax import lax

D = 1024
FF = 16384
RANK = 128
TOKEN_COUNT = 2048
N_HID = 8


def levels(stream_key, extent, cuts, least, high):
    def one(axis_at, blocks):
        draws = jax.random.uniform(jax.random.fold_in(jax.random.fold_in(stream_key, 6), axis_at), (blocks,), jnp.float32, least / len(cuts), high / len(cuts))
        return jnp.repeat(jnp.exp(draws), extent[axis_at] // blocks).reshape((-1,) + (1,) * (len(extent) - axis_at - 1))

    factor_of = one(*cuts[0])
    for cut in cuts[1:]:
        factor_of = factor_of * one(*cut)
    return factor_of


def bell_draw(rng, shape, width, limit, cuts=(), kind=jnp.bfloat16):
    drawn = jax.random.normal(rng, shape, jnp.float32) * width
    if len(cuts) > 0:
        drawn = levels(rng, shape, cuts, -0.22, 0.18) * drawn
    return jnp.clip(drawn, min=-limit, max=limit).astype(kind)


def setup_inputs(seed: int = 0) -> dict:
    streams_of = jax.random.split(jax.random.key(seed), 9)
    tokens = bell_draw(streams_of[0], (TOKEN_COUNT, D), 1.0, 6.0, ((0, 4), (1, 8)))
    cotangent = bell_draw(streams_of[1], (TOKEN_COUNT, D), 1.0, 6.0, ((0, 4), (1, 8)))
    frozen_in = bell_draw(streams_of[2], (D, FF), D ** -0.5, 0.1875, ((0, 4), (1, 8)))
    frozen_out = bell_draw(streams_of[3], (FF, D), FF ** -0.5, 0.046875, ((0, 8), (1, 4)))
    input_adapter_first = bell_draw(streams_of[4], (D, RANK), D ** -0.5, 0.1875, ((0, 8),))
    input_adapter_second = bell_draw(streams_of[5], (RANK, FF), RANK ** -0.5, 0.5, ((1, 8),))
    adapter_out_a = bell_draw(streams_of[6], (FF, RANK), FF ** -0.5, 0.046875, ((0, 8),))
    adapter_out_b = bell_draw(streams_of[7], (RANK, D), RANK ** -0.5, 0.5)
    return dict(tokens=tokens, cotangent=cotangent, frozen_in=frozen_in, frozen_out=frozen_out, input_adapter_first=input_adapter_first, input_adapter_second=input_adapter_second, adapter_out_a=adapter_out_a, adapter_out_b=adapter_out_b)


ADAPTER_SCALE = 0.5
GELU_K = 0.7978845608
GELU_C = 0.044715

def gelu_pair(pre_activation):
    tangent = jnp.tanh(GELU_K * (pre_activation + GELU_C * pre_activation * pre_activation * pre_activation))
    value_out = 0.5 * pre_activation * (1.0 + tangent)
    slopes = 0.5 * (1.0 + tangent) + 0.5 * pre_activation * (1.0 - tangent * tangent) * GELU_K * (1.0 + 3.0 * GELU_C * pre_activation * pre_activation)
    return (value_out, slopes)

def reference(tokens, cotangent, frozen_in, frozen_out, input_adapter_first, input_adapter_second, adapter_out_a, adapter_out_b):
    highest_precision = lax.Precision.HIGHEST
    gradient_scale = ADAPTER_SCALE / math.sqrt(TOKEN_COUNT)
    lowrank_input = jnp.dot(tokens, input_adapter_first, preferred_element_type=jnp.float32)
    backward_lowrank = jnp.dot(cotangent, adapter_out_b.T, preferred_element_type=jnp.float32)
    block_width = FF // N_HID

    def one_block(running, block_index):
        rank_sum, back_sum, dense_total_sum = running
        begin_at = (block_index * block_width).astype(jnp.int32)
        input_weight = lax.dynamic_slice_in_dim(frozen_in, begin_at, block_width, 1)
        input_second_factor = lax.dynamic_slice_in_dim(input_adapter_second, begin_at, block_width, 1)
        output_adapter_first = lax.dynamic_slice_in_dim(adapter_out_a, begin_at, block_width, 0)
        output_weight = lax.dynamic_slice_in_dim(frozen_out, begin_at, block_width, 0)
        pre_activation = jnp.dot(tokens, input_weight, preferred_element_type=jnp.float32) + ADAPTER_SCALE * jnp.dot(lowrank_input, input_second_factor.astype(jnp.float32), precision=highest_precision)
        value_out, slopes = gelu_pair(pre_activation)
        hidden_act = value_out.astype(jnp.bfloat16)
        rank_sum = rank_sum + jnp.dot(hidden_act, output_adapter_first, preferred_element_type=jnp.float32)
        dense_backward = jnp.dot(cotangent, output_weight.T, preferred_element_type=jnp.float32) + ADAPTER_SCALE * jnp.dot(backward_lowrank, output_adapter_first.astype(jnp.float32).T, precision=highest_precision)
        grad_pre = (dense_backward * slopes).astype(jnp.bfloat16)
        back_sum = back_sum + jnp.dot(grad_pre, input_second_factor.T, preferred_element_type=jnp.float32)
        dense_total_sum = dense_total_sum + jnp.dot(grad_pre, input_weight.T, preferred_element_type=jnp.float32)
        grad_oa = gradient_scale * jnp.dot(hidden_act.astype(jnp.float32).T, backward_lowrank, precision=highest_precision)
        grad_ib = gradient_scale * jnp.dot(lowrank_input.T, grad_pre.astype(jnp.float32), precision=highest_precision)
        return ((rank_sum, back_sum, dense_total_sum), (grad_oa, grad_ib))
    initial = (jnp.zeros((TOKEN_COUNT, RANK), jnp.float32), jnp.zeros((TOKEN_COUNT, RANK), jnp.float32), jnp.zeros((TOKEN_COUNT, D), jnp.float32))
    (rank_out, rank_backward, dense_total_sum), (oa_blocks, ib_blocks) = lax.scan(one_block, initial, jnp.arange(N_HID, dtype=jnp.int32))
    grad_out_a = oa_blocks.reshape(FF, RANK)
    grad_in_b = jnp.transpose(ib_blocks, (1, 0, 2)).reshape(RANK, FF)
    input_gradient = dense_total_sum + ADAPTER_SCALE * jnp.dot(rank_backward, input_adapter_first.astype(jnp.float32).T, precision=highest_precision)
    grad_out_b = gradient_scale * jnp.dot(rank_out.T, cotangent.astype(jnp.float32), precision=highest_precision)
    grad_in_a = gradient_scale * jnp.dot(tokens.astype(jnp.float32).T, rank_backward, precision=highest_precision)
    return (input_gradient, grad_in_a, grad_in_b, grad_out_a, grad_out_b)
```

```python
import functools
import math

import jax
import jax.numpy as jnp
from jax import lax
from jax.experimental import pallas as pl
from jax.experimental.pallas import tpu as pltpu
from jax.sharding import PartitionSpec as P

ADAPTER_SCALE = 0.5
GELU_K = 0.7978845608
GELU_C = 0.044715
F32 = jnp.float32
BF16 = jnp.bfloat16


def gelu_pair(pre_activation):
    tangent = jnp.tanh(
        GELU_K * (pre_activation + GELU_C * pre_activation * pre_activation * pre_activation)
    )
    value_out = 0.5 * pre_activation * (1.0 + tangent)
    slopes = 0.5 * (1.0 + tangent) + 0.5 * pre_activation * (1.0 - tangent * tangent) * GELU_K * (
        1.0 + 3.0 * GELU_C * pre_activation * pre_activation
    )
    return (value_out, slopes)


def dot(left, right, dims):
    return lax.dot_general(left, right, (dims, ((), ())), preferred_element_type=F32)


def nn(left, right):
    return dot(left, right, ((1,), (0,)))


def nt(left, right):
    return dot(left, right, ((1,), (1,)))


def tn(left, right):
    return dot(left, right, ((0,), (0,)))


def split(value):
    high = value.astype(BF16)
    return high, (value - high.astype(F32)).astype(BF16)


def fused_kernel(
    n_tok, n_hid, n_part, scale,
    tokens, cotangent, w_in, w_out, in_a, in_b, out_a, out_b,
    dx_out, terms_out, oa_all, ib_all,
    x, c, full_in, full_out, full_a, b_mat, second, first, second2, first2, a2,
    low, back, pre_s, back_s, act_s, grad_s, dense, rank_out, rank_back, oa_acc, ib_acc, terms,
    core_d, core_t, send_d, send_t, recv_d, recv_t, kept_d, kept_t, tok_send, tok_recv, all_t,
    act_send, act_recv, chip_sem, core_sem, first_sem, first_core_sem, w_sem, own_sem,
    core_r_sem, chip_r_sem, tok_sem, term_sem, grad_send, grad_recv,
):
    t, h = lax.axis_index("tok"), lax.axis_index("hid")
    n_chip = n_hid // 2
    chip, core = h // 2, h % 2
    rows, cols = tokens.shape
    depth = w_in.shape[0]
    width = full_in.shape[1]
    part_width = width // n_part
    rank = full_a.shape[1]

    def remote(source, target, send, recv, where):
        return pltpu.make_async_remote_copy(
            src_ref=source, dst_ref=target, send_sem=send, recv_sem=recv,
            device_id=where, device_id_type=pl.DeviceIdType.MESH,
        )

    def begin(*arguments):
        copy = remote(*arguments)
        copy.start()
        return copy

    sibling = (t, 2 * chip + 1 - core)
    chips = [(t, 2 * ((chip + e) % n_chip) + core) for e in range(n_chip)]
    toks = [((t + d) % n_tok, h) for d in range(n_tok)]
    barrier = pltpu.get_barrier_semaphore()
    for where in [sibling] + chips[1:] + toks[1:]:
        pl.semaphore_signal(barrier, inc=1, device_id=where, device_id_type=pl.DeviceIdType.MESH)
    pl.semaphore_wait(barrier, n_chip + n_tok - 1)

    orders = [sorted(range(n_tok), key=lambda s: (abs(s - k), s)) for k in range(n_tok)]
    sources = [t]
    for j in range(1, n_tok):
        source = jnp.int32(orders[0][j])
        for k in range(1, n_tok):
            source = jnp.where(t == k, jnp.int32(orders[k][j]), source)
        sources.append(source)

    def row_at(source):
        return pl.multiple_of(source * rows, rows)

    def part(array, source, e):
        at_col = pl.multiple_of((2 * ((chip + n_chip - e) % n_chip) + core) * cols, cols)
        return array.at[pl.ds(row_at(source), rows), pl.ds(at_col, cols)]

    def along(source, blocks, send, recv, act):
        @pl.when((source <= t) & (t + 1 < n_tok))
        def _():
            for k, (block, target) in enumerate(blocks):
                act(remote(block, target, send(0, source, k), recv(source, k), (t + 1, h)))

        @pl.when((source >= t) & (t > 0))
        def _():
            for k, (block, target) in enumerate(blocks):
                act(remote(block, target, send(1, source, k), recv(source, k), (t - 1, h)))

    def start(copy):
        copy.start()

    def wait_send(copy):
        copy.wait_send()

    def act_blocks(j):
        source = sources[j]
        mine = (tokens, cotangent)
        return [
            (mine[k] if j == 0 else part(array, source, 0), part(array, source, 0))
            for k, array in enumerate((x, c))
        ]

    def act_along(j, act):
        along(
            sources[j], act_blocks(j),
            lambda way, source, k: act_send.at[way, source, k],
            lambda source, k: act_recv.at[source, k], act,
        )

    from_chip, from_core = {}, {}

    def to_chips(j):
        for e in range(1, n_chip):
            from_chip[j, e] = [
                begin(block, target, chip_sem.at[0, j, e - 1, k], chip_sem.at[1, j, e - 1, k], chips[e])
                for k, (block, target) in enumerate(act_blocks(j))
            ]

    def to_core(j, e):
        if e == 0:
            blocks = act_blocks(j)
        else:
            blocks = [(part(array, sources[j], e),) * 2 for array in (x, c)]
        from_core[j, e] = [
            begin(block, target, core_sem.at[0, j, e, k], core_sem.at[1, j, e, k], sibling)
            for k, (block, target) in enumerate(blocks)
        ]

    def first_part(e):
        at = pl.multiple_of((2 * ((chip + n_chip - e) % n_chip) + core) * cols, cols)
        return full_a.at[pl.ds(at, cols), :]

    weights = {}
    depths = pl.ds(pl.multiple_of(t * depth, depth), depth)

    def weight_blocks(d, p):
        at = pl.multiple_of(((t + d) % n_tok) * width + p * part_width, part_width)
        here = pl.ds(p * part_width, part_width)
        return [
            (w_in.at[:, pl.ds(at, part_width)], full_in.at[depths, here]),
            (w_out.at[pl.ds(at, part_width), :], full_out.at[here, depths]),
        ]

    def send_weight(d, p, k):
        block, target = weight_blocks(d, p)[k]
        weights[d, p, k] = begin(
            block, target, w_sem.at[0, d - 1, p, k], w_sem.at[1, d - 1, p, k], toks[d]
        )

    act_along(0, start)
    to_chips(0)
    firsts = [
        begin(in_a, first_part(0), first_sem.at[0, e - 1], first_sem.at[1, e - 1], chips[e])
        for e in range(1, n_chip)
    ]
    to_core(0, 0)
    a_core = [begin(in_a, first_part(0), first_core_sem.at[0, 0], first_core_sem.at[1, 0], sibling)]
    for d in range(1, n_tok):
        send_weight(d, 0, 0)
    at = pl.multiple_of(t * width, width)
    own = [(block, target) for block, target in act_blocks(0)]
    own += [(in_a, first_part(0)), (out_b, b_mat)]
    own += [(in_b.at[:, pl.ds(at, width)], second), (out_a.at[pl.ds(at, width), :], first)]
    for p in range(n_part):
        own += weight_blocks(0, p)
    own = [
        pltpu.make_async_copy(block, target, own_sem.at[k])
        for k, (block, target) in enumerate(own)
    ]
    for copy in own:
        copy.start()

    def arrive(j):
        for k, (block, target) in enumerate(act_blocks(j)):
            remote(
                target, target, act_send.at[0, sources[j], k], act_recv.at[sources[j], k], sibling
            ).wait_recv()
        act_along(j, start)
        to_chips(j)
        to_core(j, 0)

    def pass_on(j):
        for e in range(1, n_chip):
            for copy in from_chip[j, e]:
                copy.wait_recv()
            to_core(j, e)

    def complete(j):
        for e in range(n_chip):
            for copy in from_core[j, e]:
                copy.wait_recv()

    def ranks(source):
        here = pl.ds(row_at(source), rows)
        high, rest = split(nn(x[here, :], full_a[...]))
        low[here, :rank] = high
        low[here, rank:] = rest
        high, rest = split(nt(c[here, :], b_mat[...]))
        back[here, :rank] = high
        back[here, rank:] = rest

    def hidden(p, source, begun):
        here = pl.ds(row_at(source), rows)
        those = slice(p * part_width, (p + 1) * part_width)
        pre_s[...] = nn(x[here, :], full_in[:, those]) + nn(low[here, :], second2[:, those])
        back_s[...] = nt(c[here, :], full_out[those, :]) + nt(back[here, :], first2[those, :])
        step = rows // 8
        for at in range(0, rows, step):
            some = slice(at, at + step)
            value_out, slopes = gelu_pair(pre_s[some, :])
            act_s[some, :] = value_out.astype(BF16)
            grad_s[some, :] = (back_s[some, :] * slopes).astype(BF16)
        act, grad = act_s[...], grad_s[...]
        oa_new, ib_new = tn(act, back[here, :]), tn(low[here, :], grad)
        out_new, back_new = nn(act, first[those, :]), nt(grad, second[:, those])
        if begun:
            oa_acc[p] += oa_new
            ib_acc[p] += ib_new
        else:
            oa_acc[p] = oa_new
            ib_acc[p] = ib_new
        if p == 0:
            rank_out[here, :] = out_new
            rank_back[here, :] = back_new
        else:
            rank_out[here, :] += out_new
            rank_back[here, :] += back_new
        if p < n_part - 1:
            if p == 0:
                dense[here, :] = nt(grad, full_in[:, those])
            else:
                dense[here, :] += nt(grad, full_in[:, those])
            return
        high, rest = split(rank_back[here, :])
        low[here, :rank] = high
        low[here, rank:] = rest
        high, rest = split(rank_out[here, :])
        back[here, :rank] = high
        back[here, rank:] = rest
        value = nt(grad, full_in[:, those]) + nt(low[here, :], a2[...])
        dense[here, :] = dense[here, :] + value if n_part > 1 else value

    for j in range(1, n_tok):
        arrive(j)
        if j == 1:
            for d in range(1, n_tok):
                send_weight(d, 0, 1)
            for e in range(1, n_chip):
                firsts[e - 1].wait_recv()
                a_core.append(begin(
                    first_part(e), first_part(e), first_core_sem.at[0, e], first_core_sem.at[1, e],
                    sibling,
                ))
        if j == n_tok - 1:
            for p in range(1, n_part):
                for d in range(1, n_tok):
                    for k in range(2):
                        send_weight(d, p, k)
        pass_on(j - 1)
        if j == 1:
            for copy in own:
                copy.wait()
            for copy in a_core:
                copy.wait_recv()
            half = (ADAPTER_SCALE * second[...].astype(F32)).astype(BF16)
            second2[:rank, :] = half
            second2[rank:, :] = half
            half = (ADAPTER_SCALE * first[...].astype(F32)).astype(BF16)
            first2[:, :rank] = half
            first2[:, rank:] = half
            half = (ADAPTER_SCALE * full_a[...].astype(F32)).astype(BF16)
            a2[:, :rank] = half
            a2[:, rank:] = half
        complete(j - 1)
        ranks(sources[j - 1])

    def wait_weights(p):
        for d in range(1, n_tok):
            for k in range(2):
                weights[d, p, k].wait_recv()

    def oa_blocks(source, p):
        at = pl.multiple_of(source * width + p * part_width, part_width)
        oa_at, ib_at = oa_all.at[pl.ds(at, part_width), :], ib_all.at[:, pl.ds(at, part_width)]
        return [(oa_at, oa_at), (ib_at, ib_at)]

    def oa_along(j, p, act):
        along(
            sources[j], oa_blocks(sources[j], p),
            lambda way, source, k: grad_send.at[way, source, p, k],
            lambda source, k: grad_recv.at[source, p, k], act,
        )

    def finish_grads(p):
        at = pl.multiple_of(t * width + p * part_width, part_width)
        oa = oa_acc[p]
        oa_all[pl.ds(at, part_width), :] = (scale * (oa[:, :rank] + oa[:, rank:])).astype(BF16)
        ib = ib_acc[p]
        ib_all[:, pl.ds(at, part_width)] = (scale * (ib[:rank] + ib[rank:])).astype(BF16)
        oa_along(0, p, start)

    def relay_grads(j, p):
        for k, (block, target) in enumerate(oa_blocks(sources[j], p)):
            remote(
                target, target, grad_send.at[0, sources[j], p, k], grad_recv.at[sources[j], p, k],
                sibling,
            ).wait_recv()
        oa_along(j, p, start)

    wait_weights(0)
    if n_part > 1:
        for j in range(n_tok - 1):
            hidden(0, sources[j], j > 0)
    pass_on(n_tok - 1)
    complete(n_tok - 1)
    ranks(sources[n_tok - 1])
    if n_part > 1:
        hidden(0, sources[n_tok - 1], True)
        finish_grads(0)
    for p in range(1, n_part - 1):
        wait_weights(p)
        for j in range(n_tok):
            hidden(p, sources[j], j > 0)
        finish_grads(p)
    last = n_part - 1
    if last > 0:
        wait_weights(last)

    def block(index, parity):
        return pl.ds(pl.multiple_of((2 * index + parity) * cols, cols), cols)

    def tok_rows(d):
        return pl.ds(row_at((t + d) % n_tok), rows)

    chunks = list(range(1, n_tok)) + [0, None]
    core_copies, chip_copies, tok_copies = {}, {}, []

    def to_sibling(q):
        d = chunks[q]
        core_copies[q] = []
        for e in range(n_chip):
            columns = block((chip + e) % n_chip, 1 - core)
            source = terms.at[:, columns] if d is None else dense.at[tok_rows(d), columns]
            target = core_t.at[e] if d is None else core_d.at[d, e]
            core_copies[q].append(
                begin(source, target, core_r_sem.at[0, q, e], core_r_sem.at[1, q, e], sibling)
            )

    def over_core(q):
        d = chunks[q]
        chip_copies[q] = []
        for e in list(range(1, n_chip)) + [0]:
            core_copies[q][e].wait_recv()
            columns = block((chip + e) % n_chip, core)
            if d is None:
                value = terms[:, columns] + core_t[e]
            else:
                value = dense[tok_rows(d), columns] + core_d[d, e]
            if e == 0:
                if d is None:
                    kept_t[...] = value
                else:
                    kept_d[d] = value
                continue
            sent, got = (send_t, recv_t) if d is None else (send_d.at[d], recv_d.at[d])
            sent[e - 1] = value.astype(BF16)
            chip_copies[q].append(begin(
                sent.at[e - 1], got.at[e - 1],
                chip_r_sem.at[0, q, e - 1], chip_r_sem.at[1, q, e - 1], chips[e],
            ))

    def over_chips(q):
        d = chunks[q]
        for copy in chip_copies[q]:
            copy.wait_recv()
        got = recv_t if d is None else recv_d.at[d]
        value = kept_t[...] if d is None else kept_d[d]
        for e in range(n_chip - 1):
            value = value + got[e].astype(F32)
        if d is None:
            all_t[t] = value.astype(BF16)
            for k in range(1, n_tok):
                tok_copies.append(begin(
                    all_t.at[t], all_t.at[t], term_sem.at[0, k - 1], term_sem.at[1, k - 1], toks[k]
                ))
        elif d == 0:
            kept_d[0] = value
        else:
            tok_send[d - 1] = value.astype(BF16)
            tok_copies.append(begin(
                tok_send.at[d - 1], tok_recv.at[d - 1],
                tok_sem.at[0, d - 1], tok_sem.at[1, d - 1], toks[d],
            ))

    for q in range(n_tok):
        hidden(last, (t + chunks[q]) % n_tok, q > 0)
        to_sibling(q)
        if q >= 1:
            over_core(q - 1)
        if q >= 2:
            over_chips(q - 2)
            for p in range(last):
                relay_grads(q - 1, p)
    finish_grads(last)
    over_core(n_tok - 1)
    out_cols = x.shape[1] // n_chip
    for at in range(0, x.shape[1], out_cols):
        those = slice(at, at + out_cols)
        value = tn(back[...], c[:, those])
        terms[:rank, those] = scale * (value[:rank] + value[rank:])
        value = tn(low[...], x[:, those])
        terms[rank:, those] = scale * (value[:rank] + value[rank:])
    to_sibling(n_tok)
    for j in range(n_tok - 1, n_tok):
        for p in range(last):
            relay_grads(j, p)
    over_chips(n_tok - 2)
    relay_grads(1, last)
    over_core(n_tok)
    for j in range(2, n_tok):
        relay_grads(j, last)
    over_chips(n_tok - 1)
    over_chips(n_tok)
    for copy in tok_copies:
        copy.wait_recv()
    value = kept_d[0]
    for d in range(1, n_tok):
        value = value + tok_recv[d - 1].astype(F32)
    dx_out[...] = value
    value = all_t[0].astype(F32)
    for k in range(1, n_tok):
        value = value + all_t[k].astype(F32)
    terms_out[...] = value
    for j in range(n_tok):
        act_along(j, wait_send)
        for p in range(n_part):
            oa_along(j, p, wait_send)
    for groups in (from_chip, from_core, core_copies, chip_copies):
        for group in groups.values():
            for copy in group:
                copy.wait_send()
    for copy in firsts + a_core + list(weights.values()) + tok_copies:
        copy.wait_send()


def fused(n_part, scale, tokens, cotangent, frozen_in, frozen_out, in_a, in_b, out_a, out_b):
    n_tok, n_hid = lax.axis_size("tok"), lax.axis_size("hid")
    n_chip = n_hid // 2
    rows, cols = tokens.shape
    count, features = rows * n_tok, cols * n_hid
    width = frozen_in.shape[1] // n_tok
    part_width = width // n_part
    rank = in_a.shape[1]
    sems = pltpu.SemaphoreType.DMA
    vmem = pl.BlockSpec(memory_space=pltpu.VMEM)
    whole = pl.BlockSpec(memory_space=pl.ANY)
    return pl.pallas_call(
        functools.partial(fused_kernel, n_tok, n_hid, n_part, scale),
        out_shape=(
            jax.ShapeDtypeStruct((rows, cols), F32),
            jax.ShapeDtypeStruct((2 * rank, cols), F32),
            jax.ShapeDtypeStruct((n_tok * width, rank), BF16),
            jax.ShapeDtypeStruct((rank, n_tok * width), BF16),
        ),
        in_specs=[whole] * 8,
        out_specs=(vmem,) * 4,
        scratch_shapes=[
            pltpu.VMEM((count, features), BF16),
            pltpu.VMEM((count, features), BF16),
            pltpu.VMEM((features, width), BF16),
            pltpu.VMEM((width, features), BF16),
            pltpu.VMEM((features, rank), BF16),
            pltpu.VMEM((rank, features), BF16),
            pltpu.VMEM((rank, width), BF16),
            pltpu.VMEM((width, rank), BF16),
            pltpu.VMEM((2 * rank, width), BF16),
            pltpu.VMEM((width, 2 * rank), BF16),
            pltpu.VMEM((features, 2 * rank), BF16),
            pltpu.VMEM((count, 2 * rank), BF16),
            pltpu.VMEM((count, 2 * rank), BF16),
            pltpu.VMEM((rows, part_width), F32),
            pltpu.VMEM((rows, part_width), F32),
            pltpu.VMEM((rows, part_width), BF16),
            pltpu.VMEM((rows, part_width), BF16),
            pltpu.VMEM((count, features), F32),
            pltpu.VMEM((count, rank), F32),
            pltpu.VMEM((count, rank), F32),
            pltpu.VMEM((n_part, part_width, 2 * rank), F32),
            pltpu.VMEM((n_part, 2 * rank, part_width), F32),
            pltpu.VMEM((2 * rank, features), F32),
            pltpu.VMEM((n_tok, n_chip, rows, cols), F32),
            pltpu.VMEM((n_chip, 2 * rank, cols), F32),
            pltpu.VMEM((n_tok, n_chip - 1, rows, cols), BF16),
            pltpu.VMEM((n_chip - 1, 2 * rank, cols), BF16),
            pltpu.VMEM((n_tok, n_chip - 1, rows, cols), BF16),
            pltpu.VMEM((n_chip - 1, 2 * rank, cols), BF16),
            pltpu.VMEM((n_tok, rows, cols), F32),
            pltpu.VMEM((2 * rank, cols), F32),
            pltpu.VMEM((n_tok - 1, rows, cols), BF16),
            pltpu.VMEM((n_tok - 1, rows, cols), BF16),
            pltpu.VMEM((n_tok, 2 * rank, cols), BF16),
            sems((2, n_tok, 2)),
            sems((n_tok, 2)),
            sems((2, n_tok, n_chip - 1, 2)),
            sems((2, n_tok, n_chip, 2)),
            sems((2, n_chip - 1)),
            sems((2, n_chip)),
            sems((2, n_tok - 1, n_part, 2)),
            sems((6 + 2 * n_part,)),
            sems((2, n_tok + 1, n_chip)),
            sems((2, n_tok + 1, n_chip - 1)),
            sems((2, n_tok - 1)),
            sems((2, n_tok - 1)),
            sems((2, n_tok, n_part, 2)),
            sems((n_tok, n_part, 2)),
        ],
        compiler_params=pltpu.CompilerParams(
            collective_id=1, has_side_effects=True, vmem_limit_bytes=52 * 1024 * 1024
        ),
    )(tokens, cotangent, frozen_in, frozen_out, in_a, in_b, out_a, out_b)


def finish_kernel(dx, terms, oa, ib, dx_out, in_a_out, ib_out, oa_out, out_b_out):
    rank = in_a_out.shape[1]
    ib_out[...] = ib[...].astype(F32)
    oa_out[...] = oa[...].astype(F32)
    dx_out[...] = dx[...]
    in_a_out[...] = terms[rank:, :].T
    out_b_out[...] = terms[:rank, :]


def local(tokens, cotangent, frozen_in, frozen_out, in_a, in_b, out_a, out_b):
    count = tokens.shape[0] * lax.axis_size("tok")
    scale = ADAPTER_SCALE / math.sqrt(count)
    dx, terms, oa, ib = fused(
        2, scale, tokens, cotangent, frozen_in, frozen_out, in_a, in_b, out_a, out_b
    )
    rank, cols = in_a.shape[1], tokens.shape[1]
    vmem = pl.BlockSpec(memory_space=pltpu.VMEM)
    return pl.pallas_call(
        finish_kernel,
        out_shape=(
            jax.ShapeDtypeStruct(dx.shape, F32),
            jax.ShapeDtypeStruct((cols, rank), F32),
            jax.ShapeDtypeStruct(ib.shape, F32),
            jax.ShapeDtypeStruct(oa.shape, F32),
            jax.ShapeDtypeStruct((rank, cols), F32),
        ),
        in_specs=[vmem] * 4,
        out_specs=(vmem,) * 5,
        compiler_params=pltpu.CompilerParams(vmem_limit_bytes=16 * 1024 * 1024),
    )(dx, terms, oa, ib)


def local_by_rows(
    tokens,
    cotangent,
    frozen_in,
    frozen_out,
    input_adapter_first,
    input_adapter_second,
    adapter_out_a,
    adapter_out_b,
):
    highest_precision = lax.Precision.HIGHEST
    device_local_rows = tokens.shape[0]
    rank_width = input_adapter_second.shape[0]
    gradient_scale = ADAPTER_SCALE / math.sqrt(device_local_rows * lax.axis_size("tok"))
    full_tokens, full_cotan = (
        lax.all_gather(tokens, "hid", axis=1, tiled=True),
        lax.all_gather(cotangent, "hid", axis=1, tiled=True),
    )
    in_rows = lax.all_gather(frozen_in, "tok", axis=0, tiled=True)
    in_a_full = lax.all_gather(input_adapter_first, "hid", axis=0, tiled=True)
    lowrank_input = jnp.dot(full_tokens, in_a_full, preferred_element_type=jnp.float32)
    second_float = input_adapter_second.astype(jnp.float32)
    out_a_float = adapter_out_a.astype(jnp.float32)
    pre_activation = jnp.dot(
        full_tokens, in_rows, preferred_element_type=jnp.float32
    ) + ADAPTER_SCALE * jnp.dot(lowrank_input, second_float, precision=highest_precision)
    value_out, slopes = gelu_pair(pre_activation)
    hidden_act = value_out.astype(jnp.bfloat16)
    backward_lowrank = jnp.einsum(
        "td,rd->tr", full_cotan, adapter_out_b, preferred_element_type=jnp.float32
    )
    rank_out = jnp.dot(hidden_act, adapter_out_a, preferred_element_type=jnp.float32)
    dense_backward = jnp.einsum(
        "td,fd->tf",
        full_cotan,
        lax.all_gather(frozen_out, "tok", axis=1, tiled=True),
        preferred_element_type=jnp.float32,
    )
    dense_backward = dense_backward + ADAPTER_SCALE * jnp.dot(
        backward_lowrank, out_a_float.T, precision=highest_precision
    )
    grad_pre = (dense_backward * slopes).astype(jnp.bfloat16)
    rank_backward = jnp.einsum(
        "tf,rf->tr", grad_pre, input_adapter_second, preferred_element_type=jnp.float32
    )
    dense_in = jnp.einsum("tf,df->td", grad_pre, in_rows, preferred_element_type=jnp.float32)
    grad_out_a = gradient_scale * jnp.dot(
        hidden_act.astype(jnp.float32).T, backward_lowrank, precision=highest_precision
    )
    grad_in_b = gradient_scale * jnp.dot(
        lowrank_input.T, grad_pre.astype(jnp.float32), precision=highest_precision
    )
    in_a_float = in_a_full.astype(jnp.float32)
    dx_term = dense_in + ADAPTER_SCALE * jnp.dot(
        rank_backward, in_a_float.T, precision=highest_precision
    )
    out_term = jnp.dot(rank_out.T, full_cotan.astype(jnp.float32), precision=highest_precision)
    in_term = jnp.dot(rank_backward.T, full_tokens.astype(jnp.float32), precision=highest_precision)
    rank_terms = jnp.concatenate([out_term, in_term], axis=0)
    input_gradient, rank_local = (
        lax.psum_scatter(dx_term, "hid", scatter_dimension=1, tiled=True),
        lax.psum_scatter(rank_terms, "hid", scatter_dimension=1, tiled=True),
    )
    grad_out_a, grad_in_b, rank_total = lax.psum((grad_out_a, grad_in_b, rank_local), "tok")
    grad_out_b = gradient_scale * rank_total[:rank_width]
    grad_in_a = gradient_scale * rank_total[rank_width:].T
    return (input_gradient, grad_in_a, grad_in_b, grad_out_a, grad_out_b)


def solution(mesh):
    in_specs = (
        P("tok", "hid"),
        P("tok", "hid"),
        P("tok", "hid"),
        P("hid", "tok"),
        P("hid", None),
        P(None, "hid"),
        P("hid", None),
        P(),
    )
    out_specs = (P("tok", "hid"), P("hid", None), P(None, "hid"), P("hid", None), P(None, "hid"))
    def body(*arrays):
        share = arrays[2].shape[1] // lax.axis_size("tok")
        return local(*arrays) if share % 256 == 0 else local_by_rows(*arrays)

    return jax.shard_map(body, mesh=mesh, in_specs=in_specs, out_specs=out_specs, check_vma=False)
```

```python
import functools
import math

import jax
import jax.numpy as jnp
from jax import lax
from jax.experimental import pallas as pl
from jax.experimental.pallas import tpu as pltpu
from jax.sharding import PartitionSpec as P

ADAPTER_SCALE = 0.5
GELU_K = 0.7978845608
GELU_C = 0.044715
F32 = jnp.float32
BF16 = jnp.bfloat16


def gelu_pair(pre_activation):
    tangent = jnp.tanh(
        GELU_K * (pre_activation + GELU_C * pre_activation * pre_activation * pre_activation)
    )
    value_out = 0.5 * pre_activation * (1.0 + tangent)
    slopes = 0.5 * (1.0 + tangent) + 0.5 * pre_activation * (1.0 - tangent * tangent) * GELU_K * (
        1.0 + 3.0 * GELU_C * pre_activation * pre_activation
    )
    return (value_out, slopes)


def dot(left, right, dims):
    return lax.dot_general(left, right, (dims, ((), ())), preferred_element_type=F32)


def nn(left, right):
    return dot(left, right, ((1,), (0,)))


def nt(left, right):
    return dot(left, right, ((1,), (1,)))


def tn(left, right):
    return dot(left, right, ((0,), (0,)))


def split(value):
    high = value.astype(BF16)
    return high, (value - high.astype(F32)).astype(BF16)


def fused_kernel(
    n_tok, n_hid, n_part, scale,
    tokens, cotangent, w_in, w_out, in_a, in_b, out_a, out_b,
    dx_out, terms_out, oa_all, ib_all,
    x, c, full_in, full_out, full_a, b_mat, second, first, second2, first2, a2,
    low, back, pre_s, back_s, act_s, grad_s, dense, rank_out, rank_back, oa_acc, ib_acc, terms,
    core_d, core_t, kept_d, kept_t, pend_d, pend_t, one_send, one_send_t, one_recv, one_recv_t,
    two_send, two_send_t, two_recv, two_recv_t, line_send, line_recv, all_t,
    act_send, act_recv, chip_sem, core_sem, first_sem, first_core_sem, w_sem, own_sem,
    core_r_sem, one_sem, two_sem, line_sem, line_got, term_sem, grad_send, grad_recv,
):
    t, h = lax.axis_index("tok"), lax.axis_index("hid")
    n_chip = n_hid // 2
    chip, core = h // 2, h % 2
    rows, cols = tokens.shape
    depth = w_in.shape[0]
    width = full_in.shape[1]
    part_width = width // n_part
    rank = full_a.shape[1]

    def remote(source, target, send, recv, where):
        return pltpu.make_async_remote_copy(
            src_ref=source, dst_ref=target, send_sem=send, recv_sem=recv,
            device_id=where, device_id_type=pl.DeviceIdType.MESH,
        )

    def begin(*arguments):
        copy = remote(*arguments)
        copy.start()
        return copy

    sibling = (t, 2 * chip + 1 - core)
    chips = [(t, 2 * ((chip + e) % n_chip) + core) for e in range(n_chip)]
    toks = [((t + d) % n_tok, h) for d in range(n_tok)]
    barrier = pltpu.get_barrier_semaphore()
    for where in [sibling] + chips[1:] + toks[1:]:
        pl.semaphore_signal(barrier, inc=1, device_id=where, device_id_type=pl.DeviceIdType.MESH)
    pl.semaphore_wait(barrier, n_chip + n_tok - 1)

    orders = [sorted(range(n_tok), key=lambda s: (abs(s - k), s)) for k in range(n_tok)]
    sources = [t]
    for j in range(1, n_tok):
        source = jnp.int32(orders[0][j])
        for k in range(1, n_tok):
            source = jnp.where(t == k, jnp.int32(orders[k][j]), source)
        sources.append(source)

    def row_at(source):
        return pl.multiple_of(source * rows, rows)

    def part(array, source, e):
        at_col = pl.multiple_of((2 * ((chip + n_chip - e) % n_chip) + core) * cols, cols)
        return array.at[pl.ds(row_at(source), rows), pl.ds(at_col, cols)]

    def along(source, blocks, send, recv, act):
        @pl.when((source <= t) & (t + 1 < n_tok))
        def _():
            for k, (block, target) in enumerate(blocks):
                act(remote(block, target, send(0, source, k), recv(source, k), (t + 1, h)))

        @pl.when((source >= t) & (t > 0))
        def _():
            for k, (block, target) in enumerate(blocks):
                act(remote(block, target, send(1, source, k), recv(source, k), (t - 1, h)))

    def start(copy):
        copy.start()

    def wait_send(copy):
        copy.wait_send()

    def act_blocks(j):
        source = sources[j]
        mine = (tokens, cotangent)
        return [
            (mine[k] if j == 0 else part(array, source, 0), part(array, source, 0))
            for k, array in enumerate((x, c))
        ]

    def act_along(j, act):
        along(
            sources[j], act_blocks(j),
            lambda way, source, k: act_send.at[way, source, k],
            lambda source, k: act_recv.at[source, k], act,
        )

    from_chip, from_core = {}, {}

    def to_chips(j):
        for e in range(1, n_chip):
            from_chip[j, e] = [
                begin(block, target, chip_sem.at[0, j, e - 1, k], chip_sem.at[1, j, e - 1, k], chips[e])
                for k, (block, target) in enumerate(act_blocks(j))
            ]

    def to_core(j, e):
        if e == 0:
            blocks = act_blocks(j)
        else:
            blocks = [(part(array, sources[j], e),) * 2 for array in (x, c)]
        from_core[j, e] = [
            begin(block, target, core_sem.at[0, j, e, k], core_sem.at[1, j, e, k], sibling)
            for k, (block, target) in enumerate(blocks)
        ]

    def first_part(e):
        at = pl.multiple_of((2 * ((chip + n_chip - e) % n_chip) + core) * cols, cols)
        return full_a.at[pl.ds(at, cols), :]

    weights = {}
    depths = pl.ds(pl.multiple_of(t * depth, depth), depth)

    def weight_blocks(d, p):
        at = pl.multiple_of(((t + d) % n_tok) * width + p * part_width, part_width)
        here = pl.ds(p * part_width, part_width)
        return [
            (w_in.at[:, pl.ds(at, part_width)], full_in.at[depths, here]),
            (w_out.at[pl.ds(at, part_width), :], full_out.at[here, depths]),
        ]

    def send_weight(d, p, k):
        block, target = weight_blocks(d, p)[k]
        weights[d, p, k] = begin(
            block, target, w_sem.at[0, d - 1, p, k], w_sem.at[1, d - 1, p, k], toks[d]
        )

    act_along(0, start)
    to_chips(0)
    firsts = [
        begin(in_a, first_part(0), first_sem.at[0, e - 1], first_sem.at[1, e - 1], chips[e])
        for e in range(1, n_chip)
    ]
    to_core(0, 0)
    a_core = [begin(in_a, first_part(0), first_core_sem.at[0, 0], first_core_sem.at[1, 0], sibling)]
    pieces = [(d, p, k) for p in range(n_part) for k in range(2) for d in range(1, n_tok)]
    pieces = [piece for piece in pieces if piece[1:] != (0, 0) or piece[0] in (1, n_tok - 1)]
    rest = [(d, 0, 0) for d in range(2, n_tok - 1)] + pieces[min(2, n_tok - 1):]
    for piece in pieces[:min(2, n_tok - 1)]:
        send_weight(*piece)
    at = pl.multiple_of(t * width, width)
    own = [(block, target) for block, target in act_blocks(0)]
    own += [(in_a, first_part(0)), (out_b, b_mat)]
    own += [(in_b.at[:, pl.ds(at, width)], second), (out_a.at[pl.ds(at, width), :], first)]
    for p in range(n_part):
        own += weight_blocks(0, p)
    own = [
        pltpu.make_async_copy(block, target, own_sem.at[k])
        for k, (block, target) in enumerate(own)
    ]
    for copy in own:
        copy.start()

    def arrive(j):
        for k, (block, target) in enumerate(act_blocks(j)):
            remote(
                target, target, act_send.at[0, sources[j], k], act_recv.at[sources[j], k], sibling
            ).wait_recv()
        act_along(j, start)
        to_chips(j)
        to_core(j, 0)

    def pass_on(j):
        for e in range(1, n_chip):
            for copy in from_chip[j, e]:
                copy.wait_recv()
            to_core(j, e)

    def complete(j):
        for e in range(n_chip):
            for copy in from_core[j, e]:
                copy.wait_recv()

    def ranks(source):
        here = pl.ds(row_at(source), rows)
        high, rest = split(nn(x[here, :], full_a[...]))
        low[here, :rank] = high
        low[here, rank:] = rest
        high, rest = split(nt(c[here, :], b_mat[...]))
        back[here, :rank] = high
        back[here, rank:] = rest

    def hidden(p, source, begun):
        here = pl.ds(row_at(source), rows)
        those = slice(p * part_width, (p + 1) * part_width)
        pre_s[...] = nn(x[here, :], full_in[:, those]) + nn(low[here, :], second2[:, those])
        back_s[...] = nt(c[here, :], full_out[those, :]) + nt(back[here, :], first2[those, :])
        step = rows // 8
        for at in range(0, rows, step):
            some = slice(at, at + step)
            value_out, slopes = gelu_pair(pre_s[some, :])
            act_s[some, :] = value_out.astype(BF16)
            grad_s[some, :] = (back_s[some, :] * slopes).astype(BF16)
        act, grad = act_s[...], grad_s[...]
        oa_new, ib_new = tn(act, back[here, :]), tn(low[here, :], grad)
        out_new, back_new = nn(act, first[those, :]), nt(grad, second[:, those])
        if begun:
            oa_acc[p] += oa_new
            ib_acc[p] += ib_new
        else:
            oa_acc[p] = oa_new
            ib_acc[p] = ib_new
        if p == 0:
            rank_out[here, :] = out_new
            rank_back[here, :] = back_new
        else:
            rank_out[here, :] += out_new
            rank_back[here, :] += back_new
        if p < n_part - 1:
            if p == 0:
                dense[here, :] = nt(grad, full_in[:, those])
            else:
                dense[here, :] += nt(grad, full_in[:, those])
            return
        high, rest = split(rank_back[here, :])
        low[here, :rank] = high
        low[here, rank:] = rest
        high, rest = split(rank_out[here, :])
        back[here, :rank] = high
        back[here, rank:] = rest
        value = nt(grad, full_in[:, those]) + nt(low[here, :], a2[...])
        dense[here, :] = dense[here, :] + value if n_part > 1 else value

    def prepare():
        for e in range(1, n_chip):
            firsts[e - 1].wait_recv()
            a_core.append(begin(
                first_part(e), first_part(e), first_core_sem.at[0, e], first_core_sem.at[1, e],
                sibling,
            ))
        for copy in own:
            copy.wait()
        for copy in a_core:
            copy.wait_recv()
        half = (ADAPTER_SCALE * second[...].astype(F32)).astype(BF16)
        second2[:rank, :] = half
        second2[rank:, :] = half
        half = (ADAPTER_SCALE * first[...].astype(F32)).astype(BF16)
        first2[:, :rank] = half
        first2[:, rank:] = half
        half = (ADAPTER_SCALE * full_a[...].astype(F32)).astype(BF16)
        a2[:, :rank] = half
        a2[:, rank:] = half

    share = -(-len(rest) // (n_tok - 1))
    for j in range(1, n_tok):
        arrive(j)
        for piece in rest[(j - 1) * share:j * share]:
            send_weight(*piece)
        if j >= 2:
            pass_on(j - 2)
            complete(j - 2)
        if j == n_tok - 1:
            prepare()
        if j >= 3:
            ranks(sources[j - 3])
    for j in range(max(n_tok - 2, 0), n_tok):
        if j < n_tok - 1:
            pass_on(j)
            complete(j)
        ranks(sources[j - 1])

    def wait_weights(p):
        for d in range(1, n_tok):
            for k in range(2):
                weights[d, p, k].wait_recv()

    def oa_blocks(source, p):
        at = pl.multiple_of(source * width + p * part_width, part_width)
        oa_at, ib_at = oa_all.at[pl.ds(at, part_width), :], ib_all.at[:, pl.ds(at, part_width)]
        return [(oa_at, oa_at), (ib_at, ib_at)]

    def oa_along(j, p, act):
        along(
            sources[j], oa_blocks(sources[j], p),
            lambda way, source, k: grad_send.at[way, source, p, k],
            lambda source, k: grad_recv.at[source, p, k], act,
        )

    def finish_grads(p):
        at = pl.multiple_of(t * width + p * part_width, part_width)
        oa = oa_acc[p]
        oa_all[pl.ds(at, part_width), :] = (scale * (oa[:, :rank] + oa[:, rank:])).astype(BF16)
        ib = ib_acc[p]
        ib_all[:, pl.ds(at, part_width)] = (scale * (ib[:rank] + ib[rank:])).astype(BF16)
        oa_along(0, p, start)

    def relay_grads(j, p):
        for k, (block, target) in enumerate(oa_blocks(sources[j], p)):
            remote(
                target, target, grad_send.at[0, sources[j], p, k], grad_recv.at[sources[j], p, k],
                sibling,
            ).wait_recv()
        oa_along(j, p, start)

    wait_weights(0)
    if n_part > 1:
        for j in range(n_tok - 1):
            hidden(0, sources[j], j > 0)
    pass_on(n_tok - 1)
    complete(n_tok - 1)
    ranks(sources[n_tok - 1])
    if n_part > 1:
        hidden(0, sources[n_tok - 1], True)
        finish_grads(0)
    for p in range(1, n_part - 1):
        wait_weights(p)
        for j in range(n_tok):
            hidden(p, sources[j], j > 0)
        finish_grads(p)
    last = n_part - 1
    if last > 0:
        wait_weights(last)

    at_x, at_y = chip % 2, chip // 2
    square = [
        2 * ((at_y + e // 2) % 2) + (at_x + e % 2) % 2 for e in range(n_chip)
    ]
    core_copies, first_copies, second_copies, tok_copies = {}, {}, {}, []
    blocks = [sources[n_tok - 1 - q] for q in range(n_tok)]

    def columns(e, parity):
        return pl.ds(pl.multiple_of((2 * square[e] + parity) * cols, cols), cols)

    def here(q):
        return pl.ds(row_at(blocks[q]), rows)

    def buffers(q):
        if q == n_tok:
            return core_t, kept_t, pend_t, one_send_t, one_recv_t, two_send_t, two_recv_t
        return tuple(
            array.at[q] for array in (core_d, kept_d, pend_d, one_send, one_recv, two_send, two_recv)
        )

    def to_sibling(q):
        got = buffers(q)[0]
        core_copies[q] = []
        for e in range(n_chip):
            those = columns(e, 1 - core)
            source = terms.at[:, those] if q == n_tok else dense.at[here(q), those]
            core_copies[q].append(
                begin(source, got.at[e], core_r_sem.at[0, q, e], core_r_sem.at[1, q, e], sibling)
            )

    def over_core(q):
        got, kept, pend, sent, recv = buffers(q)[:5]
        half = kept.shape[0] // 2
        first_copies[q] = []
        for e in (3, 1, 2, 0):
            core_copies[q][e].wait_recv()
            those = columns(e, core)
            mine = terms[:, those] if q == n_tok else dense[here(q), those]
            value = mine + got[e]
            for i in range(2):
                some = value[i * half:(i + 1) * half]
                if e == 0:
                    kept[i * half:(i + 1) * half, :] = some
                elif e == 2 - i:
                    pend[i] = some
                else:
                    sent[i, 0 if e == 1 + i else 1] = some.astype(BF16)
        for i in range(2):
            first_copies[q].append(begin(
                sent.at[i], recv.at[i], one_sem.at[0, q, i], one_sem.at[1, q, i],
                (t, 2 * square[1 + i] + core),
            ))

    def over_first(q):
        _, kept, pend, _, recv, sent, second_recv = buffers(q)
        half = kept.shape[0] // 2
        second_copies[q] = []
        for i in range(2):
            first_copies[q][i].wait_recv()
            sent[i] = (pend[i] + recv[i, 1].astype(F32)).astype(BF16)
            second_copies[q].append(begin(
                sent.at[i], second_recv.at[i], two_sem.at[0, q, i], two_sem.at[1, q, i],
                (t, 2 * square[2 - i] + core),
            ))
            some = slice(i * half, (i + 1) * half)
            kept[some, :] = kept[some, :] + recv[i, 0].astype(F32)

    def over_second(q):
        _, kept, _, _, _, _, recv = buffers(q)
        half = kept.shape[0] // 2
        for i in range(2):
            second_copies[q][i].wait_recv()
            some = slice(i * half, (i + 1) * half)
            kept[some, :] = kept[some, :] + recv[i].astype(F32)

    def line_copy(q, way):
        where = (t + 1 - 2 * way, h)
        return remote(
            line_send.at[min(q, n_tok - 2)], line_recv.at[way, blocks[q]],
            line_sem.at[way, min(q, n_tok - 2)], line_got.at[way, blocks[q]], where,
        )

    def from_line(q, way):
        line_copy(q, way).wait_recv()
        kept_d[q] = kept_d[q] + line_recv[way, blocks[q]].astype(F32)

    def over_line(q):
        target = blocks[q]
        pl.when((target >= t) & (t > 0))(lambda: from_line(q, 0))
        pl.when((target <= t) & (t + 1 < n_tok))(lambda: from_line(q, 1))
        if q == n_tok - 1:
            return
        line_send[q] = kept_d[q].astype(BF16)
        pl.when(target > t)(lambda: line_copy(q, 0).start())
        pl.when(target < t)(lambda: line_copy(q, 1).start())

    def share_terms():
        all_t[t] = kept_t[...].astype(BF16)
        for k in range(1, n_tok):
            tok_copies.append(begin(
                all_t.at[t], all_t.at[t], term_sem.at[0, k - 1], term_sem.at[1, k - 1], toks[k]
            ))

    def sum_terms():
        out_cols = x.shape[1] // n_chip
        for at in range(0, x.shape[1], out_cols):
            those = slice(at, at + out_cols)
            value = tn(back[...], c[:, those])
            terms[:rank, those] = scale * (value[:rank] + value[rank:])
            value = tn(low[...], x[:, those])
            terms[rank:, those] = scale * (value[:rank] + value[rank:])

    def relay_all(j):
        for p in range(last):
            relay_grads(j, p)

    final = n_tok - 1
    for q in range(n_tok):
        hidden(last, blocks[q], q > 0)
        to_sibling(q)
        if q >= 1:
            over_core(q - 1)
        if q >= 2:
            relay_all(q - 1)
        if q >= 3:
            over_first(q - 3)
    finish_grads(last)
    over_first(final - 2)
    sum_terms()
    to_sibling(n_tok)
    for j in range(max(n_tok - 1, 1), n_tok):
        relay_all(j)
    for q in range(final - 2):
        over_second(q)
        over_line(q)
    over_first(final - 1)
    over_core(n_tok)
    over_second(final - 2)
    over_line(final - 2)
    over_core(final)
    relay_grads(1, last)
    over_first(n_tok)
    over_second(final - 1)
    over_line(final - 1)
    over_first(final)
    over_second(n_tok)
    share_terms()
    relay_grads(2, last)
    over_second(final)
    for j in range(3, n_tok):
        relay_grads(j, last)
    over_line(final)
    dx_out[...] = kept_d[final]
    for copy in tok_copies:
        copy.wait_recv()
    value = all_t[0].astype(F32)
    for k in range(1, n_tok):
        value = value + all_t[k].astype(F32)
    terms_out[...] = value
    for q in range(final):
        pl.when(blocks[q] > t)(lambda: line_copy(q, 0).wait_send())
        pl.when(blocks[q] < t)(lambda: line_copy(q, 1).wait_send())
    for j in range(n_tok):
        act_along(j, wait_send)
        for p in range(n_part):
            oa_along(j, p, wait_send)
    for groups in (from_chip, from_core, core_copies, first_copies, second_copies):
        for group in groups.values():
            for copy in group:
                copy.wait_send()
    for copy in firsts + a_core + list(weights.values()) + tok_copies:
        copy.wait_send()


def fused(n_part, scale, tokens, cotangent, frozen_in, frozen_out, in_a, in_b, out_a, out_b):
    n_tok, n_hid = lax.axis_size("tok"), lax.axis_size("hid")
    n_chip = n_hid // 2
    rows, cols = tokens.shape
    count, features = rows * n_tok, cols * n_hid
    width = frozen_in.shape[1] // n_tok
    part_width = width // n_part
    rank = in_a.shape[1]
    sems = pltpu.SemaphoreType.DMA
    vmem = pl.BlockSpec(memory_space=pltpu.VMEM)
    whole = pl.BlockSpec(memory_space=pl.ANY)
    return pl.pallas_call(
        functools.partial(fused_kernel, n_tok, n_hid, n_part, scale),
        out_shape=(
            jax.ShapeDtypeStruct((rows, cols), F32),
            jax.ShapeDtypeStruct((2 * rank, cols), F32),
            jax.ShapeDtypeStruct((n_tok * width, rank), BF16),
            jax.ShapeDtypeStruct((rank, n_tok * width), BF16),
        ),
        in_specs=[whole] * 8,
        out_specs=(vmem,) * 4,
        scratch_shapes=[
            pltpu.VMEM((count, features), BF16),
            pltpu.VMEM((count, features), BF16),
            pltpu.VMEM((features, width), BF16),
            pltpu.VMEM((width, features), BF16),
            pltpu.VMEM((features, rank), BF16),
            pltpu.VMEM((rank, features), BF16),
            pltpu.VMEM((rank, width), BF16),
            pltpu.VMEM((width, rank), BF16),
            pltpu.VMEM((2 * rank, width), BF16),
            pltpu.VMEM((width, 2 * rank), BF16),
            pltpu.VMEM((features, 2 * rank), BF16),
            pltpu.VMEM((count, 2 * rank), BF16),
            pltpu.VMEM((count, 2 * rank), BF16),
            pltpu.VMEM((rows, part_width), F32),
            pltpu.VMEM((rows, part_width), F32),
            pltpu.VMEM((rows, part_width), BF16),
            pltpu.VMEM((rows, part_width), BF16),
            pltpu.VMEM((count, features), F32),
            pltpu.VMEM((count, rank), F32),
            pltpu.VMEM((count, rank), F32),
            pltpu.VMEM((n_part, part_width, 2 * rank), F32),
            pltpu.VMEM((n_part, 2 * rank, part_width), F32),
            pltpu.VMEM((2 * rank, features), F32),
            pltpu.VMEM((n_tok, n_chip, rows, cols), F32),
            pltpu.VMEM((n_chip, 2 * rank, cols), F32),
            pltpu.VMEM((n_tok, rows, cols), F32),
            pltpu.VMEM((2 * rank, cols), F32),
            pltpu.VMEM((n_tok, 2, rows // 2, cols), F32),
            pltpu.VMEM((2, rank, cols), F32),
            pltpu.VMEM((n_tok, 2, 2, rows // 2, cols), BF16),
            pltpu.VMEM((2, 2, rank, cols), BF16),
            pltpu.VMEM((n_tok, 2, 2, rows // 2, cols), BF16),
            pltpu.VMEM((2, 2, rank, cols), BF16),
            pltpu.VMEM((n_tok, 2, rows // 2, cols), BF16),
            pltpu.VMEM((2, rank, cols), BF16),
            pltpu.VMEM((n_tok, 2, rows // 2, cols), BF16),
            pltpu.VMEM((2, rank, cols), BF16),
            pltpu.VMEM((n_tok - 1, rows, cols), BF16),
            pltpu.VMEM((2, n_tok, rows, cols), BF16),
            pltpu.VMEM((n_tok, 2 * rank, cols), BF16),
            sems((2, n_tok, 2)),
            sems((n_tok, 2)),
            sems((2, n_tok, n_chip - 1, 2)),
            sems((2, n_tok, n_chip, 2)),
            sems((2, n_chip - 1)),
            sems((2, n_chip)),
            sems((2, n_tok - 1, n_part, 2)),
            sems((6 + 2 * n_part,)),
            sems((2, n_tok + 1, n_chip)),
            sems((2, n_tok + 1, 2)),
            sems((2, n_tok + 1, 2)),
            sems((2, n_tok - 1)),
            sems((2, n_tok)),
            sems((2, n_tok - 1)),
            sems((2, n_tok, n_part, 2)),
            sems((n_tok, n_part, 2)),
        ],
        compiler_params=pltpu.CompilerParams(
            collective_id=1, has_side_effects=True, vmem_limit_bytes=60 * 1024 * 1024
        ),
    )(tokens, cotangent, frozen_in, frozen_out, in_a, in_b, out_a, out_b)


def finish_kernel(dx, terms, oa, ib, dx_out, in_a_out, ib_out, oa_out, out_b_out):
    rank = in_a_out.shape[1]
    ib_out[...] = ib[...].astype(F32)
    oa_out[...] = oa[...].astype(F32)
    dx_out[...] = dx[...]
    in_a_out[...] = terms[rank:, :].T
    out_b_out[...] = terms[:rank, :]


def local(tokens, cotangent, frozen_in, frozen_out, in_a, in_b, out_a, out_b):
    count = tokens.shape[0] * lax.axis_size("tok")
    scale = ADAPTER_SCALE / math.sqrt(count)
    dx, terms, oa, ib = fused(
        2, scale, tokens, cotangent, frozen_in, frozen_out, in_a, in_b, out_a, out_b
    )
    rank, cols = in_a.shape[1], tokens.shape[1]
    vmem = pl.BlockSpec(memory_space=pltpu.VMEM)
    return pl.pallas_call(
        finish_kernel,
        out_shape=(
            jax.ShapeDtypeStruct(dx.shape, F32),
            jax.ShapeDtypeStruct((cols, rank), F32),
            jax.ShapeDtypeStruct(ib.shape, F32),
            jax.ShapeDtypeStruct(oa.shape, F32),
            jax.ShapeDtypeStruct((rank, cols), F32),
        ),
        in_specs=[vmem] * 4,
        out_specs=(vmem,) * 5,
        compiler_params=pltpu.CompilerParams(vmem_limit_bytes=60 * 1024 * 1024),
    )(dx, terms, oa, ib)


def local_by_rows(
    tokens,
    cotangent,
    frozen_in,
    frozen_out,
    input_adapter_first,
    input_adapter_second,
    adapter_out_a,
    adapter_out_b,
):
    highest_precision = lax.Precision.HIGHEST
    device_local_rows = tokens.shape[0]
    rank_width = input_adapter_second.shape[0]
    gradient_scale = ADAPTER_SCALE / math.sqrt(device_local_rows * lax.axis_size("tok"))
    full_tokens, full_cotan = (
        lax.all_gather(tokens, "hid", axis=1, tiled=True),
        lax.all_gather(cotangent, "hid", axis=1, tiled=True),
    )
    in_rows = lax.all_gather(frozen_in, "tok", axis=0, tiled=True)
    in_a_full = lax.all_gather(input_adapter_first, "hid", axis=0, tiled=True)
    lowrank_input = jnp.dot(full_tokens, in_a_full, preferred_element_type=jnp.float32)
    second_float = input_adapter_second.astype(jnp.float32)
    out_a_float = adapter_out_a.astype(jnp.float32)
    pre_activation = jnp.dot(
        full_tokens, in_rows, preferred_element_type=jnp.float32
    ) + ADAPTER_SCALE * jnp.dot(lowrank_input, second_float, precision=highest_precision)
    value_out, slopes = gelu_pair(pre_activation)
    hidden_act = value_out.astype(jnp.bfloat16)
    backward_lowrank = jnp.einsum(
        "td,rd->tr", full_cotan, adapter_out_b, preferred_element_type=jnp.float32
    )
    rank_out = jnp.dot(hidden_act, adapter_out_a, preferred_element_type=jnp.float32)
    dense_backward = jnp.einsum(
        "td,fd->tf",
        full_cotan,
        lax.all_gather(frozen_out, "tok", axis=1, tiled=True),
        preferred_element_type=jnp.float32,
    )
    dense_backward = dense_backward + ADAPTER_SCALE * jnp.dot(
        backward_lowrank, out_a_float.T, precision=highest_precision
    )
    grad_pre = (dense_backward * slopes).astype(jnp.bfloat16)
    rank_backward = jnp.einsum(
        "tf,rf->tr", grad_pre, input_adapter_second, preferred_element_type=jnp.float32
    )
    dense_in = jnp.einsum("tf,df->td", grad_pre, in_rows, preferred_element_type=jnp.float32)
    grad_out_a = gradient_scale * jnp.dot(
        hidden_act.astype(jnp.float32).T, backward_lowrank, precision=highest_precision
    )
    grad_in_b = gradient_scale * jnp.dot(
        lowrank_input.T, grad_pre.astype(jnp.float32), precision=highest_precision
    )
    in_a_float = in_a_full.astype(jnp.float32)
    dx_term = dense_in + ADAPTER_SCALE * jnp.dot(
        rank_backward, in_a_float.T, precision=highest_precision
    )
    out_term = jnp.dot(rank_out.T, full_cotan.astype(jnp.float32), precision=highest_precision)
    in_term = jnp.dot(rank_backward.T, full_tokens.astype(jnp.float32), precision=highest_precision)
    rank_terms = jnp.concatenate([out_term, in_term], axis=0)
    input_gradient, rank_local = (
        lax.psum_scatter(dx_term, "hid", scatter_dimension=1, tiled=True),
        lax.psum_scatter(rank_terms, "hid", scatter_dimension=1, tiled=True),
    )
    grad_out_a, grad_in_b, rank_total = lax.psum((grad_out_a, grad_in_b, rank_local), "tok")
    grad_out_b = gradient_scale * rank_total[:rank_width]
    grad_in_a = gradient_scale * rank_total[rank_width:].T
    return (input_gradient, grad_in_a, grad_in_b, grad_out_a, grad_out_b)


def solution(mesh):
    in_specs = (
        P("tok", "hid"),
        P("tok", "hid"),
        P("tok", "hid"),
        P("hid", "tok"),
        P("hid", None),
        P(None, "hid"),
        P("hid", None),
        P(),
    )
    out_specs = (P("tok", "hid"), P("hid", None), P(None, "hid"), P("hid", None), P(None, "hid"))
    def body(*arrays):
        share = arrays[2].shape[1] // lax.axis_size("tok")
        wide = share % 256 == 0 and lax.axis_size("tok") > 2
        wide = wide and lax.axis_size("hid") == 2 ** len(("y", "x", "core"))
        return local(*arrays) if wide else local_by_rows(*arrays)

    return jax.shard_map(body, mesh=mesh, in_specs=in_specs, out_specs=out_specs, check_vma=False)
```

```python
import functools
import math

import jax
import jax.numpy as jnp
from jax import lax
from jax.experimental import pallas as pl
from jax.experimental.pallas import tpu as pltpu
from jax.sharding import PartitionSpec as P

ADAPTER_SCALE = 0.5
GELU_K = 0.7978845608
GELU_C = 0.044715
F32 = jnp.float32
BF16 = jnp.bfloat16


def gelu_pair(pre_activation):
    tangent = jnp.tanh(
        GELU_K * (pre_activation + GELU_C * pre_activation * pre_activation * pre_activation)
    )
    value_out = 0.5 * pre_activation * (1.0 + tangent)
    slopes = 0.5 * (1.0 + tangent) + 0.5 * pre_activation * (1.0 - tangent * tangent) * GELU_K * (
        1.0 + 3.0 * GELU_C * pre_activation * pre_activation
    )
    return (value_out, slopes)


def dot(left, right, dims):
    return lax.dot_general(left, right, (dims, ((), ())), preferred_element_type=F32)


def nn(left, right):
    return dot(left, right, ((1,), (0,)))


def nt(left, right):
    return dot(left, right, ((1,), (1,)))


def tn(left, right):
    return dot(left, right, ((0,), (0,)))


def split(value):
    high = value.astype(BF16)
    return high, (value - high.astype(F32)).astype(BF16)


def fused_kernel(
    n_tok, n_hid, n_part, scale,
    tokens, cotangent, w_in, w_out, in_a, in_b, out_a, out_b,
    dx_out, terms_out, oa_all, ib_all,
    x, c, full_in, full_out, full_a, b_mat, second, first, second2, first2, a2,
    low, back, pre_s, back_s, act_s, grad_s, dense, rank_out, rank_back, oa_acc, ib_acc, terms,
    core_d, core_t, kept_d, kept_t, pend_d, pend_t, one_send, one_send_t, one_recv, one_recv_t,
    two_send, two_send_t, two_recv, two_recv_t, line_send, line_recv, all_t,
    act_send, act_recv, chip_sem, core_sem, first_sem, first_core_sem, w_sem, own_sem,
    core_r_sem, one_sem, two_sem, line_sem, line_got, term_sem, grad_send, grad_recv,
):
    t, h = lax.axis_index("tok"), lax.axis_index("hid")
    n_chip = n_hid // 2
    chip, core = h // 2, h % 2
    rows, cols = tokens.shape
    depth = w_in.shape[0]
    width = full_in.shape[1]
    part_width = width // n_part
    rank = full_a.shape[1]

    def remote(source, target, send, recv, where):
        return pltpu.make_async_remote_copy(
            src_ref=source, dst_ref=target, send_sem=send, recv_sem=recv,
            device_id=where, device_id_type=pl.DeviceIdType.MESH,
        )

    def begin(*arguments):
        copy = remote(*arguments)
        copy.start()
        return copy

    sibling = (t, 2 * chip + 1 - core)
    chips = [(t, 2 * ((chip + e) % n_chip) + core) for e in range(n_chip)]
    toks = [((t + d) % n_tok, h) for d in range(n_tok)]
    barrier = pltpu.get_barrier_semaphore()
    for where in [sibling] + chips[1:] + toks[1:]:
        pl.semaphore_signal(barrier, inc=1, device_id=where, device_id_type=pl.DeviceIdType.MESH)
    pl.semaphore_wait(barrier, n_chip + n_tok - 1)

    orders = [sorted(range(n_tok), key=lambda s: (abs(s - k), s)) for k in range(n_tok)]
    sources = [t]
    for j in range(1, n_tok):
        source = jnp.int32(orders[0][j])
        for k in range(1, n_tok):
            source = jnp.where(t == k, jnp.int32(orders[k][j]), source)
        sources.append(source)

    def row_at(source):
        return pl.multiple_of(source * rows, rows)

    def part(array, source, e):
        at_col = pl.multiple_of((2 * ((chip + n_chip - e) % n_chip) + core) * cols, cols)
        return array.at[pl.ds(row_at(source), rows), pl.ds(at_col, cols)]

    def along(source, blocks, send, recv, act):
        @pl.when((source <= t) & (t + 1 < n_tok))
        def _():
            for k, (block, target) in enumerate(blocks):
                act(remote(block, target, send(0, source, k), recv(source, k), (t + 1, h)))

        @pl.when((source >= t) & (t > 0))
        def _():
            for k, (block, target) in enumerate(blocks):
                act(remote(block, target, send(1, source, k), recv(source, k), (t - 1, h)))

    def start(copy):
        copy.start()

    def wait_send(copy):
        copy.wait_send()

    def act_blocks(j):
        source = sources[j]
        mine = (tokens, cotangent)
        return [
            (mine[k] if j == 0 else part(array, source, 0), part(array, source, 0))
            for k, array in enumerate((x, c))
        ]

    def act_along(j, act):
        along(
            sources[j], act_blocks(j),
            lambda way, source, k: act_send.at[way, source, k],
            lambda source, k: act_recv.at[source, k], act,
        )

    from_chip, from_core = {}, {}

    def to_chips(j):
        for e in range(1, n_chip):
            from_chip[j, e] = [
                begin(block, target, chip_sem.at[0, j, e - 1, k], chip_sem.at[1, j, e - 1, k], chips[e])
                for k, (block, target) in enumerate(act_blocks(j))
            ]

    def to_core(j, e):
        if e == 0:
            blocks = act_blocks(j)
        else:
            blocks = [(part(array, sources[j], e),) * 2 for array in (x, c)]
        from_core[j, e] = [
            begin(block, target, core_sem.at[0, j, e, k], core_sem.at[1, j, e, k], sibling)
            for k, (block, target) in enumerate(blocks)
        ]

    def first_part(e):
        at = pl.multiple_of((2 * ((chip + n_chip - e) % n_chip) + core) * cols, cols)
        return full_a.at[pl.ds(at, cols), :]

    weights = {}
    depths = pl.ds(pl.multiple_of(t * depth, depth), depth)

    def weight_blocks(d, p):
        at = pl.multiple_of(((t + d) % n_tok) * width + p * part_width, part_width)
        here = pl.ds(p * part_width, part_width)
        return [
            (w_in.at[:, pl.ds(at, part_width)], full_in.at[depths, here]),
            (w_out.at[pl.ds(at, part_width), :], full_out.at[here, depths]),
        ]

    def send_weight(d, p, k):
        block, target = weight_blocks(d, p)[k]
        weights[d, p, k] = begin(
            block, target, w_sem.at[0, d - 1, p, k], w_sem.at[1, d - 1, p, k], toks[d]
        )

    act_along(0, start)
    to_chips(0)
    firsts = [
        begin(in_a, first_part(0), first_sem.at[0, e - 1], first_sem.at[1, e - 1], chips[e])
        for e in range(1, n_chip)
    ]
    to_core(0, 0)
    a_core = [begin(in_a, first_part(0), first_core_sem.at[0, 0], first_core_sem.at[1, 0], sibling)]
    pieces = [(d, p, k) for p in range(n_part) for k in range(2) for d in range(1, n_tok)]
    pieces = [piece for piece in pieces if piece[1:] != (0, 0) or piece[0] in (1, n_tok - 1)]
    rest = [(d, 0, 0) for d in range(2, n_tok - 1)] + pieces[min(2, n_tok - 1):]
    for piece in pieces[:min(2, n_tok - 1)]:
        send_weight(*piece)
    at = pl.multiple_of(t * width, width)
    own = [(block, target) for block, target in act_blocks(0)]
    own += [(in_a, first_part(0)), (out_b, b_mat)]
    own += [(in_b.at[:, pl.ds(at, width)], second), (out_a.at[pl.ds(at, width), :], first)]
    for p in range(n_part):
        own += weight_blocks(0, p)
    own = [
        pltpu.make_async_copy(block, target, own_sem.at[k])
        for k, (block, target) in enumerate(own)
    ]
    for copy in own:
        copy.start()

    def arrive(j):
        for k, (block, target) in enumerate(act_blocks(j)):
            remote(
                target, target, act_send.at[0, sources[j], k], act_recv.at[sources[j], k], sibling
            ).wait_recv()
        act_along(j, start)
        to_chips(j)
        to_core(j, 0)

    def pass_on(j):
        for e in range(1, n_chip):
            for copy in from_chip[j, e]:
                copy.wait_recv()
            to_core(j, e)

    def complete(j):
        for e in range(n_chip):
            for copy in from_core[j, e]:
                copy.wait_recv()

    def ranks(source):
        here = pl.ds(row_at(source), rows)
        high, rest = split(nn(x[here, :], full_a[...]))
        low[here, :rank] = high
        low[here, rank:] = rest
        high, rest = split(nt(c[here, :], b_mat[...]))
        back[here, :rank] = high
        back[here, rank:] = rest

    def hidden(p, source, begun):
        here = pl.ds(row_at(source), rows)
        those = slice(p * part_width, (p + 1) * part_width)
        pre_s[...] = nn(x[here, :], full_in[:, those]) + nn(low[here, :], second2[:, those])
        back_s[...] = nt(c[here, :], full_out[those, :]) + nt(back[here, :], first2[those, :])
        step = rows // 8
        for at in range(0, rows, step):
            some = slice(at, at + step)
            value_out, slopes = gelu_pair(pre_s[some, :])
            act_s[some, :] = value_out.astype(BF16)
            grad_s[some, :] = (back_s[some, :] * slopes).astype(BF16)
        act, grad = act_s[...], grad_s[...]
        oa_new, ib_new = tn(act, back[here, :]), tn(low[here, :], grad)
        out_new, back_new = nn(act, first[those, :]), nt(grad, second[:, those])
        if begun:
            oa_acc[p] += oa_new
            ib_acc[p] += ib_new
        else:
            oa_acc[p] = oa_new
            ib_acc[p] = ib_new
        if p == 0:
            rank_out[here, :] = out_new
            rank_back[here, :] = back_new
        else:
            rank_out[here, :] += out_new
            rank_back[here, :] += back_new
        if p < n_part - 1:
            if p == 0:
                dense[here, :] = nt(grad, full_in[:, those])
            else:
                dense[here, :] += nt(grad, full_in[:, those])
            return
        high, rest = split(rank_back[here, :])
        low[here, :rank] = high
        low[here, rank:] = rest
        high, rest = split(rank_out[here, :])
        back[here, :rank] = high
        back[here, rank:] = rest
        value = nt(grad, full_in[:, those]) + nt(low[here, :], a2[...])
        dense[here, :] = dense[here, :] + value if n_part > 1 else value

    def prepare():
        for e in range(1, n_chip):
            firsts[e - 1].wait_recv()
            a_core.append(begin(
                first_part(e), first_part(e), first_core_sem.at[0, e], first_core_sem.at[1, e],
                sibling,
            ))
        for copy in own:
            copy.wait()
        for copy in a_core:
            copy.wait_recv()
        half = (ADAPTER_SCALE * second[...].astype(F32)).astype(BF16)
        second2[:rank, :] = half
        second2[rank:, :] = half
        half = (ADAPTER_SCALE * first[...].astype(F32)).astype(BF16)
        first2[:, :rank] = half
        first2[:, rank:] = half
        half = (ADAPTER_SCALE * full_a[...].astype(F32)).astype(BF16)
        a2[:, :rank] = half
        a2[:, rank:] = half

    early = len(pieces) // 3
    for j in range(1, n_tok):
        arrive(j)
        for piece in {2: rest[:early], n_tok - 1: rest[early:]}.get(j, []):
            send_weight(*piece)
        if j >= 2:
            pass_on(j - 2)
            complete(j - 2)
        if j == n_tok - 1:
            prepare()
        if j >= 3:
            ranks(sources[j - 3])
    for j in range(max(n_tok - 2, 0), n_tok):
        if j < n_tok - 1:
            pass_on(j)
            complete(j)
        ranks(sources[j - 1])

    def wait_weights(p):
        for d in range(1, n_tok):
            for k in range(2):
                weights[d, p, k].wait_recv()

    def oa_blocks(source, p):
        at = pl.multiple_of(source * width + p * part_width, part_width)
        oa_at, ib_at = oa_all.at[pl.ds(at, part_width), :], ib_all.at[:, pl.ds(at, part_width)]
        return [(oa_at, oa_at), (ib_at, ib_at)]

    def grads_along(source, p, act):
        along(
            source, oa_blocks(source, p),
            lambda way, source, k: grad_send.at[way, source, p, k],
            lambda source, k: grad_recv.at[source, p, k], act,
        )

    def finish_grads(p):
        at = pl.multiple_of(t * width + p * part_width, part_width)
        oa = oa_acc[p]
        oa_all[pl.ds(at, part_width), :] = (scale * (oa[:, :rank] + oa[:, rank:])).astype(BF16)
        ib = ib_acc[p]
        ib_all[:, pl.ds(at, part_width)] = (scale * (ib[:rank] + ib[rank:])).astype(BF16)
        grads_along(t, p, start)

    def grad_hop(s, p):
        def relay(source):
            blocks = oa_blocks(source, p)
            for k, (block, target) in enumerate(blocks):
                remote(
                    target, target, grad_send.at[0, source, p, k], grad_recv.at[source, p, k],
                    sibling,
                ).wait_recv()
            grads_along(source, p, start)

        pl.when(t >= s + 1)(lambda: relay(t - 1 - s))
        pl.when(t + 1 + s < n_tok)(lambda: relay(t + 1 + s))

    wait_weights(0)
    if n_part > 1:
        for j in range(n_tok - 1):
            hidden(0, sources[j], j > 0)
    pass_on(n_tok - 1)
    complete(n_tok - 1)
    ranks(sources[n_tok - 1])
    if n_part > 1:
        hidden(0, sources[n_tok - 1], True)
        finish_grads(0)
    for p in range(1, n_part - 1):
        wait_weights(p)
        for j in range(n_tok):
            hidden(p, sources[j], j > 0)
        finish_grads(p)
    last = n_part - 1
    if last > 0:
        wait_weights(last)

    at_x, at_y = chip % 2, chip // 2
    square = [
        2 * ((at_y + e // 2) % 2) + (at_x + e % 2) % 2 for e in range(n_chip)
    ]
    core_copies, first_copies, second_copies, tok_copies = {}, {}, {}, []
    blocks = [sources[n_tok - 1 - q] for q in range(n_tok)]

    def columns(e, parity):
        return pl.ds(pl.multiple_of((2 * square[e] + parity) * cols, cols), cols)

    def here(q):
        return pl.ds(row_at(blocks[q]), rows)

    def buffers(q):
        if q == n_tok:
            return core_t, kept_t, pend_t, one_send_t, one_recv_t, two_send_t, two_recv_t
        return tuple(
            array.at[q] for array in (core_d, kept_d, pend_d, one_send, one_recv, two_send, two_recv)
        )

    def to_sibling(q):
        got = buffers(q)[0]
        core_copies[q] = []
        for e in range(n_chip):
            those = columns(e, 1 - core)
            source = terms.at[:, those] if q == n_tok else dense.at[here(q), those]
            core_copies[q].append(
                begin(source, got.at[e], core_r_sem.at[0, q, e], core_r_sem.at[1, q, e], sibling)
            )

    def over_core(q):
        got, kept, pend, sent, recv = buffers(q)[:5]
        half = kept.shape[0] // 2
        first_copies[q] = []
        for e in (3, 1, 2, 0):
            core_copies[q][e].wait_recv()
            those = columns(e, core)
            mine = terms[:, those] if q == n_tok else dense[here(q), those]
            value = mine + got[e]
            for i in range(2):
                some = value[i * half:(i + 1) * half]
                if e == 0:
                    kept[i * half:(i + 1) * half, :] = some
                elif e == 2 - i:
                    pend[i] = some
                else:
                    sent[i, 0 if e == 1 + i else 1] = some.astype(BF16)
        for i in range(2):
            first_copies[q].append(begin(
                sent.at[i], recv.at[i], one_sem.at[0, q, i], one_sem.at[1, q, i],
                (t, 2 * square[1 + i] + core),
            ))

    def over_first(q):
        _, kept, pend, _, recv, sent, second_recv = buffers(q)
        half = kept.shape[0] // 2
        second_copies[q] = []
        for i in range(2):
            first_copies[q][i].wait_recv()
            sent[i] = (pend[i] + recv[i, 1].astype(F32)).astype(BF16)
            second_copies[q].append(begin(
                sent.at[i], second_recv.at[i], two_sem.at[0, q, i], two_sem.at[1, q, i],
                (t, 2 * square[2 - i] + core),
            ))
            some = slice(i * half, (i + 1) * half)
            kept[some, :] = kept[some, :] + recv[i, 0].astype(F32)

    def over_second(q):
        _, kept, _, _, _, _, recv = buffers(q)
        half = kept.shape[0] // 2
        for i in range(2):
            second_copies[q][i].wait_recv()
            some = slice(i * half, (i + 1) * half)
            kept[some, :] = kept[some, :] + recv[i].astype(F32)

    def line_copy(q, way):
        where = (t + 1 - 2 * way, h)
        return remote(
            line_send.at[min(q, n_tok - 2)], line_recv.at[way, blocks[q]],
            line_sem.at[way, min(q, n_tok - 2)], line_got.at[way, blocks[q]], where,
        )

    def from_line(q, way):
        line_copy(q, way).wait_recv()
        kept_d[q] = kept_d[q] + line_recv[way, blocks[q]].astype(F32)

    def over_line(q):
        target = blocks[q]
        pl.when((target >= t) & (t > 0))(lambda: from_line(q, 0))
        pl.when((target <= t) & (t + 1 < n_tok))(lambda: from_line(q, 1))
        if q == n_tok - 1:
            return
        line_send[q] = kept_d[q].astype(BF16)
        pl.when(target > t)(lambda: line_copy(q, 0).start())
        pl.when(target < t)(lambda: line_copy(q, 1).start())

    def share_terms():
        all_t[t] = kept_t[...].astype(BF16)
        for k in range(1, n_tok):
            tok_copies.append(begin(
                all_t.at[t], all_t.at[t], term_sem.at[0, k - 1], term_sem.at[1, k - 1], toks[k]
            ))

    def sum_terms():
        out_cols = x.shape[1] // n_chip
        for at in range(0, x.shape[1], out_cols):
            those = slice(at, at + out_cols)
            value = tn(back[...], c[:, those])
            terms[:rank, those] = scale * (value[:rank] + value[rank:])
            value = tn(low[...], x[:, those])
            terms[rank:, those] = scale * (value[:rank] + value[rank:])

    def hop(s):
        for p in range(last):
            grad_hop(s, p)

    final = n_tok - 1
    for q in range(n_tok):
        hidden(last, blocks[q], q > 0)
        to_sibling(q)
        if q >= 1:
            over_core(q - 1)
        if q == 2:
            hop(0)
    finish_grads(last)
    for q in range(final - 1):
        over_first(q)
    sum_terms()
    to_sibling(n_tok)
    hop(1)
    over_core(n_tok)
    over_first(final - 1)
    over_core(final)
    for q in range(final - 1):
        over_second(q)
        over_line(q)
    grad_hop(0, last)
    over_first(n_tok)
    over_second(final - 1)
    over_line(final - 1)
    over_first(final)
    over_second(n_tok)
    share_terms()
    for s in range(2, n_tok - 1):
        hop(s)
    over_second(final)
    for s in range(1, n_tok - 1):
        grad_hop(s, last)
    over_line(final)
    dx_out[...] = kept_d[final]
    for copy in tok_copies:
        copy.wait_recv()
    value = all_t[0].astype(F32)
    for k in range(1, n_tok):
        value = value + all_t[k].astype(F32)
    terms_out[...] = value
    for q in range(final):
        pl.when(blocks[q] > t)(lambda: line_copy(q, 0).wait_send())
        pl.when(blocks[q] < t)(lambda: line_copy(q, 1).wait_send())
    for j in range(n_tok):
        act_along(j, wait_send)
        for p in range(n_part):
            grads_along(sources[j], p, wait_send)
    for groups in (from_chip, from_core, core_copies, first_copies, second_copies):
        for group in groups.values():
            for copy in group:
                copy.wait_send()
    for copy in firsts + a_core + list(weights.values()) + tok_copies:
        copy.wait_send()


def fused(n_part, scale, tokens, cotangent, frozen_in, frozen_out, in_a, in_b, out_a, out_b):
    n_tok, n_hid = lax.axis_size("tok"), lax.axis_size("hid")
    n_chip = n_hid // 2
    rows, cols = tokens.shape
    count, features = rows * n_tok, cols * n_hid
    width = frozen_in.shape[1] // n_tok
    part_width = width // n_part
    rank = in_a.shape[1]
    sems = pltpu.SemaphoreType.DMA
    vmem = pl.BlockSpec(memory_space=pltpu.VMEM)
    whole = pl.BlockSpec(memory_space=pl.ANY)
    return pl.pallas_call(
        functools.partial(fused_kernel, n_tok, n_hid, n_part, scale),
        out_shape=(
            jax.ShapeDtypeStruct((rows, cols), F32),
            jax.ShapeDtypeStruct((2 * rank, cols), F32),
            jax.ShapeDtypeStruct((n_tok * width, rank), BF16),
            jax.ShapeDtypeStruct((rank, n_tok * width), BF16),
        ),
        in_specs=[whole] * 8,
        out_specs=(vmem,) * 4,
        scratch_shapes=[
            pltpu.VMEM((count, features), BF16),
            pltpu.VMEM((count, features), BF16),
            pltpu.VMEM((features, width), BF16),
            pltpu.VMEM((width, features), BF16),
            pltpu.VMEM((features, rank), BF16),
            pltpu.VMEM((rank, features), BF16),
            pltpu.VMEM((rank, width), BF16),
            pltpu.VMEM((width, rank), BF16),
            pltpu.VMEM((2 * rank, width), BF16),
            pltpu.VMEM((width, 2 * rank), BF16),
            pltpu.VMEM((features, 2 * rank), BF16),
            pltpu.VMEM((count, 2 * rank), BF16),
            pltpu.VMEM((count, 2 * rank), BF16),
            pltpu.VMEM((rows, part_width), F32),
            pltpu.VMEM((rows, part_width), F32),
            pltpu.VMEM((rows, part_width), BF16),
            pltpu.VMEM((rows, part_width), BF16),
            pltpu.VMEM((count, features), F32),
            pltpu.VMEM((count, rank), F32),
            pltpu.VMEM((count, rank), F32),
            pltpu.VMEM((n_part, part_width, 2 * rank), F32),
            pltpu.VMEM((n_part, 2 * rank, part_width), F32),
            pltpu.VMEM((2 * rank, features), F32),
            pltpu.VMEM((n_tok, n_chip, rows, cols), F32),
            pltpu.VMEM((n_chip, 2 * rank, cols), F32),
            pltpu.VMEM((n_tok, rows, cols), F32),
            pltpu.VMEM((2 * rank, cols), F32),
            pltpu.VMEM((n_tok, 2, rows // 2, cols), F32),
            pltpu.VMEM((2, rank, cols), F32),
            pltpu.VMEM((n_tok, 2, 2, rows // 2, cols), BF16),
            pltpu.VMEM((2, 2, rank, cols), BF16),
            pltpu.VMEM((n_tok, 2, 2, rows // 2, cols), BF16),
            pltpu.VMEM((2, 2, rank, cols), BF16),
            pltpu.VMEM((n_tok, 2, rows // 2, cols), BF16),
            pltpu.VMEM((2, rank, cols), BF16),
            pltpu.VMEM((n_tok, 2, rows // 2, cols), BF16),
            pltpu.VMEM((2, rank, cols), BF16),
            pltpu.VMEM((n_tok - 1, rows, cols), BF16),
            pltpu.VMEM((2, n_tok, rows, cols), BF16),
            pltpu.VMEM((n_tok, 2 * rank, cols), BF16),
            sems((2, n_tok, 2)),
            sems((n_tok, 2)),
            sems((2, n_tok, n_chip - 1, 2)),
            sems((2, n_tok, n_chip, 2)),
            sems((2, n_chip - 1)),
            sems((2, n_chip)),
            sems((2, n_tok - 1, n_part, 2)),
            sems((6 + 2 * n_part,)),
            sems((2, n_tok + 1, n_chip)),
            sems((2, n_tok + 1, 2)),
            sems((2, n_tok + 1, 2)),
            sems((2, n_tok - 1)),
            sems((2, n_tok)),
            sems((2, n_tok - 1)),
            sems((2, n_tok, n_part, 2)),
            sems((n_tok, n_part, 2)),
        ],
        compiler_params=pltpu.CompilerParams(
            collective_id=1, has_side_effects=True, vmem_limit_bytes=60 * 1024 * 1024
        ),
    )(tokens, cotangent, frozen_in, frozen_out, in_a, in_b, out_a, out_b)


def finish_kernel(dx, terms, oa, ib, dx_out, in_a_out, ib_out, oa_out, out_b_out):
    rank = in_a_out.shape[1]
    ib_out[...] = ib[...].astype(F32)
    oa_out[...] = oa[...].astype(F32)
    dx_out[...] = dx[...]
    in_a_out[...] = terms[rank:, :].T
    out_b_out[...] = terms[:rank, :]


def local(tokens, cotangent, frozen_in, frozen_out, in_a, in_b, out_a, out_b):
    count = tokens.shape[0] * lax.axis_size("tok")
    scale = ADAPTER_SCALE / math.sqrt(count)
    dx, terms, oa, ib = fused(
        2, scale, tokens, cotangent, frozen_in, frozen_out, in_a, in_b, out_a, out_b
    )
    rank, cols = in_a.shape[1], tokens.shape[1]
    vmem = pl.BlockSpec(memory_space=pltpu.VMEM)
    return pl.pallas_call(
        finish_kernel,
        out_shape=(
            jax.ShapeDtypeStruct(dx.shape, F32),
            jax.ShapeDtypeStruct((cols, rank), F32),
            jax.ShapeDtypeStruct(ib.shape, F32),
            jax.ShapeDtypeStruct(oa.shape, F32),
            jax.ShapeDtypeStruct((rank, cols), F32),
        ),
        in_specs=[vmem] * 4,
        out_specs=(vmem,) * 5,
        compiler_params=pltpu.CompilerParams(vmem_limit_bytes=60 * 1024 * 1024),
    )(dx, terms, oa, ib)


def local_by_rows(
    tokens,
    cotangent,
    frozen_in,
    frozen_out,
    input_adapter_first,
    input_adapter_second,
    adapter_out_a,
    adapter_out_b,
):
    highest_precision = lax.Precision.HIGHEST
    device_local_rows = tokens.shape[0]
    rank_width = input_adapter_second.shape[0]
    gradient_scale = ADAPTER_SCALE / math.sqrt(device_local_rows * lax.axis_size("tok"))
    full_tokens, full_cotan = (
        lax.all_gather(tokens, "hid", axis=1, tiled=True),
        lax.all_gather(cotangent, "hid", axis=1, tiled=True),
    )
    in_rows = lax.all_gather(frozen_in, "tok", axis=0, tiled=True)
    in_a_full = lax.all_gather(input_adapter_first, "hid", axis=0, tiled=True)
    lowrank_input = jnp.dot(full_tokens, in_a_full, preferred_element_type=jnp.float32)
    second_float = input_adapter_second.astype(jnp.float32)
    out_a_float = adapter_out_a.astype(jnp.float32)
    pre_activation = jnp.dot(
        full_tokens, in_rows, preferred_element_type=jnp.float32
    ) + ADAPTER_SCALE * jnp.dot(lowrank_input, second_float, precision=highest_precision)
    value_out, slopes = gelu_pair(pre_activation)
    hidden_act = value_out.astype(jnp.bfloat16)
    backward_lowrank = jnp.einsum(
        "td,rd->tr", full_cotan, adapter_out_b, preferred_element_type=jnp.float32
    )
    rank_out = jnp.dot(hidden_act, adapter_out_a, preferred_element_type=jnp.float32)
    dense_backward = jnp.einsum(
        "td,fd->tf",
        full_cotan,
        lax.all_gather(frozen_out, "tok", axis=1, tiled=True),
        preferred_element_type=jnp.float32,
    )
    dense_backward = dense_backward + ADAPTER_SCALE * jnp.dot(
        backward_lowrank, out_a_float.T, precision=highest_precision
    )
    grad_pre = (dense_backward * slopes).astype(jnp.bfloat16)
    rank_backward = jnp.einsum(
        "tf,rf->tr", grad_pre, input_adapter_second, preferred_element_type=jnp.float32
    )
    dense_in = jnp.einsum("tf,df->td", grad_pre, in_rows, preferred_element_type=jnp.float32)
    grad_out_a = gradient_scale * jnp.dot(
        hidden_act.astype(jnp.float32).T, backward_lowrank, precision=highest_precision
    )
    grad_in_b = gradient_scale * jnp.dot(
        lowrank_input.T, grad_pre.astype(jnp.float32), precision=highest_precision
    )
    in_a_float = in_a_full.astype(jnp.float32)
    dx_term = dense_in + ADAPTER_SCALE * jnp.dot(
        rank_backward, in_a_float.T, precision=highest_precision
    )
    out_term = jnp.dot(rank_out.T, full_cotan.astype(jnp.float32), precision=highest_precision)
    in_term = jnp.dot(rank_backward.T, full_tokens.astype(jnp.float32), precision=highest_precision)
    rank_terms = jnp.concatenate([out_term, in_term], axis=0)
    input_gradient, rank_local = (
        lax.psum_scatter(dx_term, "hid", scatter_dimension=1, tiled=True),
        lax.psum_scatter(rank_terms, "hid", scatter_dimension=1, tiled=True),
    )
    grad_out_a, grad_in_b, rank_total = lax.psum((grad_out_a, grad_in_b, rank_local), "tok")
    grad_out_b = gradient_scale * rank_total[:rank_width]
    grad_in_a = gradient_scale * rank_total[rank_width:].T
    return (input_gradient, grad_in_a, grad_in_b, grad_out_a, grad_out_b)


def solution(mesh):
    in_specs = (
        P("tok", "hid"),
        P("tok", "hid"),
        P("tok", "hid"),
        P("hid", "tok"),
        P("hid", None),
        P(None, "hid"),
        P("hid", None),
        P(),
    )
    out_specs = (P("tok", "hid"), P("hid", None), P(None, "hid"), P("hid", None), P(None, "hid"))
    def body(*arrays):
        share = arrays[2].shape[1] // lax.axis_size("tok")
        wide = share % 256 == 0 and lax.axis_size("tok") > 2
        wide = wide and lax.axis_size("hid") == 2 ** len(("y", "x", "core"))
        return local(*arrays) if wide else local_by_rows(*arrays)

    return jax.shard_map(body, mesh=mesh, in_specs=in_specs, out_specs=out_specs, check_vma=False)
```

```python
import functools
import math

import jax
import jax.numpy as jnp
from jax import lax
from jax.experimental import pallas as pl
from jax.experimental.pallas import tpu as pltpu
from jax.sharding import PartitionSpec as P

ADAPTER_SCALE = 0.5
GELU_K = 0.7978845608
GELU_C = 0.044715
F32 = jnp.float32
BF16 = jnp.bfloat16


def gelu_pair(pre_activation):
    tangent = jnp.tanh(
        GELU_K * (pre_activation + GELU_C * pre_activation * pre_activation * pre_activation)
    )
    value_out = 0.5 * pre_activation * (1.0 + tangent)
    slopes = 0.5 * (1.0 + tangent) + 0.5 * pre_activation * (1.0 - tangent * tangent) * GELU_K * (
        1.0 + 3.0 * GELU_C * pre_activation * pre_activation
    )
    return (value_out, slopes)


def dot(left, right, dims):
    return lax.dot_general(left, right, (dims, ((), ())), preferred_element_type=F32)


def nn(left, right):
    return dot(left, right, ((1,), (0,)))


def nt(left, right):
    return dot(left, right, ((1,), (1,)))


def tn(left, right):
    return dot(left, right, ((0,), (0,)))


def split(value):
    high = value.astype(BF16)
    return high, (value - high.astype(F32)).astype(BF16)


def fused_kernel(
    n_tok, n_hid, n_part, scale,
    tokens, cotangent, w_in, w_out, in_a, in_b, out_a, out_b,
    dx_out, terms_out, oa_all, ib_all,
    x, c, full_in, full_out, full_a, b_mat, second, first, second2, first2, a2,
    low, back, pre_s, back_s, act_s, grad_s, dense, rank_out, rank_back, oa_acc, ib_acc, terms,
    core_d, core_t, kept_d, kept_t, pend_d, pend_t, one_send, one_send_t, one_recv, one_recv_t,
    two_send, two_send_t, two_recv, two_recv_t, line_send, line_recv, all_t,
    act_send, act_recv, chip_sem, core_sem, first_sem, first_core_sem, w_sem, own_sem,
    core_r_sem, one_sem, two_sem, line_sem, line_got, term_sem, grad_send, grad_recv,
):
    t, h = lax.axis_index("tok"), lax.axis_index("hid")
    n_chip = n_hid // 2
    chip, core = h // 2, h % 2
    rows, cols = tokens.shape
    depth = w_in.shape[0]
    width = full_in.shape[1]
    part_width = width // n_part
    rank = full_a.shape[1]

    def remote(source, target, send, recv, where):
        return pltpu.make_async_remote_copy(
            src_ref=source, dst_ref=target, send_sem=send, recv_sem=recv,
            device_id=where, device_id_type=pl.DeviceIdType.MESH,
        )

    def begin(*arguments):
        copy = remote(*arguments)
        copy.start()
        return copy

    sibling = (t, 2 * chip + 1 - core)
    chips = [(t, 2 * ((chip + e) % n_chip) + core) for e in range(n_chip)]
    toks = [((t + d) % n_tok, h) for d in range(n_tok)]
    barrier = pltpu.get_barrier_semaphore()
    for where in [sibling] + chips[1:] + toks[1:]:
        pl.semaphore_signal(barrier, inc=1, device_id=where, device_id_type=pl.DeviceIdType.MESH)
    pl.semaphore_wait(barrier, n_chip + n_tok - 1)

    orders = [
        sorted(range(n_tok), key=lambda s: (abs(s - k), -abs(2 * s - n_tok + 1)))
        for k in range(n_tok)
    ]
    sources = [t]
    for j in range(1, n_tok):
        source = jnp.int32(orders[0][j])
        for k in range(1, n_tok):
            source = jnp.where(t == k, jnp.int32(orders[k][j]), source)
        sources.append(source)

    def row_at(source):
        return pl.multiple_of(source * rows, rows)

    def part(array, source, e):
        at_col = pl.multiple_of((2 * ((chip + n_chip - e) % n_chip) + core) * cols, cols)
        return array.at[pl.ds(row_at(source), rows), pl.ds(at_col, cols)]

    def along(source, blocks, send, recv, act):
        @pl.when((source <= t) & (t + 1 < n_tok))
        def _():
            for k, (block, target) in enumerate(blocks):
                act(remote(block, target, send(0, source, k), recv(source, k), (t + 1, h)))

        @pl.when((source >= t) & (t > 0))
        def _():
            for k, (block, target) in enumerate(blocks):
                act(remote(block, target, send(1, source, k), recv(source, k), (t - 1, h)))

    def start(copy):
        copy.start()

    def wait_send(copy):
        copy.wait_send()

    def act_blocks(j):
        source = sources[j]
        mine = (tokens, cotangent)
        return [
            (mine[k] if j == 0 else part(array, source, 0), part(array, source, 0))
            for k, array in enumerate((x, c))
        ]

    def act_along(j, act):
        along(
            sources[j], act_blocks(j),
            lambda way, source, k: act_send.at[way, source, k],
            lambda source, k: act_recv.at[source, k], act,
        )

    from_chip, from_core = {}, {}

    def to_chips(j):
        for e in range(1, n_chip):
            from_chip[j, e] = [
                begin(block, target, chip_sem.at[0, j, e - 1, k], chip_sem.at[1, j, e - 1, k], chips[e])
                for k, (block, target) in enumerate(act_blocks(j))
            ]

    def to_core(j, e):
        if e == 0:
            blocks = act_blocks(j)
        else:
            blocks = [(part(array, sources[j], e),) * 2 for array in (x, c)]
        from_core[j, e] = [
            begin(block, target, core_sem.at[0, j, e, k], core_sem.at[1, j, e, k], sibling)
            for k, (block, target) in enumerate(blocks)
        ]

    def first_part(e):
        at = pl.multiple_of((2 * ((chip + n_chip - e) % n_chip) + core) * cols, cols)
        return full_a.at[pl.ds(at, cols), :]

    weights = {}
    depths = pl.ds(pl.multiple_of(t * depth, depth), depth)

    def weight_blocks(d, p):
        at = pl.multiple_of(((t + d) % n_tok) * width + p * part_width, part_width)
        here = pl.ds(p * part_width, part_width)
        return [
            (w_in.at[:, pl.ds(at, part_width)], full_in.at[depths, here]),
            (w_out.at[pl.ds(at, part_width), :], full_out.at[here, depths]),
        ]

    def send_weight(d, p, k):
        block, target = weight_blocks(d, p)[k]
        weights[d, p, k] = begin(
            block, target, w_sem.at[0, d - 1, p, k], w_sem.at[1, d - 1, p, k], toks[d]
        )

    act_along(0, start)
    to_chips(0)
    firsts = [
        begin(in_a, first_part(0), first_sem.at[0, e - 1], first_sem.at[1, e - 1], chips[e])
        for e in range(1, n_chip)
    ]
    to_core(0, 0)
    a_core = [begin(in_a, first_part(0), first_core_sem.at[0, 0], first_core_sem.at[1, 0], sibling)]
    pieces = [(d, p, k) for p in range(n_part) for k in range(2) for d in range(1, n_tok)]
    pieces = [piece for piece in pieces if piece[1:] != (0, 0) or piece[0] in (1, n_tok - 1)]
    rest = [(d, 0, 0) for d in range(2, n_tok - 1)] + pieces[min(2, n_tok - 1):]
    for piece in pieces[:min(2, n_tok - 1)]:
        send_weight(*piece)
    at = pl.multiple_of(t * width, width)
    own = [(block, target) for block, target in act_blocks(0)]
    own += [(in_a, first_part(0)), (out_b, b_mat)]
    own += [(in_b.at[:, pl.ds(at, width)], second), (out_a.at[pl.ds(at, width), :], first)]
    for p in range(n_part):
        own += weight_blocks(0, p)
    own = [
        pltpu.make_async_copy(block, target, own_sem.at[k])
        for k, (block, target) in enumerate(own)
    ]
    for copy in own:
        copy.start()

    def arrive(j):
        for k, (block, target) in enumerate(act_blocks(j)):
            remote(
                target, target, act_send.at[0, sources[j], k], act_recv.at[sources[j], k], sibling
            ).wait_recv()
        act_along(j, start)
        to_chips(j)
        to_core(j, 0)

    def pass_on(j):
        for e in range(1, n_chip):
            for copy in from_chip[j, e]:
                copy.wait_recv()
            to_core(j, e)

    def complete(j):
        for e in range(n_chip):
            for copy in from_core[j, e]:
                copy.wait_recv()

    def ranks(source):
        here = pl.ds(row_at(source), rows)
        high, rest = split(nn(x[here, :], full_a[...]))
        low[here, :rank] = high
        low[here, rank:] = rest
        high, rest = split(nt(c[here, :], b_mat[...]))
        back[here, :rank] = high
        back[here, rank:] = rest

    def hidden(p, source, begun):
        here = pl.ds(row_at(source), rows)
        those = slice(p * part_width, (p + 1) * part_width)
        pre_s[...] = nn(x[here, :], full_in[:, those]) + nn(low[here, :], second2[:, those])
        back_s[...] = nt(c[here, :], full_out[those, :]) + nt(back[here, :], first2[those, :])
        step = rows // 8
        for at in range(0, rows, step):
            some = slice(at, at + step)
            value_out, slopes = gelu_pair(pre_s[some, :])
            act_s[some, :] = value_out.astype(BF16)
            grad_s[some, :] = (back_s[some, :] * slopes).astype(BF16)
        act, grad = act_s[...], grad_s[...]
        oa_new, ib_new = tn(act, back[here, :]), tn(low[here, :], grad)
        out_new, back_new = nn(act, first[those, :]), nt(grad, second[:, those])
        if begun:
            oa_acc[p] += oa_new
            ib_acc[p] += ib_new
        else:
            oa_acc[p] = oa_new
            ib_acc[p] = ib_new
        if p == 0:
            rank_out[here, :] = out_new
            rank_back[here, :] = back_new
        else:
            rank_out[here, :] += out_new
            rank_back[here, :] += back_new
        if p < n_part - 1:
            if p == 0:
                dense[here, :] = nt(grad, full_in[:, those])
            else:
                dense[here, :] += nt(grad, full_in[:, those])
            return
        high, rest = split(rank_back[here, :])
        low[here, :rank] = high
        low[here, rank:] = rest
        high, rest = split(rank_out[here, :])
        back[here, :rank] = high
        back[here, rank:] = rest
        value = nt(grad, full_in[:, those]) + nt(low[here, :], a2[...])
        dense[here, :] = dense[here, :] + value if n_part > 1 else value

    def prepare():
        for e in range(1, n_chip):
            firsts[e - 1].wait_recv()
            a_core.append(begin(
                first_part(e), first_part(e), first_core_sem.at[0, e], first_core_sem.at[1, e],
                sibling,
            ))
        for copy in own:
            copy.wait()
        for copy in a_core:
            copy.wait_recv()
        half = (ADAPTER_SCALE * second[...].astype(F32)).astype(BF16)
        second2[:rank, :] = half
        second2[rank:, :] = half
        half = (ADAPTER_SCALE * first[...].astype(F32)).astype(BF16)
        first2[:, :rank] = half
        first2[:, rank:] = half
        half = (ADAPTER_SCALE * full_a[...].astype(F32)).astype(BF16)
        a2[:, :rank] = half
        a2[:, rank:] = half

    early = len(pieces) // 3
    for j in range(1, n_tok):
        arrive(j)
        for piece in {2: rest[:early], n_tok - 1: rest[early:]}.get(j, []):
            send_weight(*piece)
        if j >= 2:
            pass_on(j - 2)
            complete(j - 2)
        if j == n_tok - 1:
            prepare()
        if j >= 3:
            ranks(sources[j - 3])
    for j in range(max(n_tok - 2, 0), n_tok):
        if j < n_tok - 1:
            pass_on(j)
            complete(j)
        ranks(sources[j - 1])

    def wait_weights(p):
        for d in range(1, n_tok):
            for k in range(2):
                weights[d, p, k].wait_recv()

    def oa_blocks(source, p):
        at = pl.multiple_of(source * width + p * part_width, part_width)
        oa_at, ib_at = oa_all.at[pl.ds(at, part_width), :], ib_all.at[:, pl.ds(at, part_width)]
        return [(oa_at, oa_at), (ib_at, ib_at)]

    def grads_along(source, p, act):
        along(
            source, oa_blocks(source, p),
            lambda way, source, k: grad_send.at[way, source, p, k],
            lambda source, k: grad_recv.at[source, p, k], act,
        )

    def finish_grads(p):
        at = pl.multiple_of(t * width + p * part_width, part_width)
        oa = oa_acc[p]
        oa_all[pl.ds(at, part_width), :] = (scale * (oa[:, :rank] + oa[:, rank:])).astype(BF16)
        ib = ib_acc[p]
        ib_all[:, pl.ds(at, part_width)] = (scale * (ib[:rank] + ib[rank:])).astype(BF16)
        grads_along(t, p, start)

    def grad_hop(s, p):
        def relay(source):
            blocks = oa_blocks(source, p)
            for k, (block, target) in enumerate(blocks):
                remote(
                    target, target, grad_send.at[0, source, p, k], grad_recv.at[source, p, k],
                    sibling,
                ).wait_recv()
            grads_along(source, p, start)

        pl.when(t >= s + 1)(lambda: relay(t - 1 - s))
        pl.when(t + 1 + s < n_tok)(lambda: relay(t + 1 + s))

    wait_weights(0)
    if n_part > 1:
        for j in range(n_tok - 1):
            hidden(0, sources[j], j > 0)
    pass_on(n_tok - 1)
    complete(n_tok - 1)
    ranks(sources[n_tok - 1])
    if n_part > 1:
        hidden(0, sources[n_tok - 1], True)
        finish_grads(0)
    for p in range(1, n_part - 1):
        wait_weights(p)
        for j in range(n_tok):
            hidden(p, sources[j], j > 0)
        finish_grads(p)
    last = n_part - 1
    if last > 0:
        wait_weights(last)

    at_x, at_y = chip % 2, chip // 2
    square = [
        2 * ((at_y + e // 2) % 2) + (at_x + e % 2) % 2 for e in range(n_chip)
    ]
    core_copies, first_copies, second_copies, tok_copies = {}, {}, {}, []
    blocks = [sources[n_tok - 1 - q] for q in range(n_tok)]

    def columns(e, parity):
        return pl.ds(pl.multiple_of((2 * square[e] + parity) * cols, cols), cols)

    def here(q):
        return pl.ds(row_at(blocks[q]), rows)

    def buffers(q):
        if q == n_tok:
            return core_t, kept_t, pend_t, one_send_t, one_recv_t, two_send_t, two_recv_t
        return tuple(
            array.at[q] for array in (core_d, kept_d, pend_d, one_send, one_recv, two_send, two_recv)
        )

    def to_sibling(q):
        got = buffers(q)[0]
        core_copies[q] = []
        for e in range(n_chip):
            those = columns(e, 1 - core)
            source = terms.at[:, those] if q == n_tok else dense.at[here(q), those]
            core_copies[q].append(
                begin(source, got.at[e], core_r_sem.at[0, q, e], core_r_sem.at[1, q, e], sibling)
            )

    def over_core(q):
        got, kept, pend, sent, recv = buffers(q)[:5]
        half = kept.shape[0] // 2
        first_copies[q] = []
        for e in (3, 1, 2, 0):
            core_copies[q][e].wait_recv()
            those = columns(e, core)
            mine = terms[:, those] if q == n_tok else dense[here(q), those]
            value = mine + got[e]
            for i in range(2):
                some = value[i * half:(i + 1) * half]
                if e == 0:
                    kept[i * half:(i + 1) * half, :] = some
                elif e == 2 - i:
                    pend[i] = some
                else:
                    sent[i, 0 if e == 1 + i else 1] = some.astype(BF16)
        for i in range(2):
            first_copies[q].append(begin(
                sent.at[i], recv.at[i], one_sem.at[0, q, i], one_sem.at[1, q, i],
                (t, 2 * square[1 + i] + core),
            ))

    def over_first(q):
        _, kept, pend, _, recv, sent, second_recv = buffers(q)
        half = kept.shape[0] // 2
        second_copies[q] = []
        for i in range(2):
            first_copies[q][i].wait_recv()
            sent[i] = (pend[i] + recv[i, 1].astype(F32)).astype(BF16)
            second_copies[q].append(begin(
                sent.at[i], second_recv.at[i], two_sem.at[0, q, i], two_sem.at[1, q, i],
                (t, 2 * square[2 - i] + core),
            ))
            some = slice(i * half, (i + 1) * half)
            kept[some, :] = kept[some, :] + recv[i, 0].astype(F32)

    def over_second(q):
        _, kept, _, _, _, _, recv = buffers(q)
        half = kept.shape[0] // 2
        for i in range(2):
            second_copies[q][i].wait_recv()
            some = slice(i * half, (i + 1) * half)
            kept[some, :] = kept[some, :] + recv[i].astype(F32)

    def line_copy(q, way):
        where = (t + 1 - 2 * way, h)
        return remote(
            line_send.at[min(q, n_tok - 2)], line_recv.at[way, blocks[q]],
            line_sem.at[way, min(q, n_tok - 2)], line_got.at[way, blocks[q]], where,
        )

    def send_line(q, way):
        line_send[q] = kept_d[q].astype(BF16)
        line_copy(q, way).start()

    def add_line(q, way):
        line_copy(q, way).wait_recv()
        kept_d[q] = kept_d[q] + line_recv[way, blocks[q]].astype(F32)

    def start_line(q):
        pl.when((blocks[q] > t) & (t == 0))(lambda: send_line(q, 0))
        pl.when((blocks[q] < t) & (t == n_tok - 1))(lambda: send_line(q, 1))

    def over_line(q):
        def add_and_send(way):
            add_line(q, way)
            send_line(q, way)

        pl.when((blocks[q] > t) & (t > 0))(lambda: add_and_send(0))
        pl.when((blocks[q] < t) & (t < n_tok - 1))(lambda: add_and_send(1))

    def share_terms():
        all_t[t] = kept_t[...].astype(BF16)
        for k in range(1, n_tok):
            tok_copies.append(begin(
                all_t.at[t], all_t.at[t], term_sem.at[0, k - 1], term_sem.at[1, k - 1], toks[k]
            ))

    def sum_terms():
        out_cols = x.shape[1] // n_chip
        for at in range(0, x.shape[1], out_cols):
            those = slice(at, at + out_cols)
            value = tn(back[...], c[:, those])
            terms[:rank, those] = scale * (value[:rank] + value[rank:])
            value = tn(low[...], x[:, those])
            terms[rank:, those] = scale * (value[:rank] + value[rank:])

    def hop(s):
        for p in range(last):
            grad_hop(s, p)

    final = n_tok - 1
    for q in range(n_tok):
        hidden(last, blocks[q], q > 0)
        to_sibling(q)
        if q >= 1:
            over_core(q - 1)
        if q == 2:
            hop(0)
    finish_grads(last)
    for q in range(final - 1):
        over_first(q)
    sum_terms()
    to_sibling(n_tok)
    hop(1)
    over_core(n_tok)
    over_first(final - 1)
    over_second(0)
    start_line(0)
    grad_hop(0, last)
    for q in range(1, final - 1):
        over_second(q)
        start_line(q)
    over_first(n_tok)
    over_core(final)
    over_line(0)
    over_second(final - 1)
    start_line(final - 1)
    over_second(n_tok)
    share_terms()
    if n_tok > 2:
        grad_hop(1, last)
    over_first(final)
    for q in range(1, final):
        over_line(q)
    for s in range(2, n_tok - 1):
        hop(s)
    over_second(final)
    for s in range(2, n_tok - 1):
        grad_hop(s, last)
    pl.when(t > 0)(lambda: add_line(final, 0))
    pl.when(t < n_tok - 1)(lambda: add_line(final, 1))
    dx_out[...] = kept_d[final]
    for copy in tok_copies:
        copy.wait_recv()
    value = all_t[0].astype(F32)
    for k in range(1, n_tok):
        value = value + all_t[k].astype(F32)
    terms_out[...] = value
    for q in range(final):
        pl.when(blocks[q] > t)(lambda: line_copy(q, 0).wait_send())
        pl.when(blocks[q] < t)(lambda: line_copy(q, 1).wait_send())
    for j in range(n_tok):
        act_along(j, wait_send)
        for p in range(n_part):
            grads_along(sources[j], p, wait_send)
    for groups in (from_chip, from_core, core_copies, first_copies, second_copies):
        for group in groups.values():
            for copy in group:
                copy.wait_send()
    for copy in firsts + a_core + list(weights.values()) + tok_copies:
        copy.wait_send()


def fused(n_part, scale, tokens, cotangent, frozen_in, frozen_out, in_a, in_b, out_a, out_b):
    n_tok, n_hid = lax.axis_size("tok"), lax.axis_size("hid")
    n_chip = n_hid // 2
    rows, cols = tokens.shape
    count, features = rows * n_tok, cols * n_hid
    width = frozen_in.shape[1] // n_tok
    part_width = width // n_part
    rank = in_a.shape[1]
    sems = pltpu.SemaphoreType.DMA
    vmem = pl.BlockSpec(memory_space=pltpu.VMEM)
    whole = pl.BlockSpec(memory_space=pl.ANY)
    arguments = (tokens, cotangent, frozen_in, frozen_out, in_a, in_b, out_a, out_b)
    return pl.pallas_call(
        functools.partial(fused_kernel, n_tok, n_hid, n_part, scale),
        out_shape=(
            jax.ShapeDtypeStruct((rows, cols), F32),
            jax.ShapeDtypeStruct((2 * rank, cols), F32),
            jax.ShapeDtypeStruct((n_tok * width, rank), BF16),
            jax.ShapeDtypeStruct((rank, n_tok * width), BF16),
        ),
        in_specs=[whole] * 8,
        out_specs=(vmem,) * 4,
        scratch_shapes=[
            pltpu.VMEM((count, features), BF16),
            pltpu.VMEM((count, features), BF16),
            pltpu.VMEM((features, width), BF16),
            pltpu.VMEM((width, features), BF16),
            pltpu.VMEM((features, rank), BF16),
            pltpu.VMEM((rank, features), BF16),
            pltpu.VMEM((rank, width), BF16),
            pltpu.VMEM((width, rank), BF16),
            pltpu.VMEM((2 * rank, width), BF16),
            pltpu.VMEM((width, 2 * rank), BF16),
            pltpu.VMEM((features, 2 * rank), BF16),
            pltpu.VMEM((count, 2 * rank), BF16),
            pltpu.VMEM((count, 2 * rank), BF16),
            pltpu.VMEM((rows, part_width), F32),
            pltpu.VMEM((rows, part_width), F32),
            pltpu.VMEM((rows, part_width), BF16),
            pltpu.VMEM((rows, part_width), BF16),
            pltpu.VMEM((count, features), F32),
            pltpu.VMEM((count, rank), F32),
            pltpu.VMEM((count, rank), F32),
            pltpu.VMEM((n_part, part_width, 2 * rank), F32),
            pltpu.VMEM((n_part, 2 * rank, part_width), F32),
            pltpu.VMEM((2 * rank, features), F32),
            pltpu.VMEM((n_tok, n_chip, rows, cols), F32),
            pltpu.VMEM((n_chip, 2 * rank, cols), F32),
            pltpu.VMEM((n_tok, rows, cols), F32),
            pltpu.VMEM((2 * rank, cols), F32),
            pltpu.VMEM((n_tok, 2, rows // 2, cols), F32),
            pltpu.VMEM((2, rank, cols), F32),
            pltpu.VMEM((n_tok, 2, 2, rows // 2, cols), BF16),
            pltpu.VMEM((2, 2, rank, cols), BF16),
            pltpu.VMEM((n_tok, 2, 2, rows // 2, cols), BF16),
            pltpu.VMEM((2, 2, rank, cols), BF16),
            pltpu.VMEM((n_tok, 2, rows // 2, cols), BF16),
            pltpu.VMEM((2, rank, cols), BF16),
            pltpu.VMEM((n_tok, 2, rows // 2, cols), BF16),
            pltpu.VMEM((2, rank, cols), BF16),
            pltpu.VMEM((n_tok - 1, rows, cols), BF16),
            pltpu.VMEM((2, n_tok, rows, cols), BF16),
            pltpu.VMEM((n_tok, 2 * rank, cols), BF16),
            sems((2, n_tok, 2)),
            sems((n_tok, 2)),
            sems((2, n_tok, n_chip - 1, 2)),
            sems((2, n_tok, n_chip, 2)),
            sems((2, n_chip - 1)),
            sems((2, n_chip)),
            sems((2, n_tok - 1, n_part, 2)),
            sems((6 + 2 * n_part,)),
            sems((2, n_tok + 1, n_chip)),
            sems((2, n_tok + 1, 2)),
            sems((2, n_tok + 1, 2)),
            sems((2, n_tok - 1)),
            sems((2, n_tok)),
            sems((2, n_tok - 1)),
            sems((2, n_tok, n_part, 2)),
            sems((n_tok, n_part, 2)),
        ],
        compiler_params=pltpu.CompilerParams(
            collective_id=1, has_side_effects=True, vmem_limit_bytes=52 * 1024 * 1024
        ),
    )(*(pltpu.with_memory_space_constraint(array, pltpu.HBM) for array in arguments))


def finish_kernel(dx, terms, oa, ib, dx_out, in_a_out, ib_out, oa_out, out_b_out):
    rank = in_a_out.shape[1]
    ib_out[...] = ib[...].astype(F32)
    oa_out[...] = oa[...].astype(F32)
    dx_out[...] = dx[...]
    in_a_out[...] = terms[rank:, :].T
    out_b_out[...] = terms[:rank, :]


def local(tokens, cotangent, frozen_in, frozen_out, in_a, in_b, out_a, out_b):
    count = tokens.shape[0] * lax.axis_size("tok")
    scale = ADAPTER_SCALE / math.sqrt(count)
    dx, terms, oa, ib = fused(
        2, scale, tokens, cotangent, frozen_in, frozen_out, in_a, in_b, out_a, out_b
    )
    rank, cols = in_a.shape[1], tokens.shape[1]
    vmem = pl.BlockSpec(memory_space=pltpu.VMEM)
    return pl.pallas_call(
        finish_kernel,
        out_shape=(
            jax.ShapeDtypeStruct(dx.shape, F32),
            jax.ShapeDtypeStruct((cols, rank), F32),
            jax.ShapeDtypeStruct(ib.shape, F32),
            jax.ShapeDtypeStruct(oa.shape, F32),
            jax.ShapeDtypeStruct((rank, cols), F32),
        ),
        in_specs=[vmem] * 4,
        out_specs=(vmem,) * 5,
        compiler_params=pltpu.CompilerParams(vmem_limit_bytes=16 * 1024 * 1024),
    )(dx, terms, oa, ib)


def local_by_rows(
    tokens,
    cotangent,
    frozen_in,
    frozen_out,
    input_adapter_first,
    input_adapter_second,
    adapter_out_a,
    adapter_out_b,
):
    highest_precision = lax.Precision.HIGHEST
    device_local_rows = tokens.shape[0]
    rank_width = input_adapter_second.shape[0]
    gradient_scale = ADAPTER_SCALE / math.sqrt(device_local_rows * lax.axis_size("tok"))
    full_tokens, full_cotan = (
        lax.all_gather(tokens, "hid", axis=1, tiled=True),
        lax.all_gather(cotangent, "hid", axis=1, tiled=True),
    )
    in_rows = lax.all_gather(frozen_in, "tok", axis=0, tiled=True)
    in_a_full = lax.all_gather(input_adapter_first, "hid", axis=0, tiled=True)
    lowrank_input = jnp.dot(full_tokens, in_a_full, preferred_element_type=jnp.float32)
    second_float = input_adapter_second.astype(jnp.float32)
    out_a_float = adapter_out_a.astype(jnp.float32)
    pre_activation = jnp.dot(
        full_tokens, in_rows, preferred_element_type=jnp.float32
    ) + ADAPTER_SCALE * jnp.dot(lowrank_input, second_float, precision=highest_precision)
    value_out, slopes = gelu_pair(pre_activation)
    hidden_act = value_out.astype(jnp.bfloat16)
    backward_lowrank = jnp.einsum(
        "td,rd->tr", full_cotan, adapter_out_b, preferred_element_type=jnp.float32
    )
    rank_out = jnp.dot(hidden_act, adapter_out_a, preferred_element_type=jnp.float32)
    dense_backward = jnp.einsum(
        "td,fd->tf",
        full_cotan,
        lax.all_gather(frozen_out, "tok", axis=1, tiled=True),
        preferred_element_type=jnp.float32,
    )
    dense_backward = dense_backward + ADAPTER_SCALE * jnp.dot(
        backward_lowrank, out_a_float.T, precision=highest_precision
    )
    grad_pre = (dense_backward * slopes).astype(jnp.bfloat16)
    rank_backward = jnp.einsum(
        "tf,rf->tr", grad_pre, input_adapter_second, preferred_element_type=jnp.float32
    )
    dense_in = jnp.einsum("tf,df->td", grad_pre, in_rows, preferred_element_type=jnp.float32)
    grad_out_a = gradient_scale * jnp.dot(
        hidden_act.astype(jnp.float32).T, backward_lowrank, precision=highest_precision
    )
    grad_in_b = gradient_scale * jnp.dot(
        lowrank_input.T, grad_pre.astype(jnp.float32), precision=highest_precision
    )
    in_a_float = in_a_full.astype(jnp.float32)
    dx_term = dense_in + ADAPTER_SCALE * jnp.dot(
        rank_backward, in_a_float.T, precision=highest_precision
    )
    out_term = jnp.dot(rank_out.T, full_cotan.astype(jnp.float32), precision=highest_precision)
    in_term = jnp.dot(rank_backward.T, full_tokens.astype(jnp.float32), precision=highest_precision)
    rank_terms = jnp.concatenate([out_term, in_term], axis=0)
    input_gradient, rank_local = (
        lax.psum_scatter(dx_term, "hid", scatter_dimension=1, tiled=True),
        lax.psum_scatter(rank_terms, "hid", scatter_dimension=1, tiled=True),
    )
    grad_out_a, grad_in_b, rank_total = lax.psum((grad_out_a, grad_in_b, rank_local), "tok")
    grad_out_b = gradient_scale * rank_total[:rank_width]
    grad_in_a = gradient_scale * rank_total[rank_width:].T
    return (input_gradient, grad_in_a, grad_in_b, grad_out_a, grad_out_b)


def solution(mesh):
    in_specs = (
        P("tok", "hid"),
        P("tok", "hid"),
        P("tok", "hid"),
        P("hid", "tok"),
        P("hid", None),
        P(None, "hid"),
        P("hid", None),
        P(),
    )
    out_specs = (P("tok", "hid"), P("hid", None), P(None, "hid"), P("hid", None), P(None, "hid"))
    def body(*arrays):
        share = arrays[2].shape[1] // lax.axis_size("tok")
        wide = share % 256 == 0 and lax.axis_size("tok") > 2
        wide = wide and lax.axis_size("hid") == 2 ** len(("y", "x", "core"))
        return local(*arrays) if wide else local_by_rows(*arrays)

    return jax.shard_map(body, mesh=mesh, in_specs=in_specs, out_specs=out_specs, check_vma=False)
```

```python
import functools
import math

import jax
import jax.numpy as jnp
from jax import lax
from jax.experimental import pallas as pl
from jax.experimental.pallas import tpu as pltpu
from jax.sharding import PartitionSpec as P

ADAPTER_SCALE = 0.5
GELU_K = 0.7978845608
GELU_C = 0.044715
F32 = jnp.float32
BF16 = jnp.bfloat16


def gelu_pair(pre_activation):
    tangent = jnp.tanh(
        GELU_K * (pre_activation + GELU_C * pre_activation * pre_activation * pre_activation)
    )
    value_out = 0.5 * pre_activation * (1.0 + tangent)
    slopes = 0.5 * (1.0 + tangent) + 0.5 * pre_activation * (1.0 - tangent * tangent) * GELU_K * (
        1.0 + 3.0 * GELU_C * pre_activation * pre_activation
    )
    return (value_out, slopes)


def dot(left, right, dims):
    return lax.dot_general(left, right, (dims, ((), ())), preferred_element_type=F32)


def nn(left, right):
    return dot(left, right, ((1,), (0,)))


def nt(left, right):
    return dot(left, right, ((1,), (1,)))


def tn(left, right):
    return dot(left, right, ((0,), (0,)))


def split(value):
    high = value.astype(BF16)
    return high, (value - high.astype(F32)).astype(BF16)


def fused_kernel(
    n_tok, n_hid, n_part, scale,
    tokens, cotangent, w_in, w_out, in_a, in_b, out_a, out_b,
    dx_out, terms_out, oa_all, ib_all,
    x, c, full_in, full_out, full_a, b_mat, second, first, second2, first2, a2,
    low, back, outs, pre_s, slopes, act_s, grad_s, dense, rank_out, rank_back, oa_acc, ib_acc, terms,
    core_d, core_t, kept_d, kept_t, pend_d, pend_t, one_send, one_send_t, one_recv, one_recv_t,
    two_send, two_send_t, two_recv, two_recv_t, line_send, line_recv, all_t,
    act_send, act_recv, chip_sem, core_sem, first_sem, first_core_sem, w_sem, own_sem,
    core_r_sem, one_sem, two_sem, line_sem, line_got, term_sem, grad_send, grad_recv,
):
    t, h = lax.axis_index("tok"), lax.axis_index("hid")
    n_chip = n_hid // 2
    chip, core = h // 2, h % 2
    rows, cols = tokens.shape
    depth = w_in.shape[0]
    width = full_in.shape[1]
    part_width = width // n_part
    rank = full_a.shape[1]

    def remote(source, target, send, recv, where):
        return pltpu.make_async_remote_copy(
            src_ref=source, dst_ref=target, send_sem=send, recv_sem=recv,
            device_id=where, device_id_type=pl.DeviceIdType.MESH,
        )

    def begin(*arguments):
        copy = remote(*arguments)
        copy.start()
        return copy

    sibling = (t, 2 * chip + 1 - core)
    chips = [(t, 2 * ((chip + e) % n_chip) + core) for e in range(n_chip)]
    toks = [((t + d) % n_tok, h) for d in range(n_tok)]
    barrier = pltpu.get_barrier_semaphore()
    for where in [sibling] + chips[1:] + toks[1:]:
        pl.semaphore_signal(barrier, inc=1, device_id=where, device_id_type=pl.DeviceIdType.MESH)
    pl.semaphore_wait(barrier, n_chip + n_tok - 1)

    orders = [
        sorted(range(n_tok), key=lambda s: (abs(s - k), -abs(2 * s - n_tok + 1)))
        for k in range(n_tok)
    ]
    sources = [t]
    for j in range(1, n_tok):
        source = jnp.int32(orders[0][j])
        for k in range(1, n_tok):
            source = jnp.where(t == k, jnp.int32(orders[k][j]), source)
        sources.append(source)

    def row_at(source):
        return pl.multiple_of(source * rows, rows)

    def part(array, source, e):
        at_col = pl.multiple_of((2 * ((chip + n_chip - e) % n_chip) + core) * cols, cols)
        return array.at[pl.ds(row_at(source), rows), pl.ds(at_col, cols)]

    def along(source, blocks, send, recv, act):
        @pl.when((source <= t) & (t + 1 < n_tok))
        def _():
            for k, (block, target) in enumerate(blocks):
                act(remote(block, target, send(0, source, k), recv(source, k), (t + 1, h)))

        @pl.when((source >= t) & (t > 0))
        def _():
            for k, (block, target) in enumerate(blocks):
                act(remote(block, target, send(1, source, k), recv(source, k), (t - 1, h)))

    def start(copy):
        copy.start()

    def wait_send(copy):
        copy.wait_send()

    def act_blocks(j):
        source = sources[j]
        mine = (tokens, cotangent)
        return [
            (mine[k] if j == 0 else part(array, source, 0), part(array, source, 0))
            for k, array in enumerate((x, c))
        ]

    def act_along(j, act):
        along(
            sources[j], act_blocks(j),
            lambda way, source, k: act_send.at[way, source, k],
            lambda source, k: act_recv.at[source, k], act,
        )

    from_chip, from_core = {}, {}

    def to_chips(j):
        for e in range(1, n_chip):
            from_chip[j, e] = [
                begin(block, target, chip_sem.at[0, j, e - 1, k], chip_sem.at[1, j, e - 1, k], chips[e])
                for k, (block, target) in enumerate(act_blocks(j))
            ]

    def to_core(j, e):
        if e == 0:
            blocks = act_blocks(j)
        else:
            blocks = [(part(array, sources[j], e),) * 2 for array in (x, c)]
        from_core[j, e] = [
            begin(block, target, core_sem.at[0, j, e, k], core_sem.at[1, j, e, k], sibling)
            for k, (block, target) in enumerate(blocks)
        ]

    def first_part(e):
        at = pl.multiple_of((2 * ((chip + n_chip - e) % n_chip) + core) * cols, cols)
        return full_a.at[pl.ds(at, cols), :]

    weights = {}
    depths = pl.ds(pl.multiple_of(t * depth, depth), depth)

    def weight_blocks(d, p):
        at = pl.multiple_of(((t + d) % n_tok) * width + p * part_width, part_width)
        here = pl.ds(p * part_width, part_width)
        return [
            (w_in.at[:, pl.ds(at, part_width)], full_in.at[depths, here]),
            (w_out.at[pl.ds(at, part_width), :], full_out.at[here, depths]),
        ]

    def send_weight(d, p, k):
        block, target = weight_blocks(d, p)[k]
        weights[d, p, k] = begin(
            block, target, w_sem.at[0, d - 1, p, k], w_sem.at[1, d - 1, p, k], toks[d]
        )

    act_along(0, start)
    to_chips(0)
    firsts = [
        begin(in_a, first_part(0), first_sem.at[0, e - 1], first_sem.at[1, e - 1], chips[e])
        for e in range(1, n_chip)
    ]
    to_core(0, 0)
    a_core = [begin(in_a, first_part(0), first_core_sem.at[0, 0], first_core_sem.at[1, 0], sibling)]
    pieces = [(d, p, k) for p in range(n_part) for k in range(2) for d in range(1, n_tok)]
    pieces = [piece for piece in pieces if piece[1:] != (0, 0) or piece[0] in (1, n_tok - 1)]
    rest = [(d, 0, 0) for d in range(2, n_tok - 1)] + pieces[min(2, n_tok - 1):]
    for piece in pieces[:min(2, n_tok - 1)]:
        send_weight(*piece)
    at = pl.multiple_of(t * width, width)
    own = [(block, target) for block, target in act_blocks(0)]
    own += [(in_a, first_part(0)), (out_b, b_mat)]
    own += [(in_b.at[:, pl.ds(at, width)], second), (out_a.at[pl.ds(at, width), :], first)]
    for p in range(n_part):
        own += weight_blocks(0, p)
    own = [
        pltpu.make_async_copy(block, target, own_sem.at[k])
        for k, (block, target) in enumerate(own)
    ]
    for copy in own:
        copy.start()

    def arrive(j):
        for k, (block, target) in enumerate(act_blocks(j)):
            remote(
                target, target, act_send.at[0, sources[j], k], act_recv.at[sources[j], k], sibling
            ).wait_recv()
        act_along(j, start)
        to_chips(j)
        to_core(j, 0)

    def pass_on(j):
        for e in range(1, n_chip):
            for copy in from_chip[j, e]:
                copy.wait_recv()
            to_core(j, e)

    def complete(j):
        for e in range(n_chip):
            for copy in from_core[j, e]:
                copy.wait_recv()

    def ranks(source):
        here = pl.ds(row_at(source), rows)
        high, rest = split(nn(x[here, :], full_a[...]))
        low[here, :rank] = high
        low[here, rank:] = rest
        high, rest = split(nt(c[here, :], b_mat[...]))
        back[here, :rank] = high
        back[here, rank:] = rest

    def forward(p, source, begun):
        here = pl.ds(row_at(source), rows)
        those = slice(p * part_width, (p + 1) * part_width)
        pre_s[...] = nn(x[here, :], full_in[:, those]) + nn(low[here, :], second2[:, those])
        step = rows // 8
        for at in range(0, rows, step):
            some = slice(at, at + step)
            value_out, slope = gelu_pair(pre_s[some, :])
            act_s[some, :] = value_out.astype(BF16)
            slopes[pl.ds(pl.multiple_of(row_at(source) + at, step), step), :] = slope
        act = act_s[...]
        oa_new, out_new = tn(act, back[here, :]), nn(act, first[those, :])
        oa_acc[p] = oa_acc[p] + oa_new if begun else oa_new
        value = out_new if p == 0 else rank_out[here, :] + out_new
        if p < n_part - 1:
            rank_out[here, :] = value
        else:
            high, rest = split(value)
            outs[here, :rank] = high
            outs[here, rank:] = rest

    def backward(p, source, begun):
        here = pl.ds(row_at(source), rows)
        those = slice(p * part_width, (p + 1) * part_width)
        value = nt(c[here, :], full_out[those, :]) + nt(back[here, :], first2[those, :])
        grad_s[...] = (value * slopes[here, :]).astype(BF16)
        grad = grad_s[...]
        ib_new, back_new = tn(low[here, :], grad), nt(grad, second[:, those])
        ib_acc[p] = ib_acc[p] + ib_new if begun else ib_new
        value = back_new if p == 0 else rank_back[here, :] + back_new
        if p < n_part - 1:
            rank_back[here, :] = value
            value = nt(grad, full_in[:, those])
        else:
            high, rest = split(value)
            low[here, :rank] = high
            low[here, rank:] = rest
            value = nt(grad, full_in[:, those]) + nt(low[here, :], a2[...])
        dense[here, :] = value if p == 0 else dense[here, :] + value

    def hidden(p, source, begun):
        forward(p, source, begun)
        backward(p, source, begun)

    def prepare():
        for e in range(1, n_chip):
            firsts[e - 1].wait_recv()
            a_core.append(begin(
                first_part(e), first_part(e), first_core_sem.at[0, e], first_core_sem.at[1, e],
                sibling,
            ))
        for copy in own:
            copy.wait()
        for copy in a_core:
            copy.wait_recv()
        half = (ADAPTER_SCALE * second[...].astype(F32)).astype(BF16)
        second2[:rank, :] = half
        second2[rank:, :] = half
        half = (ADAPTER_SCALE * first[...].astype(F32)).astype(BF16)
        first2[:, :rank] = half
        first2[:, rank:] = half
        half = (ADAPTER_SCALE * full_a[...].astype(F32)).astype(BF16)
        a2[:, :rank] = half
        a2[:, rank:] = half

    early = len(pieces) // 3
    for j in range(1, n_tok):
        arrive(j)
        for piece in {2: rest[:early], n_tok - 1: rest[early:]}.get(j, []):
            send_weight(*piece)
        if j >= 2:
            pass_on(j - 2)
            complete(j - 2)
        if j == n_tok - 1:
            prepare()
        if j >= 3:
            ranks(sources[j - 3])
    for j in range(max(n_tok - 2, 0), n_tok):
        if j < n_tok - 1:
            pass_on(j)
            complete(j)
        ranks(sources[j - 1])

    def wait_weights(p, k):
        for d in range(1, n_tok):
            weights[d, p, k].wait_recv()

    def grad_block(source, p, k):
        at = pl.multiple_of(source * width + p * part_width, part_width)
        if k == 0:
            return oa_all.at[pl.ds(at, part_width), :]
        return ib_all.at[:, pl.ds(at, part_width)]

    def grads_along(source, p, k, act):
        block = grad_block(source, p, k)
        along(
            source, [(block, block)],
            lambda way, source, _: grad_send.at[way, source, p, k],
            lambda source, _: grad_recv.at[source, p, k], act,
        )

    def finish_grad(p, k):
        block = grad_block(t, p, k)
        if k == 0:
            value = oa_acc[p]
            value = value[:, :rank] + value[:, rank:]
        else:
            value = ib_acc[p]
            value = value[:rank] + value[rank:]
        block[...] = (scale * value).astype(BF16)
        grads_along(t, p, k, start)

    def grad_hop(s, p, k):
        def relay(source):
            block = grad_block(source, p, k)
            remote(
                block, block, grad_send.at[0, source, p, k], grad_recv.at[source, p, k], sibling
            ).wait_recv()
            grads_along(source, p, k, start)

        pl.when(t >= s + 1)(lambda: relay(t - 1 - s))
        pl.when(t + 1 + s < n_tok)(lambda: relay(t + 1 + s))

    last = n_part - 1
    for p in range(last):
        for k in range(2):
            wait_weights(p, k)
        for j in range(n_tok):
            if p == 0 and j == n_tok - 1:
                pass_on(j)
                complete(j)
                ranks(sources[j])
            hidden(p, sources[j], j > 0)
        for k in range(2):
            finish_grad(p, k)
    wait_weights(last, 0)
    for j in range(n_tok):
        forward(last, sources[j], j > 0)
    finish_grad(last, 0)

    at_x, at_y = chip % 2, chip // 2
    square = [
        2 * ((at_y + e // 2) % 2) + (at_x + e % 2) % 2 for e in range(n_chip)
    ]
    core_copies, first_copies, second_copies, tok_copies = {}, {}, {}, []
    blocks = [sources[n_tok - 1 - q] for q in range(n_tok)]

    def columns(e, parity):
        return pl.ds(pl.multiple_of((2 * square[e] + parity) * cols, cols), cols)

    def here(q):
        return pl.ds(row_at(blocks[q]), rows)

    def buffers(q):
        if q >= n_tok:
            return tuple(array.at[q - n_tok] for array in (
                core_t, kept_t, pend_t, one_send_t, one_recv_t, two_send_t, two_recv_t
            ))
        return tuple(
            array.at[q] for array in (core_d, kept_d, pend_d, one_send, one_recv, two_send, two_recv)
        )

    def to_sibling(q):
        got = buffers(q)[0]
        core_copies[q] = []
        for e in range(n_chip):
            those = columns(e, 1 - core)
            source = terms.at[q - n_tok, :, those] if q >= n_tok else dense.at[here(q), those]
            core_copies[q].append(
                begin(source, got.at[e], core_r_sem.at[0, q, e], core_r_sem.at[1, q, e], sibling)
            )

    def over_core(q):
        got, kept, pend, sent, recv = buffers(q)[:5]
        half = kept.shape[0] // 2
        first_copies[q] = []
        for e in (3, 1, 2, 0):
            core_copies[q][e].wait_recv()
            those = columns(e, core)
            mine = terms[q - n_tok, :, those] if q >= n_tok else dense[here(q), those]
            value = mine + got[e]
            for i in range(2):
                some = value[i * half:(i + 1) * half]
                if e == 0:
                    kept[i * half:(i + 1) * half, :] = some
                elif e == 2 - i:
                    pend[i] = some
                else:
                    sent[i, 0 if e == 1 + i else 1] = some.astype(BF16)
        for i in range(2):
            first_copies[q].append(begin(
                sent.at[i], recv.at[i], one_sem.at[0, q, i], one_sem.at[1, q, i],
                (t, 2 * square[1 + i] + core),
            ))

    def over_first(q):
        _, kept, pend, _, recv, sent, second_recv = buffers(q)
        half = kept.shape[0] // 2
        second_copies[q] = []
        for i in range(2):
            first_copies[q][i].wait_recv()
            sent[i] = (pend[i] + recv[i, 1].astype(F32)).astype(BF16)
            second_copies[q].append(begin(
                sent.at[i], second_recv.at[i], two_sem.at[0, q, i], two_sem.at[1, q, i],
                (t, 2 * square[2 - i] + core),
            ))
            some = slice(i * half, (i + 1) * half)
            kept[some, :] = kept[some, :] + recv[i, 0].astype(F32)

    def over_second(q):
        _, kept, _, _, _, _, recv = buffers(q)
        half = kept.shape[0] // 2
        for i in range(2):
            second_copies[q][i].wait_recv()
            some = slice(i * half, (i + 1) * half)
            kept[some, :] = kept[some, :] + recv[i].astype(F32)

    def line_copy(q, way):
        where = (t + 1 - 2 * way, h)
        return remote(
            line_send.at[min(q, n_tok - 2)], line_recv.at[way, blocks[q]],
            line_sem.at[way, min(q, n_tok - 2)], line_got.at[way, blocks[q]], where,
        )

    def send_line(q, way):
        line_send[q] = kept_d[q].astype(BF16)
        line_copy(q, way).start()

    def add_line(q, way):
        line_copy(q, way).wait_recv()
        kept_d[q] = kept_d[q] + line_recv[way, blocks[q]].astype(F32)

    def start_line(q):
        pl.when((blocks[q] > t) & (t == 0))(lambda: send_line(q, 0))
        pl.when((blocks[q] < t) & (t == n_tok - 1))(lambda: send_line(q, 1))

    def over_line(q):
        def add_and_send(way):
            add_line(q, way)
            send_line(q, way)

        pl.when((blocks[q] > t) & (t > 0))(lambda: add_and_send(0))
        pl.when((blocks[q] < t) & (t < n_tok - 1))(lambda: add_and_send(1))

    def share_terms(i):
        all_t[i, t] = kept_t[i].astype(BF16)
        for k in range(1, n_tok):
            tok_copies.append(begin(
                all_t.at[i, t], all_t.at[i, t],
                term_sem.at[0, k - 1, i], term_sem.at[1, k - 1, i], toks[k],
            ))

    def sum_terms(i):
        ranks_of, of = ((outs, c), (low, x))[i]
        out_cols = x.shape[1] // n_chip
        for at in range(0, x.shape[1], out_cols):
            those = slice(at, at + out_cols)
            value = tn(ranks_of[...], of[:, those])
            terms[i, :, those] = scale * (value[:rank] + value[rank:])

    early = [(p, k) for p in range(last) for k in range(2)] + [(last, 0)]

    def hop(s):
        for p, k in early:
            grad_hop(s, p, k)

    final, out_term, in_term = n_tok - 1, n_tok, n_tok + 1
    sum_terms(0)
    to_sibling(out_term)
    over_core(out_term)
    wait_weights(last, 1)
    for q in range(n_tok):
        backward(last, blocks[q], q > 0)
        to_sibling(q)
        if q == 0:
            over_first(out_term)
        if q >= 1:
            over_core(q - 1)
        if q == 1:
            over_second(out_term)
            share_terms(0)
        if q == 2:
            hop(0)
    finish_grad(last, 1)
    sum_terms(1)
    to_sibling(in_term)
    for q in range(final - 1):
        over_first(q)
    over_core(in_term)
    hop(1)
    over_first(final - 1)
    over_second(0)
    start_line(0)
    grad_hop(0, last, 1)
    for q in range(1, final - 1):
        over_second(q)
        start_line(q)
    over_first(in_term)
    over_core(final)
    over_line(0)
    over_second(final - 1)
    start_line(final - 1)
    over_second(in_term)
    share_terms(1)
    if n_tok > 2:
        grad_hop(1, last, 1)
    over_first(final)
    for q in range(1, final):
        over_line(q)
    for s in range(2, n_tok - 1):
        hop(s)
    over_second(final)
    for s in range(2, n_tok - 1):
        grad_hop(s, last, 1)
    pl.when(t > 0)(lambda: add_line(final, 0))
    pl.when(t < n_tok - 1)(lambda: add_line(final, 1))
    dx_out[...] = kept_d[final]
    for copy in tok_copies:
        copy.wait_recv()
    for i in range(2):
        value = all_t[i, 0].astype(F32)
        for k in range(1, n_tok):
            value = value + all_t[i, k].astype(F32)
        terms_out[i * rank:(i + 1) * rank, :] = value
    for q in range(final):
        pl.when(blocks[q] > t)(lambda: line_copy(q, 0).wait_send())
        pl.when(blocks[q] < t)(lambda: line_copy(q, 1).wait_send())
    for j in range(n_tok):
        act_along(j, wait_send)
        for p in range(n_part):
            for k in range(2):
                grads_along(sources[j], p, k, wait_send)
    for groups in (from_chip, from_core, core_copies, first_copies, second_copies):
        for group in groups.values():
            for copy in group:
                copy.wait_send()
    for copy in firsts + a_core + list(weights.values()) + tok_copies:
        copy.wait_send()


def fused(n_part, scale, tokens, cotangent, frozen_in, frozen_out, in_a, in_b, out_a, out_b):
    n_tok, n_hid = lax.axis_size("tok"), lax.axis_size("hid")
    n_chip = n_hid // 2
    rows, cols = tokens.shape
    count, features = rows * n_tok, cols * n_hid
    width = frozen_in.shape[1] // n_tok
    part_width = width // n_part
    rank = in_a.shape[1]
    sems = pltpu.SemaphoreType.DMA
    vmem = pl.BlockSpec(memory_space=pltpu.VMEM)
    whole = pl.BlockSpec(memory_space=pl.ANY)
    arguments = (tokens, cotangent, frozen_in, frozen_out, in_a, in_b, out_a, out_b)
    return pl.pallas_call(
        functools.partial(fused_kernel, n_tok, n_hid, n_part, scale),
        out_shape=(
            jax.ShapeDtypeStruct((rows, cols), F32),
            jax.ShapeDtypeStruct((2 * rank, cols), F32),
            jax.ShapeDtypeStruct((n_tok * width, rank), BF16),
            jax.ShapeDtypeStruct((rank, n_tok * width), BF16),
        ),
        in_specs=[whole] * 8,
        out_specs=(vmem,) * 4,
        scratch_shapes=[
            pltpu.VMEM((count, features), BF16),
            pltpu.VMEM((count, features), BF16),
            pltpu.VMEM((features, width), BF16),
            pltpu.VMEM((width, features), BF16),
            pltpu.VMEM((features, rank), BF16),
            pltpu.VMEM((rank, features), BF16),
            pltpu.VMEM((rank, width), BF16),
            pltpu.VMEM((width, rank), BF16),
            pltpu.VMEM((2 * rank, width), BF16),
            pltpu.VMEM((width, 2 * rank), BF16),
            pltpu.VMEM((features, 2 * rank), BF16),
            pltpu.VMEM((count, 2 * rank), BF16),
            pltpu.VMEM((count, 2 * rank), BF16),
            pltpu.VMEM((count, 2 * rank), BF16),
            pltpu.VMEM((rows, part_width), F32),
            pltpu.VMEM((count, part_width), F32),
            pltpu.VMEM((rows, part_width), BF16),
            pltpu.VMEM((rows, part_width), BF16),
            pltpu.VMEM((count, features), F32),
            pltpu.VMEM((count, rank), F32),
            pltpu.VMEM((count, rank), F32),
            pltpu.VMEM((n_part, part_width, 2 * rank), F32),
            pltpu.VMEM((n_part, 2 * rank, part_width), F32),
            pltpu.VMEM((2, rank, features), F32),
            pltpu.VMEM((n_tok, n_chip, rows, cols), F32),
            pltpu.VMEM((2, n_chip, rank, cols), F32),
            pltpu.VMEM((n_tok, rows, cols), F32),
            pltpu.VMEM((2, rank, cols), F32),
            pltpu.VMEM((n_tok, 2, rows // 2, cols), F32),
            pltpu.VMEM((2, 2, rank // 2, cols), F32),
            pltpu.VMEM((n_tok, 2, 2, rows // 2, cols), BF16),
            pltpu.VMEM((2, 2, 2, rank // 2, cols), BF16),
            pltpu.VMEM((n_tok, 2, 2, rows // 2, cols), BF16),
            pltpu.VMEM((2, 2, 2, rank // 2, cols), BF16),
            pltpu.VMEM((n_tok, 2, rows // 2, cols), BF16),
            pltpu.VMEM((2, 2, rank // 2, cols), BF16),
            pltpu.VMEM((n_tok, 2, rows // 2, cols), BF16),
            pltpu.VMEM((2, 2, rank // 2, cols), BF16),
            pltpu.VMEM((n_tok - 1, rows, cols), BF16),
            pltpu.VMEM((2, n_tok, rows, cols), BF16),
            pltpu.VMEM((2, n_tok, rank, cols), BF16),
            sems((2, n_tok, 2)),
            sems((n_tok, 2)),
            sems((2, n_tok, n_chip - 1, 2)),
            sems((2, n_tok, n_chip, 2)),
            sems((2, n_chip - 1)),
            sems((2, n_chip)),
            sems((2, n_tok - 1, n_part, 2)),
            sems((6 + 2 * n_part,)),
            sems((2, n_tok + 2, n_chip)),
            sems((2, n_tok + 2, 2)),
            sems((2, n_tok + 2, 2)),
            sems((2, n_tok - 1)),
            sems((2, n_tok)),
            sems((2, n_tok - 1, 2)),
            sems((2, n_tok, n_part, 2)),
            sems((n_tok, n_part, 2)),
        ],
        compiler_params=pltpu.CompilerParams(
            collective_id=1, has_side_effects=True, vmem_limit_bytes=52 * 1024 * 1024
        ),
    )(*(pltpu.with_memory_space_constraint(array, pltpu.HBM) for array in arguments))


def finish_kernel(dx, terms, oa, ib, dx_out, in_a_out, ib_out, oa_out, out_b_out):
    rank = in_a_out.shape[1]
    ib_out[...] = ib[...].astype(F32)
    oa_out[...] = oa[...].astype(F32)
    dx_out[...] = dx[...]
    in_a_out[...] = terms[rank:, :].T
    out_b_out[...] = terms[:rank, :]


def local(tokens, cotangent, frozen_in, frozen_out, in_a, in_b, out_a, out_b):
    count = tokens.shape[0] * lax.axis_size("tok")
    scale = ADAPTER_SCALE / math.sqrt(count)
    dx, terms, oa, ib = fused(
        2, scale, tokens, cotangent, frozen_in, frozen_out, in_a, in_b, out_a, out_b
    )
    rank, cols = in_a.shape[1], tokens.shape[1]
    vmem = pl.BlockSpec(memory_space=pltpu.VMEM)
    return pl.pallas_call(
        finish_kernel,
        out_shape=(
            jax.ShapeDtypeStruct(dx.shape, F32),
            jax.ShapeDtypeStruct((cols, rank), F32),
            jax.ShapeDtypeStruct(ib.shape, F32),
            jax.ShapeDtypeStruct(oa.shape, F32),
            jax.ShapeDtypeStruct((rank, cols), F32),
        ),
        in_specs=[vmem] * 4,
        out_specs=(vmem,) * 5,
        compiler_params=pltpu.CompilerParams(vmem_limit_bytes=16 * 1024 * 1024),
    )(dx, terms, oa, ib)


def local_by_rows(
    tokens,
    cotangent,
    frozen_in,
    frozen_out,
    input_adapter_first,
    input_adapter_second,
    adapter_out_a,
    adapter_out_b,
):
    highest_precision = lax.Precision.HIGHEST
    device_local_rows = tokens.shape[0]
    rank_width = input_adapter_second.shape[0]
    gradient_scale = ADAPTER_SCALE / math.sqrt(device_local_rows * lax.axis_size("tok"))
    full_tokens, full_cotan = (
        lax.all_gather(tokens, "hid", axis=1, tiled=True),
        lax.all_gather(cotangent, "hid", axis=1, tiled=True),
    )
    in_rows = lax.all_gather(frozen_in, "tok", axis=0, tiled=True)
    in_a_full = lax.all_gather(input_adapter_first, "hid", axis=0, tiled=True)
    lowrank_input = jnp.dot(full_tokens, in_a_full, preferred_element_type=jnp.float32)
    second_float = input_adapter_second.astype(jnp.float32)
    out_a_float = adapter_out_a.astype(jnp.float32)
    pre_activation = jnp.dot(
        full_tokens, in_rows, preferred_element_type=jnp.float32
    ) + ADAPTER_SCALE * jnp.dot(lowrank_input, second_float, precision=highest_precision)
    value_out, slopes = gelu_pair(pre_activation)
    hidden_act = value_out.astype(jnp.bfloat16)
    backward_lowrank = jnp.einsum(
        "td,rd->tr", full_cotan, adapter_out_b, preferred_element_type=jnp.float32
    )
    rank_out = jnp.dot(hidden_act, adapter_out_a, preferred_element_type=jnp.float32)
    dense_backward = jnp.einsum(
        "td,fd->tf",
        full_cotan,
        lax.all_gather(frozen_out, "tok", axis=1, tiled=True),
        preferred_element_type=jnp.float32,
    )
    dense_backward = dense_backward + ADAPTER_SCALE * jnp.dot(
        backward_lowrank, out_a_float.T, precision=highest_precision
    )
    grad_pre = (dense_backward * slopes).astype(jnp.bfloat16)
    rank_backward = jnp.einsum(
        "tf,rf->tr", grad_pre, input_adapter_second, preferred_element_type=jnp.float32
    )
    dense_in = jnp.einsum("tf,df->td", grad_pre, in_rows, preferred_element_type=jnp.float32)
    grad_out_a = gradient_scale * jnp.dot(
        hidden_act.astype(jnp.float32).T, backward_lowrank, precision=highest_precision
    )
    grad_in_b = gradient_scale * jnp.dot(
        lowrank_input.T, grad_pre.astype(jnp.float32), precision=highest_precision
    )
    in_a_float = in_a_full.astype(jnp.float32)
    dx_term = dense_in + ADAPTER_SCALE * jnp.dot(
        rank_backward, in_a_float.T, precision=highest_precision
    )
    out_term = jnp.dot(rank_out.T, full_cotan.astype(jnp.float32), precision=highest_precision)
    in_term = jnp.dot(rank_backward.T, full_tokens.astype(jnp.float32), precision=highest_precision)
    rank_terms = jnp.concatenate([out_term, in_term], axis=0)
    input_gradient, rank_local = (
        lax.psum_scatter(dx_term, "hid", scatter_dimension=1, tiled=True),
        lax.psum_scatter(rank_terms, "hid", scatter_dimension=1, tiled=True),
    )
    grad_out_a, grad_in_b, rank_total = lax.psum((grad_out_a, grad_in_b, rank_local), "tok")
    grad_out_b = gradient_scale * rank_total[:rank_width]
    grad_in_a = gradient_scale * rank_total[rank_width:].T
    return (input_gradient, grad_in_a, grad_in_b, grad_out_a, grad_out_b)


def solution(mesh):
    in_specs = (
        P("tok", "hid"),
        P("tok", "hid"),
        P("tok", "hid"),
        P("hid", "tok"),
        P("hid", None),
        P(None, "hid"),
        P("hid", None),
        P(),
    )
    out_specs = (P("tok", "hid"), P("hid", None), P(None, "hid"), P("hid", None), P(None, "hid"))
    def body(*arrays):
        share = arrays[2].shape[1] // lax.axis_size("tok")
        wide = share % 256 == 0 and lax.axis_size("tok") > 2
        wide = wide and lax.axis_size("hid") == 2 ** len(("y", "x", "core"))
        return local(*arrays) if wide else local_by_rows(*arrays)

    return jax.shard_map(body, mesh=mesh, in_specs=in_specs, out_specs=out_specs, check_vma=False)
```

```python
import functools
import math

import jax
import jax.numpy as jnp
from jax import lax
from jax.experimental import pallas as pl
from jax.experimental.pallas import tpu as pltpu
from jax.sharding import PartitionSpec as P

ADAPTER_SCALE = 0.5
GELU_K = 0.7978845608
GELU_C = 0.044715
F32 = jnp.float32
BF16 = jnp.bfloat16


def gelu_pair(pre_activation):
    tangent = jnp.tanh(
        GELU_K * (pre_activation + GELU_C * pre_activation * pre_activation * pre_activation)
    )
    value_out = 0.5 * pre_activation * (1.0 + tangent)
    slopes = 0.5 * (1.0 + tangent) + 0.5 * pre_activation * (1.0 - tangent * tangent) * GELU_K * (
        1.0 + 3.0 * GELU_C * pre_activation * pre_activation
    )
    return (value_out, slopes)


def dot(left, right, dims):
    return lax.dot_general(left, right, (dims, ((), ())), preferred_element_type=F32)


def nn(left, right):
    return dot(left, right, ((1,), (0,)))


def nt(left, right):
    return dot(left, right, ((1,), (1,)))


def tn(left, right):
    return dot(left, right, ((0,), (0,)))


def split(value):
    high = value.astype(BF16)
    return high, (value - high.astype(F32)).astype(BF16)


def fused_kernel(
    n_tok, n_hid, n_part, scale,
    tokens, cotangent, w_in, w_out, in_a, in_b, out_a, out_b,
    dx_out, terms_out, oa_all, ib_all,
    x, c, full_in, full_out, full_a, b_mat, second, first, second2, first2, a2,
    low, back, pre_s, back_s, act_s, grad_s, dense, rank_out, rank_back, oa_acc, ib_acc, terms,
    core_d, core_t, kept_d, kept_t, pend_d, pend_t, one_send, one_send_t, one_recv, one_recv_t,
    two_send, two_send_t, two_recv, two_recv_t, line_send, line_recv, pair_recv, all_t,
    act_send, act_recv, chip_sem, core_sem, first_sem, first_core_sem, w_sem, own_sem,
    core_r_sem, one_sem, two_sem, line_sem, line_got, pair_sem, term_sem, grad_send, grad_recv,
):
    t, h = lax.axis_index("tok"), lax.axis_index("hid")
    n_chip = n_hid // 2
    chip, core = h // 2, h % 2
    rows, cols = tokens.shape
    depth = w_in.shape[0]
    width = full_in.shape[1]
    part_width = width // n_part
    rank = full_a.shape[1]

    def remote(source, target, send, recv, where):
        return pltpu.make_async_remote_copy(
            src_ref=source, dst_ref=target, send_sem=send, recv_sem=recv,
            device_id=where, device_id_type=pl.DeviceIdType.MESH,
        )

    def begin(*arguments):
        copy = remote(*arguments)
        copy.start()
        return copy

    at_x, at_y = chip % 2, chip // 2
    square = [
        2 * ((at_y + e // 2) % 2) + (at_x + e % 2) % 2 for e in range(n_chip)
    ]
    sibling = (t, 2 * chip + 1 - core)
    chips = [(t, 2 * ((chip + e) % n_chip) + core) for e in range(n_chip)]
    toks = [((t + d) % n_tok, h) for d in range(n_tok)]
    barrier = pltpu.get_barrier_semaphore()
    for where in [sibling] + chips[1:] + toks[1:]:
        pl.semaphore_signal(barrier, inc=1, device_id=where, device_id_type=pl.DeviceIdType.MESH)
    pl.semaphore_wait(barrier, n_chip + n_tok - 1)

    orders = [
        sorted(range(n_tok), key=lambda s: (abs(s - k), -abs(2 * s - n_tok + 1)))
        for k in range(n_tok)
    ]
    sources = [t]
    for j in range(1, n_tok):
        source = jnp.int32(orders[0][j])
        for k in range(1, n_tok):
            source = jnp.where(t == k, jnp.int32(orders[k][j]), source)
        sources.append(source)

    def row_at(source):
        return pl.multiple_of(source * rows, rows)

    def part(array, source, e, i=None):
        at_col = pl.multiple_of((2 * square[e] + core) * cols, cols)
        count = rows if i is None else rows // 2
        at_row = pl.multiple_of(row_at(source) + (i or 0) * count, count)
        return array.at[pl.ds(at_row, count), pl.ds(at_col, cols)]

    def along(source, blocks, send, recv, act):
        @pl.when((source <= t) & (t + 1 < n_tok))
        def _():
            for k, (block, target) in enumerate(blocks):
                act(remote(block, target, send(0, source, k), recv(source, k), (t + 1, h)))

        @pl.when((source >= t) & (t > 0))
        def _():
            for k, (block, target) in enumerate(blocks):
                act(remote(block, target, send(1, source, k), recv(source, k), (t - 1, h)))

    def start(copy):
        copy.start()

    def wait_send(copy):
        copy.wait_send()

    def act_blocks(j):
        source = sources[j]
        mine = (tokens, cotangent)
        return [
            (mine[k] if j == 0 else part(array, source, 0), part(array, source, 0))
            for k, array in enumerate((x, c))
        ]

    def act_along(j, act):
        along(
            sources[j], act_blocks(j),
            lambda way, source, k: act_send.at[way, source, k],
            lambda source, k: act_recv.at[source, k], act,
        )

    from_chip, from_core = {}, {}

    def to_chips(j):
        for e in (1, 2):
            from_chip[j, e] = [
                begin(
                    block, target, chip_sem.at[0, j, e - 1, k], chip_sem.at[1, j, e - 1, k],
                    (t, 2 * square[e] + core),
                )
                for k, (block, target) in enumerate(act_blocks(j))
            ]

    def to_core(j, e):
        if e == 0:
            blocks = act_blocks(j)
        else:
            blocks = [(part(array, sources[j], e),) * 2 for array in (x, c)]
        from_core[j, e] = [
            begin(block, target, core_sem.at[0, j, e, k], core_sem.at[1, j, e, k], sibling)
            for k, (block, target) in enumerate(blocks)
        ]

    def first_part(e):
        at = pl.multiple_of((2 * ((chip + n_chip - e) % n_chip) + core) * cols, cols)
        return full_a.at[pl.ds(at, cols), :]

    weights = {}
    depths = pl.ds(pl.multiple_of(t * depth, depth), depth)

    def weight_blocks(d, p):
        at = pl.multiple_of(((t + d) % n_tok) * width + p * part_width, part_width)
        here = pl.ds(p * part_width, part_width)
        return [
            (w_in.at[:, pl.ds(at, part_width)], full_in.at[depths, here]),
            (w_out.at[pl.ds(at, part_width), :], full_out.at[here, depths]),
        ]

    def send_weight(d, p, k):
        block, target = weight_blocks(d, p)[k]
        weights[d, p, k] = begin(
            block, target, w_sem.at[0, d - 1, p, k], w_sem.at[1, d - 1, p, k], toks[d]
        )

    act_along(0, start)
    to_chips(0)
    firsts = [
        begin(in_a, first_part(0), first_sem.at[0, e - 1], first_sem.at[1, e - 1], chips[e])
        for e in range(1, n_chip)
    ]
    to_core(0, 0)
    a_core = [begin(in_a, first_part(0), first_core_sem.at[0, 0], first_core_sem.at[1, 0], sibling)]
    pieces = [(d, p, k) for p in range(n_part) for k in range(2) for d in range(1, n_tok)]
    pieces = [piece for piece in pieces if piece[1:] != (0, 0) or piece[0] in (1, n_tok - 1)]
    rest = [(d, 0, 0) for d in range(2, n_tok - 1)] + pieces[min(2, n_tok - 1):]
    for piece in pieces[:min(2, n_tok - 1)]:
        send_weight(*piece)
    at = pl.multiple_of(t * width, width)
    own = [(block, target) for block, target in act_blocks(0)]
    own += [(in_a, first_part(0)), (out_b, b_mat)]
    own += [(in_b.at[:, pl.ds(at, width)], second), (out_a.at[pl.ds(at, width), :], first)]
    for p in range(n_part):
        own += weight_blocks(0, p)
    own = [
        pltpu.make_async_copy(block, target, own_sem.at[k])
        for k, (block, target) in enumerate(own)
    ]
    for copy in own:
        copy.start()

    def arrive(j):
        for k, (block, target) in enumerate(act_blocks(j)):
            remote(
                target, target, act_send.at[0, sources[j], k], act_recv.at[sources[j], k], sibling
            ).wait_recv()
        act_along(j, start)
        to_chips(j)
        to_core(j, 0)

    def near(j):
        for e in (1, 2):
            for copy in from_chip[j, e]:
                copy.wait_recv()
            from_chip[j, 2 + e] = [
                begin(
                    part(array, sources[j], e, e - 1), part(array, sources[j], e, e - 1),
                    chip_sem.at[0, j, 1 + e, k], chip_sem.at[1, j, 1 + e, k],
                    (t, 2 * square[3 - e] + core),
                )
                for k, array in enumerate((x, c))
            ]
            to_core(j, e)

    def far(j):
        for e in (3, 4):
            for copy in from_chip[j, e]:
                copy.wait_recv()
        to_core(j, 3)

    def complete(j):
        for e in range(n_chip):
            for copy in from_core[j, e]:
                copy.wait_recv()

    def ranks(source):
        here = pl.ds(row_at(source), rows)
        high, rest = split(nn(x[here, :], full_a[...]))
        low[here, :rank] = high
        low[here, rank:] = rest
        high, rest = split(nt(c[here, :], b_mat[...]))
        back[here, :rank] = high
        back[here, rank:] = rest

    def hidden(p, source, begun):
        here = pl.ds(row_at(source), rows)
        those = slice(p * part_width, (p + 1) * part_width)
        pre_s[...] = nn(x[here, :], full_in[:, those]) + nn(low[here, :], second2[:, those])
        back_s[...] = nt(c[here, :], full_out[those, :]) + nt(back[here, :], first2[those, :])
        step = rows // 8
        for at in range(0, rows, step):
            some = slice(at, at + step)
            value_out, slopes = gelu_pair(pre_s[some, :])
            act_s[some, :] = value_out.astype(BF16)
            grad_s[some, :] = (back_s[some, :] * slopes).astype(BF16)
        act, grad = act_s[...], grad_s[...]
        oa_new, ib_new = tn(act, back[here, :]), tn(low[here, :], grad)
        out_new, back_new = nn(act, first[those, :]), nt(grad, second[:, those])
        if begun:
            oa_acc[p] += oa_new
            ib_acc[p] += ib_new
        else:
            oa_acc[p] = oa_new
            ib_acc[p] = ib_new
        if p == 0:
            rank_out[here, :] = out_new
            rank_back[here, :] = back_new
        else:
            rank_out[here, :] += out_new
            rank_back[here, :] += back_new
        if p < n_part - 1:
            if p == 0:
                dense[here, :] = nt(grad, full_in[:, those])
            else:
                dense[here, :] += nt(grad, full_in[:, those])
            return
        high, rest = split(rank_back[here, :])
        low[here, :rank] = high
        low[here, rank:] = rest
        high, rest = split(rank_out[here, :])
        back[here, :rank] = high
        back[here, rank:] = rest
        value = nt(grad, full_in[:, those]) + nt(low[here, :], a2[...])
        dense[here, :] = dense[here, :] + value if n_part > 1 else value

    def prepare():
        for e in range(1, n_chip):
            firsts[e - 1].wait_recv()
            a_core.append(begin(
                first_part(e), first_part(e), first_core_sem.at[0, e], first_core_sem.at[1, e],
                sibling,
            ))
        for copy in own:
            copy.wait()
        for copy in a_core:
            copy.wait_recv()
        half = (ADAPTER_SCALE * second[...].astype(F32)).astype(BF16)
        second2[:rank, :] = half
        second2[rank:, :] = half
        half = (ADAPTER_SCALE * first[...].astype(F32)).astype(BF16)
        first2[:, :rank] = half
        first2[:, rank:] = half
        half = (ADAPTER_SCALE * full_a[...].astype(F32)).astype(BF16)
        a2[:, :rank] = half
        a2[:, rank:] = half

    early = len(pieces) // 3

    def more(j):
        for piece in {2: rest[:early], n_tok - 1: rest[early:]}.get(j, []):
            send_weight(*piece)

    for j in range(1, n_tok - 1):
        arrive(j)
        more(j)
    near(0)
    arrive(n_tok - 1)
    more(n_tok - 1)
    far(0)
    near(1)
    complete(0)
    prepare()
    ranks(sources[0])
    for j in range(1, n_tok - 1):
        far(j)
        near(j + 1)
        complete(j)
        ranks(sources[j])
    far(n_tok - 1)

    def wait_weights(p):
        for d in range(1, n_tok):
            for k in range(2):
                weights[d, p, k].wait_recv()

    def oa_blocks(source, p):
        at = pl.multiple_of(source * width + p * part_width, part_width)
        oa_at, ib_at = oa_all.at[pl.ds(at, part_width), :], ib_all.at[:, pl.ds(at, part_width)]
        return [(oa_at, oa_at), (ib_at, ib_at)]

    def grads_along(source, p, act):
        along(
            source, oa_blocks(source, p),
            lambda way, source, k: grad_send.at[way, source, p, k],
            lambda source, k: grad_recv.at[source, p, k], act,
        )

    def finish_grads(p):
        at = pl.multiple_of(t * width + p * part_width, part_width)
        oa = oa_acc[p]
        oa_all[pl.ds(at, part_width), :] = (scale * (oa[:, :rank] + oa[:, rank:])).astype(BF16)
        ib = ib_acc[p]
        ib_all[:, pl.ds(at, part_width)] = (scale * (ib[:rank] + ib[rank:])).astype(BF16)
        grads_along(t, p, start)

    def grad_hop(s, p):
        def relay(source):
            blocks = oa_blocks(source, p)
            for k, (block, target) in enumerate(blocks):
                remote(
                    target, target, grad_send.at[0, source, p, k], grad_recv.at[source, p, k],
                    sibling,
                ).wait_recv()
            grads_along(source, p, start)

        pl.when(t >= s + 1)(lambda: relay(t - 1 - s))
        pl.when(t + 1 + s < n_tok)(lambda: relay(t + 1 + s))

    complete(n_tok - 1)
    ranks(sources[n_tok - 1])
    for p in range(n_part - 1):
        wait_weights(p)
        for j in range(n_tok):
            hidden(p, sources[j], j > 0)
        finish_grads(p)
    last = n_part - 1
    wait_weights(last)

    core_copies, first_copies, second_copies, tok_copies = {}, {}, {}, []
    blocks = [sources[n_tok - 1 - q] for q in range(n_tok)]

    def columns(e, parity):
        return pl.ds(pl.multiple_of((2 * square[e] + parity) * cols, cols), cols)

    def here(q):
        return pl.ds(row_at(blocks[q]), rows)

    def buffers(q):
        if q == n_tok:
            return core_t, kept_t, pend_t, one_send_t, one_recv_t, two_send_t, two_recv_t
        return tuple(
            array.at[q] for array in (core_d, kept_d, pend_d, one_send, one_recv, two_send, two_recv)
        )

    def to_sibling(q):
        got = buffers(q)[0]
        core_copies[q] = []
        for e in range(n_chip):
            those = columns(e, 1 - core)
            source = terms.at[:, those] if q == n_tok else dense.at[here(q), those]
            core_copies[q].append(
                begin(source, got.at[e], core_r_sem.at[0, q, e], core_r_sem.at[1, q, e], sibling)
            )

    def over_core(q):
        got, kept, pend, sent, recv = buffers(q)[:5]
        half = kept.shape[0] // 2
        first_copies[q] = []
        for e in (3, 1, 2, 0):
            core_copies[q][e].wait_recv()
            those = columns(e, core)
            mine = terms[:, those] if q == n_tok else dense[here(q), those]
            value = mine + got[e]
            for i in range(2):
                some = value[i * half:(i + 1) * half]
                if e == 0:
                    kept[i * half:(i + 1) * half, :] = some
                elif e == 2 - i:
                    pend[i] = some
                else:
                    sent[i, 0 if e == 1 + i else 1] = some.astype(BF16)
        for i in range(2):
            first_copies[q].append(begin(
                sent.at[i], recv.at[i], one_sem.at[0, q, i], one_sem.at[1, q, i],
                (t, 2 * square[1 + i] + core),
            ))

    def over_first(q):
        _, kept, pend, _, recv, sent, second_recv = buffers(q)
        half = kept.shape[0] // 2
        second_copies[q] = []
        for i in range(2):
            first_copies[q][i].wait_recv()
            sent[i] = (pend[i] + recv[i, 1].astype(F32)).astype(BF16)
            second_copies[q].append(begin(
                sent.at[i], second_recv.at[i], two_sem.at[0, q, i], two_sem.at[1, q, i],
                (t, 2 * square[2 - i] + core),
            ))
            some = slice(i * half, (i + 1) * half)
            kept[some, :] = kept[some, :] + recv[i, 0].astype(F32)

    def over_second(q):
        _, kept, _, _, _, _, recv = buffers(q)
        half = kept.shape[0] // 2
        for i in range(2):
            second_copies[q][i].wait_recv()
            some = slice(i * half, (i + 1) * half)
            kept[some, :] = kept[some, :] + recv[i].astype(F32)

    at_end = (t == 0) | (t == n_tok - 1)

    def pair_copy():
        return remote(
            line_send.at[0], pair_recv, pair_sem.at[0], pair_sem.at[1],
            (jnp.where(t == 0, 1, n_tok - 2), h),
        )

    def line_copy(q):
        return remote(
            line_send.at[q], line_recv.at[t], line_sem.at[q], line_got.at[t], (blocks[q], h)
        )

    def send_line(q):
        line_send[q] = kept_d[q].astype(BF16)
        line_copy(q).start()

    def start_pair():
        def send():
            line_send[0] = kept_d[0].astype(BF16)
            pair_copy().start()

        pl.when(at_end)(send)

    def over_pair():
        def add_and_send():
            pair_copy().wait_recv()
            kept_d[0] = kept_d[0] + pair_recv[...].astype(F32)
            send_line(0)

        pl.when(jnp.logical_not(at_end))(add_and_send)

    def add_line(source):
        def add():
            remote(
                line_recv.at[source], line_recv.at[source], line_sem.at[0], line_got.at[source],
                sibling,
            ).wait_recv()
            kept_d[n_tok - 1] = kept_d[n_tok - 1] + line_recv[source].astype(F32)

        far = (t + source == n_tok - 1) & at_end
        pl.when((t != source) & jnp.logical_not(far))(add)

    def share_terms():
        all_t[t] = kept_t[...].astype(BF16)
        for k in range(1, n_tok):
            tok_copies.append(begin(
                all_t.at[t], all_t.at[t], term_sem.at[0, k - 1], term_sem.at[1, k - 1], toks[k]
            ))

    def sum_terms():
        out_cols = x.shape[1] // n_chip
        for at in range(0, x.shape[1], out_cols):
            those = slice(at, at + out_cols)
            value = tn(back[...], c[:, those])
            terms[:rank, those] = scale * (value[:rank] + value[rank:])
            value = tn(low[...], x[:, those])
            terms[rank:, those] = scale * (value[:rank] + value[rank:])

    def hop(s):
        for p in range(last):
            grad_hop(s, p)

    final = n_tok - 1
    for q in range(n_tok):
        hidden(last, blocks[q], q > 0)
        to_sibling(q)
        if q >= 1:
            over_core(q - 1)
        if q == 2:
            hop(0)
    finish_grads(last)
    for q in range(final - 1):
        over_first(q)
    sum_terms()
    to_sibling(n_tok)
    hop(1)
    over_core(n_tok)
    over_first(final - 1)
    over_second(0)
    start_pair()
    grad_hop(0, last)
    for q in range(1, final - 1):
        over_second(q)
        send_line(q)
    over_first(n_tok)
    over_core(final)
    over_pair()
    over_second(final - 1)
    send_line(final - 1)
    over_second(n_tok)
    share_terms()
    if n_tok > 2:
        grad_hop(1, last)
    over_first(final)
    for s in range(2, n_tok - 1):
        hop(s)
    over_second(final)
    for s in range(2, n_tok - 1):
        grad_hop(s, last)
    for source in range(n_tok):
        add_line(source)
    dx_out[...] = kept_d[final]
    for copy in tok_copies:
        copy.wait_recv()
    value = all_t[0].astype(F32)
    for k in range(1, n_tok):
        value = value + all_t[k].astype(F32)
    terms_out[...] = value
    pl.when(at_end)(lambda: pair_copy().wait_send())
    pl.when(jnp.logical_not(at_end))(lambda: line_copy(0).wait_send())
    for q in range(1, final):
        line_copy(q).wait_send()
    for j in range(n_tok):
        act_along(j, wait_send)
        for p in range(n_part):
            grads_along(sources[j], p, wait_send)
    for groups in (from_chip, from_core, core_copies, first_copies, second_copies):
        for group in groups.values():
            for copy in group:
                copy.wait_send()
    for copy in firsts + a_core + list(weights.values()) + tok_copies:
        copy.wait_send()


def fused(n_part, scale, tokens, cotangent, frozen_in, frozen_out, in_a, in_b, out_a, out_b):
    n_tok, n_hid = lax.axis_size("tok"), lax.axis_size("hid")
    n_chip = n_hid // 2
    rows, cols = tokens.shape
    count, features = rows * n_tok, cols * n_hid
    width = frozen_in.shape[1] // n_tok
    part_width = width // n_part
    rank = in_a.shape[1]
    sems = pltpu.SemaphoreType.DMA
    vmem = pl.BlockSpec(memory_space=pltpu.VMEM)
    whole = pl.BlockSpec(memory_space=pl.ANY)
    arguments = (tokens, cotangent, frozen_in, frozen_out, in_a, in_b, out_a, out_b)
    return pl.pallas_call(
        functools.partial(fused_kernel, n_tok, n_hid, n_part, scale),
        out_shape=(
            jax.ShapeDtypeStruct((rows, cols), F32),
            jax.ShapeDtypeStruct((2 * rank, cols), F32),
            jax.ShapeDtypeStruct((n_tok * width, rank), BF16),
            jax.ShapeDtypeStruct((rank, n_tok * width), BF16),
        ),
        in_specs=[whole] * 8,
        out_specs=(vmem,) * 4,
        scratch_shapes=[
            pltpu.VMEM((count, features), BF16),
            pltpu.VMEM((count, features), BF16),
            pltpu.VMEM((features, width), BF16),
            pltpu.VMEM((width, features), BF16),
            pltpu.VMEM((features, rank), BF16),
            pltpu.VMEM((rank, features), BF16),
            pltpu.VMEM((rank, width), BF16),
            pltpu.VMEM((width, rank), BF16),
            pltpu.VMEM((2 * rank, width), BF16),
            pltpu.VMEM((width, 2 * rank), BF16),
            pltpu.VMEM((features, 2 * rank), BF16),
            pltpu.VMEM((count, 2 * rank), BF16),
            pltpu.VMEM((count, 2 * rank), BF16),
            pltpu.VMEM((rows, part_width), F32),
            pltpu.VMEM((rows, part_width), F32),
            pltpu.VMEM((rows, part_width), BF16),
            pltpu.VMEM((rows, part_width), BF16),
            pltpu.VMEM((count, features), F32),
            pltpu.VMEM((count, rank), F32),
            pltpu.VMEM((count, rank), F32),
            pltpu.VMEM((n_part, part_width, 2 * rank), F32),
            pltpu.VMEM((n_part, 2 * rank, part_width), F32),
            pltpu.VMEM((2 * rank, features), F32),
            pltpu.VMEM((n_tok, n_chip, rows, cols), F32),
            pltpu.VMEM((n_chip, 2 * rank, cols), F32),
            pltpu.VMEM((n_tok, rows, cols), F32),
            pltpu.VMEM((2 * rank, cols), F32),
            pltpu.VMEM((n_tok, 2, rows // 2, cols), F32),
            pltpu.VMEM((2, rank, cols), F32),
            pltpu.VMEM((n_tok, 2, 2, rows // 2, cols), BF16),
            pltpu.VMEM((2, 2, rank, cols), BF16),
            pltpu.VMEM((n_tok, 2, 2, rows // 2, cols), BF16),
            pltpu.VMEM((2, 2, rank, cols), BF16),
            pltpu.VMEM((n_tok, 2, rows // 2, cols), BF16),
            pltpu.VMEM((2, rank, cols), BF16),
            pltpu.VMEM((n_tok, 2, rows // 2, cols), BF16),
            pltpu.VMEM((2, rank, cols), BF16),
            pltpu.VMEM((n_tok - 1, rows, cols), BF16),
            pltpu.VMEM((n_tok, rows, cols), BF16),
            pltpu.VMEM((rows, cols), BF16),
            pltpu.VMEM((n_tok, 2 * rank, cols), BF16),
            sems((2, n_tok, 2)),
            sems((n_tok, 2)),
            sems((2, n_tok, 4, 2)),
            sems((2, n_tok, n_chip, 2)),
            sems((2, n_chip - 1)),
            sems((2, n_chip)),
            sems((2, n_tok - 1, n_part, 2)),
            sems((6 + 2 * n_part,)),
            sems((2, n_tok + 1, n_chip)),
            sems((2, n_tok + 1, 2)),
            sems((2, n_tok + 1, 2)),
            sems((n_tok - 1,)),
            sems((n_tok,)),
            sems((2,)),
            sems((2, n_tok - 1)),
            sems((2, n_tok, n_part, 2)),
            sems((n_tok, n_part, 2)),
        ],
        compiler_params=pltpu.CompilerParams(
            collective_id=1, has_side_effects=True, vmem_limit_bytes=52 * 1024 * 1024
        ),
    )(*(pltpu.with_memory_space_constraint(array, pltpu.HBM) for array in arguments))


def finish_kernel(dx, terms, oa, ib, dx_out, in_a_out, ib_out, oa_out, out_b_out):
    rank = in_a_out.shape[1]
    ib_out[...] = ib[...].astype(F32)
    oa_out[...] = oa[...].astype(F32)
    dx_out[...] = dx[...]
    in_a_out[...] = terms[rank:, :].T
    out_b_out[...] = terms[:rank, :]


def local(tokens, cotangent, frozen_in, frozen_out, in_a, in_b, out_a, out_b):
    count = tokens.shape[0] * lax.axis_size("tok")
    scale = ADAPTER_SCALE / math.sqrt(count)
    dx, terms, oa, ib = fused(
        2, scale, tokens, cotangent, frozen_in, frozen_out, in_a, in_b, out_a, out_b
    )
    rank, cols = in_a.shape[1], tokens.shape[1]
    vmem = pl.BlockSpec(memory_space=pltpu.VMEM)
    return pl.pallas_call(
        finish_kernel,
        out_shape=(
            jax.ShapeDtypeStruct(dx.shape, F32),
            jax.ShapeDtypeStruct((cols, rank), F32),
            jax.ShapeDtypeStruct(ib.shape, F32),
            jax.ShapeDtypeStruct(oa.shape, F32),
            jax.ShapeDtypeStruct((rank, cols), F32),
        ),
        in_specs=[vmem] * 4,
        out_specs=(vmem,) * 5,
        compiler_params=pltpu.CompilerParams(vmem_limit_bytes=16 * 1024 * 1024),
    )(dx, terms, oa, ib)


def local_by_rows(
    tokens,
    cotangent,
    frozen_in,
    frozen_out,
    input_adapter_first,
    input_adapter_second,
    adapter_out_a,
    adapter_out_b,
):
    highest_precision = lax.Precision.HIGHEST
    device_local_rows = tokens.shape[0]
    rank_width = input_adapter_second.shape[0]
    gradient_scale = ADAPTER_SCALE / math.sqrt(device_local_rows * lax.axis_size("tok"))
    full_tokens, full_cotan = (
        lax.all_gather(tokens, "hid", axis=1, tiled=True),
        lax.all_gather(cotangent, "hid", axis=1, tiled=True),
    )
    in_rows = lax.all_gather(frozen_in, "tok", axis=0, tiled=True)
    in_a_full = lax.all_gather(input_adapter_first, "hid", axis=0, tiled=True)
    lowrank_input = jnp.dot(full_tokens, in_a_full, preferred_element_type=jnp.float32)
    second_float = input_adapter_second.astype(jnp.float32)
    out_a_float = adapter_out_a.astype(jnp.float32)
    pre_activation = jnp.dot(
        full_tokens, in_rows, preferred_element_type=jnp.float32
    ) + ADAPTER_SCALE * jnp.dot(lowrank_input, second_float, precision=highest_precision)
    value_out, slopes = gelu_pair(pre_activation)
    hidden_act = value_out.astype(jnp.bfloat16)
    backward_lowrank = jnp.einsum(
        "td,rd->tr", full_cotan, adapter_out_b, preferred_element_type=jnp.float32
    )
    rank_out = jnp.dot(hidden_act, adapter_out_a, preferred_element_type=jnp.float32)
    dense_backward = jnp.einsum(
        "td,fd->tf",
        full_cotan,
        lax.all_gather(frozen_out, "tok", axis=1, tiled=True),
        preferred_element_type=jnp.float32,
    )
    dense_backward = dense_backward + ADAPTER_SCALE * jnp.dot(
        backward_lowrank, out_a_float.T, precision=highest_precision
    )
    grad_pre = (dense_backward * slopes).astype(jnp.bfloat16)
    rank_backward = jnp.einsum(
        "tf,rf->tr", grad_pre, input_adapter_second, preferred_element_type=jnp.float32
    )
    dense_in = jnp.einsum("tf,df->td", grad_pre, in_rows, preferred_element_type=jnp.float32)
    grad_out_a = gradient_scale * jnp.dot(
        hidden_act.astype(jnp.float32).T, backward_lowrank, precision=highest_precision
    )
    grad_in_b = gradient_scale * jnp.dot(
        lowrank_input.T, grad_pre.astype(jnp.float32), precision=highest_precision
    )
    in_a_float = in_a_full.astype(jnp.float32)
    dx_term = dense_in + ADAPTER_SCALE * jnp.dot(
        rank_backward, in_a_float.T, precision=highest_precision
    )
    out_term = jnp.dot(rank_out.T, full_cotan.astype(jnp.float32), precision=highest_precision)
    in_term = jnp.dot(rank_backward.T, full_tokens.astype(jnp.float32), precision=highest_precision)
    rank_terms = jnp.concatenate([out_term, in_term], axis=0)
    input_gradient, rank_local = (
        lax.psum_scatter(dx_term, "hid", scatter_dimension=1, tiled=True),
        lax.psum_scatter(rank_terms, "hid", scatter_dimension=1, tiled=True),
    )
    grad_out_a, grad_in_b, rank_total = lax.psum((grad_out_a, grad_in_b, rank_local), "tok")
    grad_out_b = gradient_scale * rank_total[:rank_width]
    grad_in_a = gradient_scale * rank_total[rank_width:].T
    return (input_gradient, grad_in_a, grad_in_b, grad_out_a, grad_out_b)


def solution(mesh):
    in_specs = (
        P("tok", "hid"),
        P("tok", "hid"),
        P("tok", "hid"),
        P("hid", "tok"),
        P("hid", None),
        P(None, "hid"),
        P("hid", None),
        P(),
    )
    out_specs = (P("tok", "hid"), P("hid", None), P(None, "hid"), P("hid", None), P(None, "hid"))
    def body(*arrays):
        share = arrays[2].shape[1] // lax.axis_size("tok")
        wide = share % 256 == 0 and lax.axis_size("tok") == lax.axis_size("hid") // 2
        wide = wide and lax.axis_size("hid") == 2 ** len(("y", "x", "core"))
        return local(*arrays) if wide else local_by_rows(*arrays)

    return jax.shard_map(body, mesh=mesh, in_specs=in_specs, out_specs=out_specs, check_vma=False)
```

```python
import functools
import math

import jax
import jax.numpy as jnp
from jax import lax
from jax.experimental import pallas as pl
from jax.experimental.pallas import tpu as pltpu
from jax.sharding import PartitionSpec as P

ADAPTER_SCALE = 0.5
GELU_K = 0.7978845608
GELU_C = 0.044715
F32 = jnp.float32
BF16 = jnp.bfloat16


def gelu_pair(pre_activation):
    tangent = jnp.tanh(
        GELU_K * (pre_activation + GELU_C * pre_activation * pre_activation * pre_activation)
    )
    value_out = 0.5 * pre_activation * (1.0 + tangent)
    slopes = 0.5 * (1.0 + tangent) + 0.5 * pre_activation * (1.0 - tangent * tangent) * GELU_K * (
        1.0 + 3.0 * GELU_C * pre_activation * pre_activation
    )
    return (value_out, slopes)


def dot(left, right, dims):
    return lax.dot_general(left, right, (dims, ((), ())), preferred_element_type=F32)


def nn(left, right):
    return dot(left, right, ((1,), (0,)))


def nt(left, right):
    return dot(left, right, ((1,), (1,)))


def tn(left, right):
    return dot(left, right, ((0,), (0,)))


def split(value):
    high = value.astype(BF16)
    return high, (value - high.astype(F32)).astype(BF16)


def fused_kernel(
    n_tok, n_hid, n_part, scale,
    tokens, cotangent, w_in, w_out, in_a, in_b, out_a, out_b,
    dx_out, terms_out, oa_all, ib_all,
    x, c, full_in, full_out, full_a, b_mat, second, first, second2, first2, a2,
    low, back, pre_s, back_s, act_s, grad_s, dense, rank_out, rank_back, oa_acc, ib_acc, terms,
    core_d, core_t, kept_d, kept_t, pend_d, pend_t, one_send, one_send_t, one_recv, one_recv_t,
    two_send, two_send_t, two_recv, two_recv_t, line_send, line_recv, all_t,
    act_send, act_recv, chip_sem, core_sem, first_sem, first_core_sem, w_sem, own_sem,
    core_r_sem, one_sem, two_sem, line_sem, line_got, term_sem, grad_send, grad_recv,
):
    t, h = lax.axis_index("tok"), lax.axis_index("hid")
    n_chip = n_hid // 2
    chip, core = h // 2, h % 2
    rows, cols = tokens.shape
    depth = w_in.shape[0]
    width = full_in.shape[1]
    part_width = width // n_part
    rank = full_a.shape[1]

    def remote(source, target, send, recv, where):
        return pltpu.make_async_remote_copy(
            src_ref=source, dst_ref=target, send_sem=send, recv_sem=recv,
            device_id=where, device_id_type=pl.DeviceIdType.MESH,
        )

    def begin(*arguments):
        copy = remote(*arguments)
        copy.start()
        return copy

    at_x, at_y = chip % 2, chip // 2
    square = [
        2 * ((at_y + e // 2) % 2) + (at_x + e % 2) % 2 for e in range(n_chip)
    ]
    sibling = (t, 2 * chip + 1 - core)
    chips = [(t, 2 * ((chip + e) % n_chip) + core) for e in range(n_chip)]
    toks = [((t + d) % n_tok, h) for d in range(n_tok)]
    barrier = pltpu.get_barrier_semaphore()
    for where in [sibling] + chips[1:] + toks[1:]:
        pl.semaphore_signal(barrier, inc=1, device_id=where, device_id_type=pl.DeviceIdType.MESH)
    pl.semaphore_wait(barrier, n_chip + n_tok - 1)

    orders = [
        sorted(range(n_tok), key=lambda s: (abs(s - k), -abs(2 * s - n_tok + 1)))
        for k in range(n_tok)
    ]
    sources = [t]
    for j in range(1, n_tok):
        source = jnp.int32(orders[0][j])
        for k in range(1, n_tok):
            source = jnp.where(t == k, jnp.int32(orders[k][j]), source)
        sources.append(source)

    def row_at(source):
        return pl.multiple_of(source * rows, rows)

    def part(array, source, e, i=None):
        at_col = pl.multiple_of((2 * square[e] + core) * cols, cols)
        count = rows if i is None else rows // 2
        at_row = pl.multiple_of(row_at(source) + (i or 0) * count, count)
        return array.at[pl.ds(at_row, count), pl.ds(at_col, cols)]

    def along(source, blocks, send, recv, act):
        @pl.when((source <= t) & (t + 1 < n_tok))
        def _():
            for k, (block, target) in enumerate(blocks):
                act(remote(block, target, send(0, source, k), recv(source, k), (t + 1, h)))

        @pl.when((source >= t) & (t > 0))
        def _():
            for k, (block, target) in enumerate(blocks):
                act(remote(block, target, send(1, source, k), recv(source, k), (t - 1, h)))

    def start(copy):
        copy.start()

    def wait_send(copy):
        copy.wait_send()

    def act_blocks(j):
        source = sources[j]
        mine = (tokens, cotangent)
        return [
            (mine[k] if j == 0 else part(array, source, 0), part(array, source, 0))
            for k, array in enumerate((x, c))
        ]

    def act_along(j, act):
        along(
            sources[j], act_blocks(j),
            lambda way, source, k: act_send.at[way, source, k],
            lambda source, k: act_recv.at[source, k], act,
        )

    from_chip, from_core = {}, {}

    def to_chips(j):
        for e in (1, 2):
            from_chip[j, e] = [
                begin(
                    block, target, chip_sem.at[0, j, e - 1, k], chip_sem.at[1, j, e - 1, k],
                    (t, 2 * square[e] + core),
                )
                for k, (block, target) in enumerate(act_blocks(j))
            ]

    def to_core(j, e):
        if e == 0:
            blocks = act_blocks(j)
        else:
            blocks = [(part(array, sources[j], e),) * 2 for array in (x, c)]
        from_core[j, e] = [
            begin(block, target, core_sem.at[0, j, e, k], core_sem.at[1, j, e, k], sibling)
            for k, (block, target) in enumerate(blocks)
        ]

    def first_part(e):
        at = pl.multiple_of((2 * ((chip + n_chip - e) % n_chip) + core) * cols, cols)
        return full_a.at[pl.ds(at, cols), :]

    weights = {}
    depths = pl.ds(pl.multiple_of(t * depth, depth), depth)

    def weight_blocks(d, p):
        at = pl.multiple_of(((t + d) % n_tok) * width + p * part_width, part_width)
        here = pl.ds(p * part_width, part_width)
        return [
            (w_in.at[:, pl.ds(at, part_width)], full_in.at[depths, here]),
            (w_out.at[pl.ds(at, part_width), :], full_out.at[here, depths]),
        ]

    def send_weight(d, p, k):
        block, target = weight_blocks(d, p)[k]
        weights[d, p, k] = begin(
            block, target, w_sem.at[0, d - 1, p, k], w_sem.at[1, d - 1, p, k], toks[d]
        )

    act_along(0, start)
    to_chips(0)
    firsts = [
        begin(in_a, first_part(0), first_sem.at[0, e - 1], first_sem.at[1, e - 1], chips[e])
        for e in range(1, n_chip)
    ]
    to_core(0, 0)
    a_core = [begin(in_a, first_part(0), first_core_sem.at[0, 0], first_core_sem.at[1, 0], sibling)]
    pieces = [(d, p, k) for p in range(n_part) for k in range(2) for d in range(1, n_tok)]
    pieces = [piece for piece in pieces if piece[1:] != (0, 0) or piece[0] in (1, n_tok - 1)]
    rest = [(d, 0, 0) for d in range(2, n_tok - 1)] + pieces[min(2, n_tok - 1):]
    for piece in pieces[:min(2, n_tok - 1)]:
        send_weight(*piece)
    at = pl.multiple_of(t * width, width)
    own = [(block, target) for block, target in act_blocks(0)]
    own += [(in_a, first_part(0)), (out_b, b_mat)]
    own += [(in_b.at[:, pl.ds(at, width)], second), (out_a.at[pl.ds(at, width), :], first)]
    for p in range(n_part):
        own += weight_blocks(0, p)
    own = [
        pltpu.make_async_copy(block, target, own_sem.at[k])
        for k, (block, target) in enumerate(own)
    ]
    for copy in own:
        copy.start()

    def arrive(j):
        for k, (block, target) in enumerate(act_blocks(j)):
            remote(
                target, target, act_send.at[0, sources[j], k], act_recv.at[sources[j], k], sibling
            ).wait_recv()
        act_along(j, start)
        to_chips(j)
        to_core(j, 0)

    def near(j):
        for e in (1, 2):
            for copy in from_chip[j, e]:
                copy.wait_recv()
            from_chip[j, 2 + e] = [
                begin(
                    part(array, sources[j], e, e - 1), part(array, sources[j], e, e - 1),
                    chip_sem.at[0, j, 1 + e, k], chip_sem.at[1, j, 1 + e, k],
                    (t, 2 * square[3 - e] + core),
                )
                for k, array in enumerate((x, c))
            ]
            to_core(j, e)

    def far(j):
        for e in (3, 4):
            for copy in from_chip[j, e]:
                copy.wait_recv()
        to_core(j, 3)

    def complete(j):
        for e in range(n_chip):
            for copy in from_core[j, e]:
                copy.wait_recv()

    def ranks(source):
        here = pl.ds(row_at(source), rows)
        high, rest = split(nn(x[here, :], full_a[...]))
        low[here, :rank] = high
        low[here, rank:] = rest
        high, rest = split(nt(c[here, :], b_mat[...]))
        back[here, :rank] = high
        back[here, rank:] = rest

    def hidden(p, source, begun):
        here = pl.ds(row_at(source), rows)
        those = slice(p * part_width, (p + 1) * part_width)
        pre_s[...] = nn(x[here, :], full_in[:, those]) + nn(low[here, :], second2[:, those])
        back_s[...] = nt(c[here, :], full_out[those, :]) + nt(back[here, :], first2[those, :])
        step = rows // 8
        for at in range(0, rows, step):
            some = slice(at, at + step)
            value_out, slopes = gelu_pair(pre_s[some, :])
            act_s[some, :] = value_out.astype(BF16)
            grad_s[some, :] = (back_s[some, :] * slopes).astype(BF16)
        act, grad = act_s[...], grad_s[...]
        oa_new, ib_new = tn(act, back[here, :]), tn(low[here, :], grad)
        out_new, back_new = nn(act, first[those, :]), nt(grad, second[:, those])
        if begun:
            oa_acc[p] += oa_new
            ib_acc[p] += ib_new
        else:
            oa_acc[p] = oa_new
            ib_acc[p] = ib_new
        if p == 0:
            rank_out[here, :] = out_new
            rank_back[here, :] = back_new
        else:
            rank_out[here, :] += out_new
            rank_back[here, :] += back_new
        if p < n_part - 1:
            if p == 0:
                dense[here, :] = nt(grad, full_in[:, those])
            else:
                dense[here, :] += nt(grad, full_in[:, those])
            return
        high, rest = split(rank_back[here, :])
        low[here, :rank] = high
        low[here, rank:] = rest
        high, rest = split(rank_out[here, :])
        back[here, :rank] = high
        back[here, rank:] = rest
        value = nt(grad, full_in[:, those]) + nt(low[here, :], a2[...])
        dense[here, :] = dense[here, :] + value if n_part > 1 else value

    def prepare():
        for e in range(1, n_chip):
            firsts[e - 1].wait_recv()
            a_core.append(begin(
                first_part(e), first_part(e), first_core_sem.at[0, e], first_core_sem.at[1, e],
                sibling,
            ))
        for copy in own:
            copy.wait()
        for copy in a_core:
            copy.wait_recv()
        half = (ADAPTER_SCALE * second[...].astype(F32)).astype(BF16)
        second2[:rank, :] = half
        second2[rank:, :] = half
        half = (ADAPTER_SCALE * first[...].astype(F32)).astype(BF16)
        first2[:, :rank] = half
        first2[:, rank:] = half
        half = (ADAPTER_SCALE * full_a[...].astype(F32)).astype(BF16)
        a2[:, :rank] = half
        a2[:, rank:] = half

    early = len(pieces) // 3

    def more(j):
        for piece in {2: rest[:early], n_tok - 1: rest[early:]}.get(j, []):
            send_weight(*piece)

    for j in range(1, n_tok - 1):
        arrive(j)
        more(j)
    near(0)
    arrive(n_tok - 1)
    more(n_tok - 1)
    far(0)
    near(1)
    complete(0)
    prepare()
    ranks(sources[0])
    for j in range(1, n_tok - 1):
        far(j)
        near(j + 1)
        complete(j)
        ranks(sources[j])
    far(n_tok - 1)

    def wait_weights(p):
        for d in range(1, n_tok):
            for k in range(2):
                weights[d, p, k].wait_recv()

    def oa_blocks(source, p):
        at = pl.multiple_of(source * width + p * part_width, part_width)
        oa_at, ib_at = oa_all.at[pl.ds(at, part_width), :], ib_all.at[:, pl.ds(at, part_width)]
        return [(oa_at, oa_at), (ib_at, ib_at)]

    def grads_along(source, p, act):
        along(
            source, oa_blocks(source, p),
            lambda way, source, k: grad_send.at[way, source, p, k],
            lambda source, k: grad_recv.at[source, p, k], act,
        )

    def finish_grads(p):
        at = pl.multiple_of(t * width + p * part_width, part_width)
        oa = oa_acc[p]
        oa_all[pl.ds(at, part_width), :] = (scale * (oa[:, :rank] + oa[:, rank:])).astype(BF16)
        ib = ib_acc[p]
        ib_all[:, pl.ds(at, part_width)] = (scale * (ib[:rank] + ib[rank:])).astype(BF16)
        grads_along(t, p, start)

    def grad_hop(s, p):
        def relay(source):
            blocks = oa_blocks(source, p)
            for k, (block, target) in enumerate(blocks):
                remote(
                    target, target, grad_send.at[0, source, p, k], grad_recv.at[source, p, k],
                    sibling,
                ).wait_recv()
            grads_along(source, p, start)

        pl.when(t >= s + 1)(lambda: relay(t - 1 - s))
        pl.when(t + 1 + s < n_tok)(lambda: relay(t + 1 + s))

    complete(n_tok - 1)
    ranks(sources[n_tok - 1])
    for p in range(n_part - 1):
        wait_weights(p)
        for j in range(n_tok):
            hidden(p, sources[j], j > 0)
        finish_grads(p)
    last = n_part - 1
    wait_weights(last)

    core_copies, first_copies, second_copies, tok_copies = {}, {}, {}, []
    blocks = [sources[n_tok - 1 - q] for q in range(n_tok)]

    def columns(e, parity):
        return pl.ds(pl.multiple_of((2 * square[e] + parity) * cols, cols), cols)

    def here(q):
        return pl.ds(row_at(blocks[q]), rows)

    def buffers(q):
        if q == n_tok:
            return core_t, kept_t, pend_t, one_send_t, one_recv_t, two_send_t, two_recv_t
        return tuple(
            array.at[q] for array in (core_d, kept_d, pend_d, one_send, one_recv, two_send, two_recv)
        )

    def to_sibling(q):
        got = buffers(q)[0]
        core_copies[q] = []
        for e in range(n_chip):
            those = columns(e, 1 - core)
            source = terms.at[:, those] if q == n_tok else dense.at[here(q), those]
            core_copies[q].append(
                begin(source, got.at[e], core_r_sem.at[0, q, e], core_r_sem.at[1, q, e], sibling)
            )

    def over_core(q):
        got, kept, pend, sent, recv = buffers(q)[:5]
        half = kept.shape[0] // 2
        first_copies[q] = []
        for e in (3, 1, 2, 0):
            core_copies[q][e].wait_recv()
            those = columns(e, core)
            mine = terms[:, those] if q == n_tok else dense[here(q), those]
            value = mine + got[e]
            for i in range(2):
                some = value[i * half:(i + 1) * half]
                if e == 0:
                    kept[i * half:(i + 1) * half, :] = some
                elif e == 2 - i:
                    pend[i] = some
                else:
                    sent[i, 0 if e == 1 + i else 1] = some.astype(BF16)
        for i in range(2):
            first_copies[q].append(begin(
                sent.at[i], recv.at[i], one_sem.at[0, q, i], one_sem.at[1, q, i],
                (t, 2 * square[1 + i] + core),
            ))

    def over_first(q):
        _, kept, pend, _, recv, sent, second_recv = buffers(q)
        half = kept.shape[0] // 2
        second_copies[q] = []
        for i in range(2):
            first_copies[q][i].wait_recv()
            sent[i] = (pend[i] + recv[i, 1].astype(F32)).astype(BF16)
            second_copies[q].append(begin(
                sent.at[i], second_recv.at[i], two_sem.at[0, q, i], two_sem.at[1, q, i],
                (t, 2 * square[2 - i] + core),
            ))
            some = slice(i * half, (i + 1) * half)
            kept[some, :] = kept[some, :] + recv[i, 0].astype(F32)

    def over_second(q):
        _, kept, _, _, _, _, recv = buffers(q)
        half = kept.shape[0] // 2
        for i in range(2):
            second_copies[q][i].wait_recv()
            some = slice(i * half, (i + 1) * half)
            kept[some, :] = kept[some, :] + recv[i].astype(F32)

    def line_copy(q, way):
        where = (t + 1 - 2 * way, h)
        return remote(
            line_send.at[min(q, n_tok - 2)], line_recv.at[way, blocks[q]],
            line_sem.at[way, min(q, n_tok - 2)], line_got.at[way, blocks[q]], where,
        )

    def send_line(q, way):
        line_send[q] = kept_d[q].astype(BF16)
        line_copy(q, way).start()

    def add_line(q, way):
        line_copy(q, way).wait_recv()
        kept_d[q] = kept_d[q] + line_recv[way, blocks[q]].astype(F32)

    def start_line(q):
        pl.when((blocks[q] > t) & (t == 0))(lambda: send_line(q, 0))
        pl.when((blocks[q] < t) & (t == n_tok - 1))(lambda: send_line(q, 1))

    def over_line(q):
        def add_and_send(way):
            add_line(q, way)
            send_line(q, way)

        pl.when((blocks[q] > t) & (t > 0))(lambda: add_and_send(0))
        pl.when((blocks[q] < t) & (t < n_tok - 1))(lambda: add_and_send(1))

    def share_terms():
        all_t[t] = kept_t[...].astype(BF16)
        for k in range(1, n_tok):
            tok_copies.append(begin(
                all_t.at[t], all_t.at[t], term_sem.at[0, k - 1], term_sem.at[1, k - 1], toks[k]
            ))

    def sum_terms():
        out_cols = x.shape[1] // n_chip
        for at in range(0, x.shape[1], out_cols):
            those = slice(at, at + out_cols)
            value = tn(back[...], c[:, those])
            terms[:rank, those] = scale * (value[:rank] + value[rank:])
            value = tn(low[...], x[:, those])
            terms[rank:, those] = scale * (value[:rank] + value[rank:])

    def hop(s):
        for p in range(last):
            grad_hop(s, p)

    final = n_tok - 1
    for q in range(n_tok):
        hidden(last, blocks[q], q > 0)
        to_sibling(q)
        if q >= 1:
            over_core(q - 1)
        if q == 2:
            hop(0)
    finish_grads(last)
    sum_terms()
    to_sibling(n_tok)
    for q in range(final - 1):
        over_first(q)
    over_core(n_tok)
    hop(1)
    over_first(final - 1)
    over_second(0)
    start_line(0)
    grad_hop(0, last)
    for q in range(1, final - 1):
        over_second(q)
        start_line(q)
    over_first(n_tok)
    over_core(final)
    over_line(0)
    over_second(final - 1)
    start_line(final - 1)
    over_second(n_tok)
    share_terms()
    if n_tok > 2:
        grad_hop(1, last)
    over_first(final)
    for q in range(1, final):
        over_line(q)
    for s in range(2, n_tok - 1):
        hop(s)
    over_second(final)
    for s in range(2, n_tok - 1):
        grad_hop(s, last)
    pl.when(t > 0)(lambda: add_line(final, 0))
    pl.when(t < n_tok - 1)(lambda: add_line(final, 1))
    dx_out[...] = kept_d[final]
    for copy in tok_copies:
        copy.wait_recv()
    value = all_t[0].astype(F32)
    for k in range(1, n_tok):
        value = value + all_t[k].astype(F32)
    terms_out[...] = value
    for q in range(final):
        pl.when(blocks[q] > t)(lambda: line_copy(q, 0).wait_send())
        pl.when(blocks[q] < t)(lambda: line_copy(q, 1).wait_send())
    for j in range(n_tok):
        act_along(j, wait_send)
        for p in range(n_part):
            grads_along(sources[j], p, wait_send)
    for groups in (from_chip, from_core, core_copies, first_copies, second_copies):
        for group in groups.values():
            for copy in group:
                copy.wait_send()
    for copy in firsts + a_core + list(weights.values()) + tok_copies:
        copy.wait_send()


def fused(n_part, scale, tokens, cotangent, frozen_in, frozen_out, in_a, in_b, out_a, out_b):
    n_tok, n_hid = lax.axis_size("tok"), lax.axis_size("hid")
    n_chip = n_hid // 2
    rows, cols = tokens.shape
    count, features = rows * n_tok, cols * n_hid
    width = frozen_in.shape[1] // n_tok
    part_width = width // n_part
    rank = in_a.shape[1]
    sems = pltpu.SemaphoreType.DMA
    vmem = pl.BlockSpec(memory_space=pltpu.VMEM)
    whole = pl.BlockSpec(memory_space=pl.ANY)
    arguments = (tokens, cotangent, frozen_in, frozen_out, in_a, in_b, out_a, out_b)
    return pl.pallas_call(
        functools.partial(fused_kernel, n_tok, n_hid, n_part, scale),
        out_shape=(
            jax.ShapeDtypeStruct((rows, cols), F32),
            jax.ShapeDtypeStruct((2 * rank, cols), F32),
            jax.ShapeDtypeStruct((n_tok * width, rank), BF16),
            jax.ShapeDtypeStruct((rank, n_tok * width), BF16),
        ),
        in_specs=[whole] * 8,
        out_specs=(vmem,) * 4,
        scratch_shapes=[
            pltpu.VMEM((count, features), BF16),
            pltpu.VMEM((count, features), BF16),
            pltpu.VMEM((features, width), BF16),
            pltpu.VMEM((width, features), BF16),
            pltpu.VMEM((features, rank), BF16),
            pltpu.VMEM((rank, features), BF16),
            pltpu.VMEM((rank, width), BF16),
            pltpu.VMEM((width, rank), BF16),
            pltpu.VMEM((2 * rank, width), BF16),
            pltpu.VMEM((width, 2 * rank), BF16),
            pltpu.VMEM((features, 2 * rank), BF16),
            pltpu.VMEM((count, 2 * rank), BF16),
            pltpu.VMEM((count, 2 * rank), BF16),
            pltpu.VMEM((rows, part_width), F32),
            pltpu.VMEM((rows, part_width), F32),
            pltpu.VMEM((rows, part_width), BF16),
            pltpu.VMEM((rows, part_width), BF16),
            pltpu.VMEM((count, features), F32),
            pltpu.VMEM((count, rank), F32),
            pltpu.VMEM((count, rank), F32),
            pltpu.VMEM((n_part, part_width, 2 * rank), F32),
            pltpu.VMEM((n_part, 2 * rank, part_width), F32),
            pltpu.VMEM((2 * rank, features), F32),
            pltpu.VMEM((n_tok, n_chip, rows, cols), F32),
            pltpu.VMEM((n_chip, 2 * rank, cols), F32),
            pltpu.VMEM((n_tok, rows, cols), F32),
            pltpu.VMEM((2 * rank, cols), F32),
            pltpu.VMEM((n_tok, 2, rows // 2, cols), F32),
            pltpu.VMEM((2, rank, cols), F32),
            pltpu.VMEM((n_tok, 2, 2, rows // 2, cols), BF16),
            pltpu.VMEM((2, 2, rank, cols), BF16),
            pltpu.VMEM((n_tok, 2, 2, rows // 2, cols), BF16),
            pltpu.VMEM((2, 2, rank, cols), BF16),
            pltpu.VMEM((n_tok, 2, rows // 2, cols), BF16),
            pltpu.VMEM((2, rank, cols), BF16),
            pltpu.VMEM((n_tok, 2, rows // 2, cols), BF16),
            pltpu.VMEM((2, rank, cols), BF16),
            pltpu.VMEM((n_tok - 1, rows, cols), BF16),
            pltpu.VMEM((2, n_tok, rows, cols), BF16),
            pltpu.VMEM((n_tok, 2 * rank, cols), BF16),
            sems((2, n_tok, 2)),
            sems((n_tok, 2)),
            sems((2, n_tok, 4, 2)),
            sems((2, n_tok, n_chip, 2)),
            sems((2, n_chip - 1)),
            sems((2, n_chip)),
            sems((2, n_tok - 1, n_part, 2)),
            sems((6 + 2 * n_part,)),
            sems((2, n_tok + 1, n_chip)),
            sems((2, n_tok + 1, 2)),
            sems((2, n_tok + 1, 2)),
            sems((2, n_tok - 1)),
            sems((2, n_tok)),
            sems((2, n_tok - 1)),
            sems((2, n_tok, n_part, 2)),
            sems((n_tok, n_part, 2)),
        ],
        compiler_params=pltpu.CompilerParams(
            collective_id=1, has_side_effects=True, vmem_limit_bytes=52 * 1024 * 1024
        ),
    )(*(pltpu.with_memory_space_constraint(array, pltpu.HBM) for array in arguments))


def finish_kernel(dx, terms, oa, ib, dx_out, in_a_out, ib_out, oa_out, out_b_out):
    rank = in_a_out.shape[1]
    ib_out[...] = ib[...].astype(F32)
    oa_out[...] = oa[...].astype(F32)
    dx_out[...] = dx[...]
    in_a_out[...] = terms[rank:, :].T
    out_b_out[...] = terms[:rank, :]


def local(tokens, cotangent, frozen_in, frozen_out, in_a, in_b, out_a, out_b):
    count = tokens.shape[0] * lax.axis_size("tok")
    scale = ADAPTER_SCALE / math.sqrt(count)
    dx, terms, oa, ib = fused(
        2, scale, tokens, cotangent, frozen_in, frozen_out, in_a, in_b, out_a, out_b
    )
    rank, cols = in_a.shape[1], tokens.shape[1]
    vmem = pl.BlockSpec(memory_space=pltpu.VMEM)
    return pl.pallas_call(
        finish_kernel,
        out_shape=(
            jax.ShapeDtypeStruct(dx.shape, F32),
            jax.ShapeDtypeStruct((cols, rank), F32),
            jax.ShapeDtypeStruct(ib.shape, F32),
            jax.ShapeDtypeStruct(oa.shape, F32),
            jax.ShapeDtypeStruct((rank, cols), F32),
        ),
        in_specs=[vmem] * 4,
        out_specs=(vmem,) * 5,
        compiler_params=pltpu.CompilerParams(vmem_limit_bytes=16 * 1024 * 1024),
    )(dx, terms, oa, ib)


def local_by_rows(
    tokens,
    cotangent,
    frozen_in,
    frozen_out,
    input_adapter_first,
    input_adapter_second,
    adapter_out_a,
    adapter_out_b,
):
    highest_precision = lax.Precision.HIGHEST
    device_local_rows = tokens.shape[0]
    rank_width = input_adapter_second.shape[0]
    gradient_scale = ADAPTER_SCALE / math.sqrt(device_local_rows * lax.axis_size("tok"))
    full_tokens, full_cotan = (
        lax.all_gather(tokens, "hid", axis=1, tiled=True),
        lax.all_gather(cotangent, "hid", axis=1, tiled=True),
    )
    in_rows = lax.all_gather(frozen_in, "tok", axis=0, tiled=True)
    in_a_full = lax.all_gather(input_adapter_first, "hid", axis=0, tiled=True)
    lowrank_input = jnp.dot(full_tokens, in_a_full, preferred_element_type=jnp.float32)
    second_float = input_adapter_second.astype(jnp.float32)
    out_a_float = adapter_out_a.astype(jnp.float32)
    pre_activation = jnp.dot(
        full_tokens, in_rows, preferred_element_type=jnp.float32
    ) + ADAPTER_SCALE * jnp.dot(lowrank_input, second_float, precision=highest_precision)
    value_out, slopes = gelu_pair(pre_activation)
    hidden_act = value_out.astype(jnp.bfloat16)
    backward_lowrank = jnp.einsum(
        "td,rd->tr", full_cotan, adapter_out_b, preferred_element_type=jnp.float32
    )
    rank_out = jnp.dot(hidden_act, adapter_out_a, preferred_element_type=jnp.float32)
    dense_backward = jnp.einsum(
        "td,fd->tf",
        full_cotan,
        lax.all_gather(frozen_out, "tok", axis=1, tiled=True),
        preferred_element_type=jnp.float32,
    )
    dense_backward = dense_backward + ADAPTER_SCALE * jnp.dot(
        backward_lowrank, out_a_float.T, precision=highest_precision
    )
    grad_pre = (dense_backward * slopes).astype(jnp.bfloat16)
    rank_backward = jnp.einsum(
        "tf,rf->tr", grad_pre, input_adapter_second, preferred_element_type=jnp.float32
    )
    dense_in = jnp.einsum("tf,df->td", grad_pre, in_rows, preferred_element_type=jnp.float32)
    grad_out_a = gradient_scale * jnp.dot(
        hidden_act.astype(jnp.float32).T, backward_lowrank, precision=highest_precision
    )
    grad_in_b = gradient_scale * jnp.dot(
        lowrank_input.T, grad_pre.astype(jnp.float32), precision=highest_precision
    )
    in_a_float = in_a_full.astype(jnp.float32)
    dx_term = dense_in + ADAPTER_SCALE * jnp.dot(
        rank_backward, in_a_float.T, precision=highest_precision
    )
    out_term = jnp.dot(rank_out.T, full_cotan.astype(jnp.float32), precision=highest_precision)
    in_term = jnp.dot(rank_backward.T, full_tokens.astype(jnp.float32), precision=highest_precision)
    rank_terms = jnp.concatenate([out_term, in_term], axis=0)
    input_gradient, rank_local = (
        lax.psum_scatter(dx_term, "hid", scatter_dimension=1, tiled=True),
        lax.psum_scatter(rank_terms, "hid", scatter_dimension=1, tiled=True),
    )
    grad_out_a, grad_in_b, rank_total = lax.psum((grad_out_a, grad_in_b, rank_local), "tok")
    grad_out_b = gradient_scale * rank_total[:rank_width]
    grad_in_a = gradient_scale * rank_total[rank_width:].T
    return (input_gradient, grad_in_a, grad_in_b, grad_out_a, grad_out_b)


def solution(mesh):
    in_specs = (
        P("tok", "hid"),
        P("tok", "hid"),
        P("tok", "hid"),
        P("hid", "tok"),
        P("hid", None),
        P(None, "hid"),
        P("hid", None),
        P(),
    )
    out_specs = (P("tok", "hid"), P("hid", None), P(None, "hid"), P("hid", None), P(None, "hid"))
    def body(*arrays):
        share = arrays[2].shape[1] // lax.axis_size("tok")
        wide = share % 256 == 0 and lax.axis_size("tok") > 2
        wide = wide and lax.axis_size("hid") == 2 ** len(("y", "x", "core"))
        return local(*arrays) if wide else local_by_rows(*arrays)

    return jax.shard_map(body, mesh=mesh, in_specs=in_specs, out_specs=out_specs, check_vma=False)
```

```python
import functools
import math

import jax
import jax.numpy as jnp
from jax import lax
from jax.experimental import pallas as pl
from jax.experimental.pallas import tpu as pltpu
from jax.sharding import PartitionSpec as P

ADAPTER_SCALE = 0.5
GELU_K = 0.7978845608
GELU_C = 0.044715
F32 = jnp.float32
BF16 = jnp.bfloat16


def gelu_pair(pre_activation):
    tangent = jnp.tanh(
        GELU_K * (pre_activation + GELU_C * pre_activation * pre_activation * pre_activation)
    )
    value_out = 0.5 * pre_activation * (1.0 + tangent)
    slopes = 0.5 * (1.0 + tangent) + 0.5 * pre_activation * (1.0 - tangent * tangent) * GELU_K * (
        1.0 + 3.0 * GELU_C * pre_activation * pre_activation
    )
    return (value_out, slopes)


def dot(left, right, dims):
    return lax.dot_general(left, right, (dims, ((), ())), preferred_element_type=F32)


def nn(left, right):
    return dot(left, right, ((1,), (0,)))


def nt(left, right):
    return dot(left, right, ((1,), (1,)))


def tn(left, right):
    return dot(left, right, ((0,), (0,)))


def split(value):
    high = value.astype(BF16)
    return high, (value - high.astype(F32)).astype(BF16)


def fused_kernel(
    n_tok, n_hid, n_part, scale,
    tokens, cotangent, w_in, w_out, in_a, in_b, out_a, out_b,
    dx_out, terms_out, oa_all, ib_all,
    x, c, full_in, full_out, full_a, b_mat, second, first, second2, first2, a2,
    low, back, pre_s, back_s, act_s, grad_s, dense, rank_out, rank_back, oa_acc, ib_acc, terms,
    core_d, core_t, kept_d, kept_t, pend_d, pend_t, one_send, one_send_t, one_recv, one_recv_t,
    two_send, two_send_t, two_recv, two_recv_t, line_send, line_recv, all_t,
    act_send, act_recv, chip_sem, core_sem, first_sem, first_core_sem, w_sem, own_sem,
    core_r_sem, one_sem, two_sem, line_sem, line_got, term_sem, grad_send, grad_recv,
):
    t, h = lax.axis_index("tok"), lax.axis_index("hid")
    n_chip = n_hid // 2
    chip, core = h // 2, h % 2
    rows, cols = tokens.shape
    depth = w_in.shape[0]
    width = full_in.shape[1]
    part_width = width // n_part
    rank = full_a.shape[1]

    def remote(source, target, send, recv, where):
        return pltpu.make_async_remote_copy(
            src_ref=source, dst_ref=target, send_sem=send, recv_sem=recv,
            device_id=where, device_id_type=pl.DeviceIdType.MESH,
        )

    def begin(*arguments):
        copy = remote(*arguments)
        copy.start()
        return copy

    at_x, at_y = chip % 2, chip // 2
    square = [
        2 * ((at_y + e // 2) % 2) + (at_x + e % 2) % 2 for e in range(n_chip)
    ]
    sibling = (t, 2 * chip + 1 - core)
    chips = [(t, 2 * ((chip + e) % n_chip) + core) for e in range(n_chip)]
    toks = [((t + d) % n_tok, h) for d in range(n_tok)]
    barrier = pltpu.get_barrier_semaphore()
    for where in [sibling] + chips[1:] + toks[1:]:
        pl.semaphore_signal(barrier, inc=1, device_id=where, device_id_type=pl.DeviceIdType.MESH)
    pl.semaphore_wait(barrier, n_chip + n_tok - 1)

    orders = [
        sorted(range(n_tok), key=lambda s: (abs(s - k), -abs(2 * s - n_tok + 1)))
        for k in range(n_tok)
    ]
    sources = [t]
    for j in range(1, n_tok):
        source = jnp.int32(orders[0][j])
        for k in range(1, n_tok):
            source = jnp.where(t == k, jnp.int32(orders[k][j]), source)
        sources.append(source)

    def row_at(source):
        return pl.multiple_of(source * rows, rows)

    def part(array, source, e, i=None):
        at_col = pl.multiple_of((2 * square[e] + core) * cols, cols)
        count = rows if i is None else rows // 2
        at_row = pl.multiple_of(row_at(source) + (i or 0) * count, count)
        return array.at[pl.ds(at_row, count), pl.ds(at_col, cols)]

    def along(source, blocks, send, recv, act):
        @pl.when((source <= t) & (t + 1 < n_tok))
        def _():
            for k, (block, target) in enumerate(blocks):
                act(remote(block, target, send(0, source, k), recv(source, k), (t + 1, h)))

        @pl.when((source >= t) & (t > 0))
        def _():
            for k, (block, target) in enumerate(blocks):
                act(remote(block, target, send(1, source, k), recv(source, k), (t - 1, h)))

    def start(copy):
        copy.start()

    def wait_send(copy):
        copy.wait_send()

    def act_blocks(j):
        source = sources[j]
        mine = (tokens, cotangent)
        return [
            (mine[k] if j == 0 else part(array, source, 0), part(array, source, 0))
            for k, array in enumerate((x, c))
        ]

    def act_along(j, act):
        along(
            sources[j], act_blocks(j),
            lambda way, source, k: act_send.at[way, source, k],
            lambda source, k: act_recv.at[source, k], act,
        )

    from_chip, from_core = {}, {}

    def to_chips(j):
        for e in (1, 2):
            from_chip[j, e] = [
                begin(
                    block, target, chip_sem.at[0, j, e - 1, k], chip_sem.at[1, j, e - 1, k],
                    (t, 2 * square[e] + core),
                )
                for k, (block, target) in enumerate(act_blocks(j))
            ]

    def to_core(j, e):
        if e == 0:
            blocks = act_blocks(j)
        else:
            blocks = [(part(array, sources[j], e),) * 2 for array in (x, c)]
        from_core[j, e] = [
            begin(block, target, core_sem.at[0, j, e, k], core_sem.at[1, j, e, k], sibling)
            for k, (block, target) in enumerate(blocks)
        ]

    def first_part(e):
        at = pl.multiple_of((2 * ((chip + n_chip - e) % n_chip) + core) * cols, cols)
        return full_a.at[pl.ds(at, cols), :]

    weights = {}
    depths = pl.ds(pl.multiple_of(t * depth, depth), depth)

    def weight_blocks(d, p):
        at = pl.multiple_of(((t + d) % n_tok) * width + p * part_width, part_width)
        here = pl.ds(p * part_width, part_width)
        return [
            (w_in.at[:, pl.ds(at, part_width)], full_in.at[depths, here]),
            (w_out.at[pl.ds(at, part_width), :], full_out.at[here, depths]),
        ]

    def send_weight(d, p, k):
        block, target = weight_blocks(d, p)[k]
        weights[d, p, k] = begin(
            block, target, w_sem.at[0, d - 1, p, k], w_sem.at[1, d - 1, p, k], toks[d]
        )

    act_along(0, start)
    to_chips(0)
    firsts = [
        begin(in_a, first_part(0), first_sem.at[0, e - 1], first_sem.at[1, e - 1], chips[e])
        for e in range(1, n_chip)
    ]
    to_core(0, 0)
    a_core = [begin(in_a, first_part(0), first_core_sem.at[0, 0], first_core_sem.at[1, 0], sibling)]
    pieces = [(d, p, k) for p in range(n_part) for k in range(2) for d in range(1, n_tok)]
    pieces = [piece for piece in pieces if piece[1:] != (0, 0) or piece[0] in (1, n_tok - 1)]
    rest = [(d, 0, 0) for d in range(2, n_tok - 1)] + pieces[min(2, n_tok - 1):]
    for piece in pieces[:min(2, n_tok - 1)]:
        send_weight(*piece)
    at = pl.multiple_of(t * width, width)
    own = [(block, target) for block, target in act_blocks(0)]
    own += [(in_a, first_part(0)), (out_b, b_mat)]
    own += [(in_b.at[:, pl.ds(at, width)], second), (out_a.at[pl.ds(at, width), :], first)]
    for p in range(n_part):
        own += weight_blocks(0, p)
    own = [
        pltpu.make_async_copy(block, target, own_sem.at[k])
        for k, (block, target) in enumerate(own)
    ]
    for copy in own:
        copy.start()

    def arrive(j):
        for k, (block, target) in enumerate(act_blocks(j)):
            remote(
                target, target, act_send.at[0, sources[j], k], act_recv.at[sources[j], k], sibling
            ).wait_recv()
        act_along(j, start)
        to_chips(j)
        to_core(j, 0)

    def near(j):
        for e in (1, 2):
            for copy in from_chip[j, e]:
                copy.wait_recv()
            from_chip[j, 2 + e] = [
                begin(
                    part(array, sources[j], e, e - 1), part(array, sources[j], e, e - 1),
                    chip_sem.at[0, j, 1 + e, k], chip_sem.at[1, j, 1 + e, k],
                    (t, 2 * square[3 - e] + core),
                )
                for k, array in enumerate((x, c))
            ]
            to_core(j, e)

    def far(j):
        for e in (3, 4):
            for copy in from_chip[j, e]:
                copy.wait_recv()
        to_core(j, 3)

    def complete(j):
        for e in range(n_chip):
            for copy in from_core[j, e]:
                copy.wait_recv()

    def ranks(source):
        here = pl.ds(row_at(source), rows)
        high, rest = split(nn(x[here, :], full_a[...]))
        low[here, :rank] = high
        low[here, rank:] = rest
        high, rest = split(nt(c[here, :], b_mat[...]))
        back[here, :rank] = high
        back[here, rank:] = rest

    def hidden(p, source, begun):
        here = pl.ds(row_at(source), rows)
        those = slice(p * part_width, (p + 1) * part_width)
        pre_s[...] = nn(x[here, :], full_in[:, those]) + nn(low[here, :], second2[:, those])
        back_s[...] = nt(c[here, :], full_out[those, :]) + nt(back[here, :], first2[those, :])
        step = rows // 8
        for at in range(0, rows, step):
            some = slice(at, at + step)
            value_out, slopes = gelu_pair(pre_s[some, :])
            act_s[some, :] = value_out.astype(BF16)
            grad_s[some, :] = (back_s[some, :] * slopes).astype(BF16)
        act, grad = act_s[...], grad_s[...]
        oa_new, ib_new = tn(act, back[here, :]), tn(low[here, :], grad)
        out_new, back_new = nn(act, first[those, :]), nt(grad, second[:, those])
        if begun:
            oa_acc[p] += oa_new
            ib_acc[p] += ib_new
        else:
            oa_acc[p] = oa_new
            ib_acc[p] = ib_new
        if p == 0:
            rank_out[here, :] = out_new
            rank_back[here, :] = back_new
        else:
            rank_out[here, :] += out_new
            rank_back[here, :] += back_new
        if p < n_part - 1:
            if p == 0:
                dense[here, :] = nt(grad, full_in[:, those])
            else:
                dense[here, :] += nt(grad, full_in[:, those])
            return
        high, rest = split(rank_back[here, :])
        low[here, :rank] = high
        low[here, rank:] = rest
        high, rest = split(rank_out[here, :])
        back[here, :rank] = high
        back[here, rank:] = rest
        value = nt(grad, full_in[:, those]) + nt(low[here, :], a2[...])
        dense[here, :] = dense[here, :] + value if n_part > 1 else value

    def prepare():
        for e in range(1, n_chip):
            firsts[e - 1].wait_recv()
            a_core.append(begin(
                first_part(e), first_part(e), first_core_sem.at[0, e], first_core_sem.at[1, e],
                sibling,
            ))
        for copy in own:
            copy.wait()
        for copy in a_core:
            copy.wait_recv()
        half = (ADAPTER_SCALE * second[...].astype(F32)).astype(BF16)
        second2[:rank, :] = half
        second2[rank:, :] = half
        half = (ADAPTER_SCALE * first[...].astype(F32)).astype(BF16)
        first2[:, :rank] = half
        first2[:, rank:] = half
        half = (ADAPTER_SCALE * full_a[...].astype(F32)).astype(BF16)
        a2[:, :rank] = half
        a2[:, rank:] = half

    early = len(pieces) // 3

    def more(j):
        for piece in {2: rest[:early], n_tok - 1: rest[early:]}.get(j, []):
            send_weight(*piece)

    for j in range(1, n_tok - 1):
        arrive(j)
        more(j)
    near(0)
    arrive(n_tok - 1)
    more(n_tok - 1)
    far(0)
    near(1)
    complete(0)
    prepare()
    ranks(sources[0])
    for j in range(1, n_tok - 1):
        far(j)
        near(j + 1)
        complete(j)
        ranks(sources[j])
    far(n_tok - 1)

    def wait_weights(p):
        for d in range(1, n_tok):
            for k in range(2):
                weights[d, p, k].wait_recv()

    def oa_blocks(source, p):
        at = pl.multiple_of(source * width + p * part_width, part_width)
        oa_at, ib_at = oa_all.at[pl.ds(at, part_width), :], ib_all.at[:, pl.ds(at, part_width)]
        return [(oa_at, oa_at), (ib_at, ib_at)]

    def grads_along(source, p, act):
        along(
            source, oa_blocks(source, p),
            lambda way, source, k: grad_send.at[way, source, p, k],
            lambda source, k: grad_recv.at[source, p, k], act,
        )

    def finish_grads(p):
        at = pl.multiple_of(t * width + p * part_width, part_width)
        oa = oa_acc[p]
        oa_all[pl.ds(at, part_width), :] = (scale * (oa[:, :rank] + oa[:, rank:])).astype(BF16)
        ib = ib_acc[p]
        ib_all[:, pl.ds(at, part_width)] = (scale * (ib[:rank] + ib[rank:])).astype(BF16)
        grads_along(t, p, start)

    def grad_hop(s, p):
        def relay(source):
            blocks = oa_blocks(source, p)
            for k, (block, target) in enumerate(blocks):
                remote(
                    target, target, grad_send.at[0, source, p, k], grad_recv.at[source, p, k],
                    sibling,
                ).wait_recv()
            grads_along(source, p, start)

        pl.when(t >= s + 1)(lambda: relay(t - 1 - s))
        pl.when(t + 1 + s < n_tok)(lambda: relay(t + 1 + s))

    complete(n_tok - 1)
    ranks(sources[n_tok - 1])
    for p in range(n_part - 1):
        wait_weights(p)
        for j in range(n_tok):
            hidden(p, sources[j], j > 0)
        finish_grads(p)
    last = n_part - 1
    wait_weights(last)

    core_copies, first_copies, second_copies, tok_copies = {}, {}, {}, []
    blocks = [sources[n_tok - 1 - q] for q in range(n_tok)]

    def columns(e, parity):
        return pl.ds(pl.multiple_of((2 * square[e] + parity) * cols, cols), cols)

    def here(q):
        return pl.ds(row_at(blocks[q]), rows)

    def buffers(q):
        if q == n_tok:
            return core_t, kept_t, pend_t, one_send_t, one_recv_t, two_send_t, two_recv_t
        return tuple(
            array.at[q] for array in (core_d, kept_d, pend_d, one_send, one_recv, two_send, two_recv)
        )

    def to_sibling(q):
        got = buffers(q)[0]
        core_copies[q] = []
        for e in range(n_chip):
            those = columns(e, 1 - core)
            source = terms.at[:, those] if q == n_tok else dense.at[here(q), those]
            core_copies[q].append(
                begin(source, got.at[e], core_r_sem.at[0, q, e], core_r_sem.at[1, q, e], sibling)
            )

    def over_core(q):
        got, kept, pend, sent, recv = buffers(q)[:5]
        half = kept.shape[0] // 2
        first_copies[q] = []
        for e in (3, 1, 2, 0):
            core_copies[q][e].wait_recv()
            those = columns(e, core)
            mine = terms[:, those] if q == n_tok else dense[here(q), those]
            value = mine + got[e]
            for i in range(2):
                some = value[i * half:(i + 1) * half]
                if e == 0:
                    kept[i * half:(i + 1) * half, :] = some
                elif e == 2 - i:
                    pend[i] = some
                else:
                    sent[i, 0 if e == 1 + i else 1] = some.astype(BF16)
        for i in range(2):
            first_copies[q].append(begin(
                sent.at[i], recv.at[i], one_sem.at[0, q, i], one_sem.at[1, q, i],
                (t, 2 * square[1 + i] + core),
            ))

    def over_first(q):
        _, kept, pend, _, recv, sent, second_recv = buffers(q)
        half = kept.shape[0] // 2
        second_copies[q] = []
        for i in range(2):
            first_copies[q][i].wait_recv()
            sent[i] = (pend[i] + recv[i, 1].astype(F32)).astype(BF16)
            second_copies[q].append(begin(
                sent.at[i], second_recv.at[i], two_sem.at[0, q, i], two_sem.at[1, q, i],
                (t, 2 * square[2 - i] + core),
            ))
            some = slice(i * half, (i + 1) * half)
            kept[some, :] = kept[some, :] + recv[i, 0].astype(F32)

    def over_second(q):
        _, kept, _, _, _, _, recv = buffers(q)
        half = kept.shape[0] // 2
        for i in range(2):
            second_copies[q][i].wait_recv()
            some = slice(i * half, (i + 1) * half)
            kept[some, :] = kept[some, :] + recv[i].astype(F32)

    def half_rows(i):
        return pl.ds(i * (rows // 2), rows // 2)

    def line_copy(q, way, i):
        where = (t + 1 - 2 * way, h)
        return remote(
            line_send.at[min(q, n_tok - 2), half_rows(i)],
            line_recv.at[way, blocks[q], half_rows(i)],
            line_sem.at[way, min(q, n_tok - 2), i], line_got.at[way, blocks[q], i], where,
        )

    def send_half(q, way, i):
        line_send[q, half_rows(i)] = kept_d[q, half_rows(i)].astype(BF16)
        line_copy(q, way, i).start()

    def add_half(q, way, i):
        line_copy(q, way, i).wait_recv()
        got = line_recv[way, blocks[q], half_rows(i)].astype(F32)
        kept_d[q, half_rows(i)] = kept_d[q, half_rows(i)] + got

    def send_line(q, way):
        for i in range(2):
            send_half(q, way, i)

    def add_line(q, way):
        for i in range(2):
            add_half(q, way, i)

    def wait_line(q, way):
        for i in range(2):
            line_copy(q, way, i).wait_send()

    def start_line(q):
        pl.when((blocks[q] > t) & (t == 0))(lambda: send_line(q, 0))
        pl.when((blocks[q] < t) & (t == n_tok - 1))(lambda: send_line(q, 1))

    def over_line(q):
        def add_and_send(way):
            for i in range(2):
                add_half(q, way, i)
                send_half(q, way, i)

        pl.when((blocks[q] > t) & (t > 0))(lambda: add_and_send(0))
        pl.when((blocks[q] < t) & (t < n_tok - 1))(lambda: add_and_send(1))

    def share_terms():
        all_t[t] = kept_t[...].astype(BF16)
        for k in range(1, n_tok):
            tok_copies.append(begin(
                all_t.at[t], all_t.at[t], term_sem.at[0, k - 1], term_sem.at[1, k - 1], toks[k]
            ))

    def sum_terms():
        out_cols = x.shape[1] // n_chip
        for at in range(0, x.shape[1], out_cols):
            those = slice(at, at + out_cols)
            value = tn(back[...], c[:, those])
            terms[:rank, those] = scale * (value[:rank] + value[rank:])
            value = tn(low[...], x[:, those])
            terms[rank:, those] = scale * (value[:rank] + value[rank:])

    def hop(s):
        for p in range(last):
            grad_hop(s, p)

    final = n_tok - 1
    for q in range(n_tok):
        hidden(last, blocks[q], q > 0)
        to_sibling(q)
        if q >= 1:
            over_core(q - 1)
        if q == 2:
            hop(0)
    finish_grads(last)
    sum_terms()
    to_sibling(n_tok)
    for q in range(final - 1):
        over_first(q)
    over_core(n_tok)
    hop(1)
    over_first(final - 1)
    over_second(0)
    start_line(0)
    grad_hop(0, last)
    for q in range(1, final - 1):
        over_second(q)
        start_line(q)
    over_first(n_tok)
    over_core(final)
    over_line(0)
    over_second(final - 1)
    start_line(final - 1)
    over_second(n_tok)
    share_terms()
    if n_tok > 2:
        grad_hop(1, last)
    over_first(final)
    for q in range(1, final):
        over_line(q)
    for s in range(2, n_tok - 1):
        hop(s)
    over_second(final)
    for s in range(2, n_tok - 1):
        grad_hop(s, last)
    pl.when(t > 0)(lambda: add_line(final, 0))
    pl.when(t < n_tok - 1)(lambda: add_line(final, 1))
    dx_out[...] = kept_d[final]
    for copy in tok_copies:
        copy.wait_recv()
    value = all_t[0].astype(F32)
    for k in range(1, n_tok):
        value = value + all_t[k].astype(F32)
    terms_out[...] = value
    for q in range(final):
        pl.when(blocks[q] > t)(lambda: wait_line(q, 0))
        pl.when(blocks[q] < t)(lambda: wait_line(q, 1))
    for j in range(n_tok):
        act_along(j, wait_send)
        for p in range(n_part):
            grads_along(sources[j], p, wait_send)
    for groups in (from_chip, from_core, core_copies, first_copies, second_copies):
        for group in groups.values():
            for copy in group:
                copy.wait_send()
    for copy in firsts + a_core + list(weights.values()) + tok_copies:
        copy.wait_send()


def fused(n_part, scale, tokens, cotangent, frozen_in, frozen_out, in_a, in_b, out_a, out_b):
    n_tok, n_hid = lax.axis_size("tok"), lax.axis_size("hid")
    n_chip = n_hid // 2
    rows, cols = tokens.shape
    count, features = rows * n_tok, cols * n_hid
    width = frozen_in.shape[1] // n_tok
    part_width = width // n_part
    rank = in_a.shape[1]
    sems = pltpu.SemaphoreType.DMA
    vmem = pl.BlockSpec(memory_space=pltpu.VMEM)
    whole = pl.BlockSpec(memory_space=pl.ANY)
    arguments = (tokens, cotangent, frozen_in, frozen_out, in_a, in_b, out_a, out_b)
    return pl.pallas_call(
        functools.partial(fused_kernel, n_tok, n_hid, n_part, scale),
        out_shape=(
            jax.ShapeDtypeStruct((rows, cols), F32),
            jax.ShapeDtypeStruct((2 * rank, cols), F32),
            jax.ShapeDtypeStruct((n_tok * width, rank), BF16),
            jax.ShapeDtypeStruct((rank, n_tok * width), BF16),
        ),
        in_specs=[whole] * 8,
        out_specs=(vmem,) * 4,
        scratch_shapes=[
            pltpu.VMEM((count, features), BF16),
            pltpu.VMEM((count, features), BF16),
            pltpu.VMEM((features, width), BF16),
            pltpu.VMEM((width, features), BF16),
            pltpu.VMEM((features, rank), BF16),
            pltpu.VMEM((rank, features), BF16),
            pltpu.VMEM((rank, width), BF16),
            pltpu.VMEM((width, rank), BF16),
            pltpu.VMEM((2 * rank, width), BF16),
            pltpu.VMEM((width, 2 * rank), BF16),
            pltpu.VMEM((features, 2 * rank), BF16),
            pltpu.VMEM((count, 2 * rank), BF16),
            pltpu.VMEM((count, 2 * rank), BF16),
            pltpu.VMEM((rows, part_width), F32),
            pltpu.VMEM((rows, part_width), F32),
            pltpu.VMEM((rows, part_width), BF16),
            pltpu.VMEM((rows, part_width), BF16),
            pltpu.VMEM((count, features), F32),
            pltpu.VMEM((count, rank), F32),
            pltpu.VMEM((count, rank), F32),
            pltpu.VMEM((n_part, part_width, 2 * rank), F32),
            pltpu.VMEM((n_part, 2 * rank, part_width), F32),
            pltpu.VMEM((2 * rank, features), F32),
            pltpu.VMEM((n_tok, n_chip, rows, cols), F32),
            pltpu.VMEM((n_chip, 2 * rank, cols), F32),
            pltpu.VMEM((n_tok, rows, cols), F32),
            pltpu.VMEM((2 * rank, cols), F32),
            pltpu.VMEM((n_tok, 2, rows // 2, cols), F32),
            pltpu.VMEM((2, rank, cols), F32),
            pltpu.VMEM((n_tok, 2, 2, rows // 2, cols), BF16),
            pltpu.VMEM((2, 2, rank, cols), BF16),
            pltpu.VMEM((n_tok, 2, 2, rows // 2, cols), BF16),
            pltpu.VMEM((2, 2, rank, cols), BF16),
            pltpu.VMEM((n_tok, 2, rows // 2, cols), BF16),
            pltpu.VMEM((2, rank, cols), BF16),
            pltpu.VMEM((n_tok, 2, rows // 2, cols), BF16),
            pltpu.VMEM((2, rank, cols), BF16),
            pltpu.VMEM((n_tok - 1, rows, cols), BF16),
            pltpu.VMEM((2, n_tok, rows, cols), BF16),
            pltpu.VMEM((n_tok, 2 * rank, cols), BF16),
            sems((2, n_tok, 2)),
            sems((n_tok, 2)),
            sems((2, n_tok, 4, 2)),
            sems((2, n_tok, n_chip, 2)),
            sems((2, n_chip - 1)),
            sems((2, n_chip)),
            sems((2, n_tok - 1, n_part, 2)),
            sems((6 + 2 * n_part,)),
            sems((2, n_tok + 1, n_chip)),
            sems((2, n_tok + 1, 2)),
            sems((2, n_tok + 1, 2)),
            sems((2, n_tok - 1, 2)),
            sems((2, n_tok, 2)),
            sems((2, n_tok - 1)),
            sems((2, n_tok, n_part, 2)),
            sems((n_tok, n_part, 2)),
        ],
        compiler_params=pltpu.CompilerParams(
            collective_id=1, has_side_effects=True, vmem_limit_bytes=52 * 1024 * 1024
        ),
    )(*(pltpu.with_memory_space_constraint(array, pltpu.HBM) for array in arguments))


def finish_kernel(dx, terms, oa, ib, dx_out, in_a_out, ib_out, oa_out, out_b_out):
    rank = in_a_out.shape[1]
    ib_out[...] = ib[...].astype(F32)
    oa_out[...] = oa[...].astype(F32)
    dx_out[...] = dx[...]
    in_a_out[...] = terms[rank:, :].T
    out_b_out[...] = terms[:rank, :]


def local(tokens, cotangent, frozen_in, frozen_out, in_a, in_b, out_a, out_b):
    count = tokens.shape[0] * lax.axis_size("tok")
    scale = ADAPTER_SCALE / math.sqrt(count)
    dx, terms, oa, ib = fused(
        2, scale, tokens, cotangent, frozen_in, frozen_out, in_a, in_b, out_a, out_b
    )
    rank, cols = in_a.shape[1], tokens.shape[1]
    vmem = pl.BlockSpec(memory_space=pltpu.VMEM)
    return pl.pallas_call(
        finish_kernel,
        out_shape=(
            jax.ShapeDtypeStruct(dx.shape, F32),
            jax.ShapeDtypeStruct((cols, rank), F32),
            jax.ShapeDtypeStruct(ib.shape, F32),
            jax.ShapeDtypeStruct(oa.shape, F32),
            jax.ShapeDtypeStruct((rank, cols), F32),
        ),
        in_specs=[vmem] * 4,
        out_specs=(vmem,) * 5,
        compiler_params=pltpu.CompilerParams(vmem_limit_bytes=16 * 1024 * 1024),
    )(dx, terms, oa, ib)


def local_by_rows(
    tokens,
    cotangent,
    frozen_in,
    frozen_out,
    input_adapter_first,
    input_adapter_second,
    adapter_out_a,
    adapter_out_b,
):
    highest_precision = lax.Precision.HIGHEST
    device_local_rows = tokens.shape[0]
    rank_width = input_adapter_second.shape[0]
    gradient_scale = ADAPTER_SCALE / math.sqrt(device_local_rows * lax.axis_size("tok"))
    full_tokens, full_cotan = (
        lax.all_gather(tokens, "hid", axis=1, tiled=True),
        lax.all_gather(cotangent, "hid", axis=1, tiled=True),
    )
    in_rows = lax.all_gather(frozen_in, "tok", axis=0, tiled=True)
    in_a_full = lax.all_gather(input_adapter_first, "hid", axis=0, tiled=True)
    lowrank_input = jnp.dot(full_tokens, in_a_full, preferred_element_type=jnp.float32)
    second_float = input_adapter_second.astype(jnp.float32)
    out_a_float = adapter_out_a.astype(jnp.float32)
    pre_activation = jnp.dot(
        full_tokens, in_rows, preferred_element_type=jnp.float32
    ) + ADAPTER_SCALE * jnp.dot(lowrank_input, second_float, precision=highest_precision)
    value_out, slopes = gelu_pair(pre_activation)
    hidden_act = value_out.astype(jnp.bfloat16)
    backward_lowrank = jnp.einsum(
        "td,rd->tr", full_cotan, adapter_out_b, preferred_element_type=jnp.float32
    )
    rank_out = jnp.dot(hidden_act, adapter_out_a, preferred_element_type=jnp.float32)
    dense_backward = jnp.einsum(
        "td,fd->tf",
        full_cotan,
        lax.all_gather(frozen_out, "tok", axis=1, tiled=True),
        preferred_element_type=jnp.float32,
    )
    dense_backward = dense_backward + ADAPTER_SCALE * jnp.dot(
        backward_lowrank, out_a_float.T, precision=highest_precision
    )
    grad_pre = (dense_backward * slopes).astype(jnp.bfloat16)
    rank_backward = jnp.einsum(
        "tf,rf->tr", grad_pre, input_adapter_second, preferred_element_type=jnp.float32
    )
    dense_in = jnp.einsum("tf,df->td", grad_pre, in_rows, preferred_element_type=jnp.float32)
    grad_out_a = gradient_scale * jnp.dot(
        hidden_act.astype(jnp.float32).T, backward_lowrank, precision=highest_precision
    )
    grad_in_b = gradient_scale * jnp.dot(
        lowrank_input.T, grad_pre.astype(jnp.float32), precision=highest_precision
    )
    in_a_float = in_a_full.astype(jnp.float32)
    dx_term = dense_in + ADAPTER_SCALE * jnp.dot(
        rank_backward, in_a_float.T, precision=highest_precision
    )
    out_term = jnp.dot(rank_out.T, full_cotan.astype(jnp.float32), precision=highest_precision)
    in_term = jnp.dot(rank_backward.T, full_tokens.astype(jnp.float32), precision=highest_precision)
    rank_terms = jnp.concatenate([out_term, in_term], axis=0)
    input_gradient, rank_local = (
        lax.psum_scatter(dx_term, "hid", scatter_dimension=1, tiled=True),
        lax.psum_scatter(rank_terms, "hid", scatter_dimension=1, tiled=True),
    )
    grad_out_a, grad_in_b, rank_total = lax.psum((grad_out_a, grad_in_b, rank_local), "tok")
    grad_out_b = gradient_scale * rank_total[:rank_width]
    grad_in_a = gradient_scale * rank_total[rank_width:].T
    return (input_gradient, grad_in_a, grad_in_b, grad_out_a, grad_out_b)


def solution(mesh):
    in_specs = (
        P("tok", "hid"),
        P("tok", "hid"),
        P("tok", "hid"),
        P("hid", "tok"),
        P("hid", None),
        P(None, "hid"),
        P("hid", None),
        P(),
    )
    out_specs = (P("tok", "hid"), P("hid", None), P(None, "hid"), P("hid", None), P(None, "hid"))
    def body(*arrays):
        share = arrays[2].shape[1] // lax.axis_size("tok")
        wide = share % 256 == 0 and lax.axis_size("tok") > 2
        wide = wide and lax.axis_size("hid") == 2 ** len(("y", "x", "core"))
        return local(*arrays) if wide else local_by_rows(*arrays)

    return jax.shard_map(body, mesh=mesh, in_specs=in_specs, out_specs=out_specs, check_vma=False)
```
